32 devices in a mesh: dp: 16 (over z, y, x), expert: 2 (over core).
Axes of the slice: x: 2, y: 2, z: 4, core: 2. Of those that a mesh axis runs over, the one named last changes fastest.
Arguments:
- tokens: bfloat16 [16384, 1536], P(('dp', 'expert')), may hold values from -6 to 6
- cotangent: bfloat16 [16384, 1536], P(('dp', 'expert')), may hold values from -6 to 6
- permutation: int32 [16384], P(('dp', 'expert')), may hold values from 0 to 16383, as said below
- lengths: int32 [64, 4], P(('dp', 'expert')), may hold values from 1 to 128, 256 in all within a row
- expert_ids: int32 [16384, 8], P(('dp', 'expert')), may hold values from 0 to 15, all different within a row
- gate_weights: float32 [16384, 8], P(('dp', 'expert')), may hold values from 0.05 to 0.25
- attn_gain: bfloat16 [1536], P(('dp', 'expert')), may hold values from 0.099609375 to 1.8984375
- qkv_weight: bfloat16 [1536, 2560], P(('dp', 'expert')), may hold values from -0.15625 to 0.15625
- out_weight: bfloat16 [1536, 1536], P(('dp', 'expert')), may hold values from -0.625 to 0.625
- ffn_gain: bfloat16 [1536], P(('dp', 'expert')), may hold values from 0.099609375 to 1.8984375
- expert_in: bfloat16 [1536, 2, 8192], P(None, None, ('dp', 'expert')), may hold values from -0.15625 to 0.15625
- expert_out: bfloat16 [8192, 1536], P(('dp', 'expert')), may hold values from -1 to 1
Outputs:
- output: bfloat16 [16384, 1536], P(('dp', 'expert'))
- input_grad: bfloat16 [16384, 1536], P(('dp', 'expert'))
- attn_gain_grad: float32 [1536], P(('dp', 'expert'))
- qkv_grad: float32 [1536, 2560], P(('dp', 'expert'))
- out_grad: float32 [1536, 1536], P(('dp', 'expert'))
- ffn_gain_grad: float32 [1536], P(('dp', 'expert'))
- expert_in_grad: float32 [1536, 2, 8192], P(None, None, ('dp', 'expert'))
- expert_out_grad: float32 [8192, 1536], P(('dp', 'expert'))
The draws below stay inside these ranges and needn't reach their ends.
Inputs may be any that keep to these rules, and one draw needn't show every extreme that they name: permutation holds each of 0 to 16383 once; each aligned block of 512 positions takes exactly 16 values from each aligned block of 512 values. `lengths`: each row sums to 256. `expert_ids`: each row names 8 different experts.
All inputs are finite; a program needn't handle non-finite values.
Results may differ from the reference program's by a relative error of at most 0.017.
Values may be sent and summed in bfloat16 or wider, within the bound.
A program may use at most 320 MiB of HBM per device.

```python
import math
import jax
import jax.numpy as jnp
import numpy as np
from jax import lax

D = 1536
HEADS = 24
KV_HEADS = 8
HEAD = 64
FF_E = 512
TOPK = 8
MB = 2
SEQS = 4
TOK_MB = 256
EXPERTS = 16
TOK_DEV = 512
RANKS = 32
TOKENS = 16384
SEQ_MAX = 128
CAP = 128
Q_DIM = 1536
QKV = 2560
N_DP = 16
N_EXPERT = 2


def draw_permutation(key, part):
    device_count = TOKENS // TOK_DEV
    peer_rows = TOK_DEV // device_count
    key_out, key_mix = jax.random.split(key)
    outgoing = jax.vmap(lambda one_key: jax.random.permutation(one_key, TOK_DEV))(jax.random.split(key_out, device_count))
    sources = jnp.arange(device_count, dtype=jnp.int32)[:, None] * TOK_DEV
    values = (outgoing.astype(jnp.int32) + sources).reshape(device_count, device_count, peer_rows)
    arranged = jnp.transpose(values, (1, 0, 2)).reshape(device_count, TOK_DEV)
    shuffle = jax.vmap(lambda one_key: jax.random.permutation(one_key, TOK_DEV))(jax.random.split(key_mix, device_count))
    dealt = jnp.take_along_axis(arranged, shuffle.astype(jnp.int32), axis=1)
    return dealt.reshape(TOKENS).astype(jnp.int32)


def block_levels(key, shape, cuts, low, high):
    factor_of, own = 1.0, jax.random.fold_in(key, 6)
    for dim, blocks in cuts:
        draws = jnp.exp(jax.random.uniform(jax.random.fold_in(own, dim), (blocks,), jnp.float32, low / len(cuts), high / len(cuts)))
        factor_of = factor_of * jnp.repeat(draws, shape[dim] // blocks).reshape([-1 if axis == dim else 1 for axis in range(len(shape))])
    return factor_of


def choose_distinct(own_key, rows, amount, top, lift):
    ranking = jax.random.permutation(jax.random.fold_in(own_key, 1), amount)
    boost = ranking
    for power in range(3):
        boost = boost * boost // amount
    boost = boost * lift // amount
    chance = jax.random.randint(jax.random.fold_in(own_key, 2), (rows, amount), 0, 4096) + boost
    sure = jax.random.permutation(jax.random.fold_in(own_key, 3), rows)[jnp.arange(amount) % rows]
    chance = jnp.where(jnp.arange(rows)[:, None] == sure[None, :], 1 << 14, chance)
    priority = chance * amount + jnp.arange(amount)
    return lax.top_k(priority.astype(jnp.int32), top)[1].astype(jnp.int32)


def split_up(count, total, bound, lean):
    portions = [(1 << 20) // math.isqrt(rank ** lean) + 1 for rank in range(2, count + 1)]
    rest, counts = total - bound - (count - 1), [1] * (count - 1)
    while rest > 0:
        movable = [i for i in range(count - 1) if counts[i] < bound]
        mass, budget = sum([portions[i] for i in movable]), rest
        for i in movable:
            extra = min(bound - counts[i], max(1, budget * portions[i] // mass), rest)
            counts[i] = counts[i] + extra
            rest = rest - extra
    return np.array([bound] + counts)


def ragged_sizes(stream_key, count, total, reach, slope):
    if count == 2:
        one = jax.random.randint(stream_key, (), max(1, total - reach), min(reach, total - 1) + 1)
        return jnp.stack([one, total - one])
    tallies = jnp.asarray(split_up(count, total, reach, slope), jnp.int32)
    twos = (count - 1) // 2
    donor, taker = tallies[1:1 + 2 * twos:2], tallies[2:2 + 2 * twos:2]
    margin = jnp.minimum(donor - 1, reach - taker)
    passed = jax.random.randint(jax.random.fold_in(stream_key, 1), (twos,), 0, 1 << 20) % (margin + 1)
    tallies = tallies.at[1:1 + 2 * twos:2].set(donor - passed).at[2:2 + 2 * twos:2].set(taker + passed)
    return tallies[jax.random.permutation(jax.random.fold_in(stream_key, 2), count)]


def noise(own_key, shape, width, reach, shards=(), kind=jnp.bfloat16):
    array = width * jax.random.normal(own_key, shape, jnp.float32)
    if shards:
        array = array * block_levels(own_key, shape, shards, -0.22, 0.18)
    return jnp.clip(array, -reach, reach).astype(kind)


def setup_inputs(seed: int = 0) -> dict:
    seeds = jax.random.split(jax.random.key(seed), 13)
    return {
        "tokens": noise(seeds[0], (TOKENS, D), 1.0, 6.0, ((0, 32),)),
        "cotangent": noise(seeds[1], (TOKENS, D), 1.0, 6.0, ((0, 32),)),
        "permutation": draw_permutation(jax.random.fold_in(seeds[12], 71), 0),
        "lengths": jax.vmap(lambda own: ragged_sizes(own, SEQS, TOK_MB, SEQ_MAX, 1))(jax.random.split(seeds[3], (RANKS * MB))).reshape((RANKS * MB, SEQS)).astype(jnp.int32),
        "expert_ids": choose_distinct(seeds[4], TOKENS, EXPERTS, TOPK, 4096),
        "gate_weights": jnp.clip(jnp.exp(math.log(0.25) - 1.609438 * jax.random.uniform(seeds[5], (TOKENS, TOPK), jnp.float32) ** block_levels(seeds[5], (TOKENS, TOPK), ((0, 32),), -0.2, 0.2)), 0.05, 0.25),
        "attn_gain": jnp.clip(1.0 + 0.18 * jax.random.normal(seeds[6], (D,), jnp.float32), 0.099609375, 1.8984375).astype(jnp.bfloat16),
        "qkv_weight": noise(seeds[7], (D, QKV), D ** -0.5, 0.15625, ((0, 32),)),
        "out_weight": noise(seeds[8], (Q_DIM, D), (Q_DIM // 16) ** -0.5, 0.625, ((0, 32),)),
        "ffn_gain": jnp.clip(1.0 + 0.18 * jax.random.normal(seeds[9], (D,), jnp.float32), 0.099609375, 1.8984375).astype(jnp.bfloat16),
        "expert_in": noise(seeds[10], (D, 2, EXPERTS * FF_E), D ** -0.5, 0.15625, ((2, 32),)),
        "expert_out": noise(seeds[11], (EXPERTS * FF_E, D), (FF_E // 16) ** -0.5, 1.0, ((0, 32),)),
    }


epsilon = 1e-05
theta_base = 10000.0
highest = lax.Precision.HIGHEST

@jax.custom_vjp
def low(v):
    return lax.optimization_barrier(v.astype(jnp.bfloat16)).astype(jnp.float32)

@jax.custom_vjp
def low_back(v):
    return v

def low_keep(v):
    return (low(v), None)

def low_pass(kept, grad):
    return (grad,)

def back_keep(v):
    return (v, None)

def back_low(kept, grad):
    return (low(grad),)
low.defvjp(low_keep, low_pass)
low_back.defvjp(back_keep, back_low)

def layout_rows(length_rows):
    seq_ends = jnp.cumsum(length_rows, axis=1, dtype=jnp.int32)
    starts = seq_ends - length_rows
    within = jnp.arange(TOK_MB, dtype=jnp.int32)
    segment = lax.optimization_barrier(jnp.sum((within[None, :, None] >= seq_ends[:, None, :]).astype(jnp.int32), axis=2, dtype=jnp.int32))
    chosen = segment[:, :, None] == jnp.arange(SEQS, dtype=jnp.int32)[None, None, :]
    seq_begin = lax.optimization_barrier(jnp.sum(jnp.where(chosen, starts[:, None, :], 0), axis=2, dtype=jnp.int32))
    position = within[None, :] - seq_begin
    segment = segment + jnp.arange(MB, dtype=jnp.int32)[:, None] * SEQS
    return (segment.reshape(-1), position.reshape(-1))

def rope_tables(position):
    half_width = HEAD // 2
    frequency = theta_base ** (-(2.0 / HEAD) * jnp.arange(half_width, dtype=jnp.float32))
    angles = position.astype(jnp.float32)[:, None] * frequency[None, :]
    return (jnp.cos(angles), jnp.sin(angles))

def rotate(values, cosine_table, sine_table):
    half_width = HEAD // 2
    front_half = values[..., :half_width]
    behind = values[..., half_width:]
    cosine_part = cosine_table[:, None, :]
    sine_part = sine_table[:, None, :]
    return jnp.concatenate([front_half * cosine_part - behind * sine_part, behind * cosine_part + front_half * sine_part], axis=-1)

def assign(picked):
    per_mb = picked.reshape(MB, TOK_MB * TOPK)
    onehot = (per_mb[:, :, None] == jnp.arange(EXPERTS, dtype=jnp.int32)[None, None, :]).astype(jnp.int32)
    earlier = jnp.cumsum(onehot, axis=1, dtype=jnp.int32) - onehot
    slot_index = lax.optimization_barrier(jnp.sum(earlier * onehot, axis=2, dtype=jnp.int32))
    micro_index = jnp.arange(MB, dtype=jnp.int32)[:, None]
    slots_all = EXPERTS * MB * CAP
    target = jnp.where(slot_index < CAP, per_mb * (MB * CAP) + micro_index * CAP + slot_index, slots_all)
    target = target.reshape(MB * TOK_MB, TOPK)
    row_ids = jnp.broadcast_to(jnp.arange(MB * TOK_MB, dtype=jnp.int32)[:, None], target.shape)
    slot_row = jnp.full((slots_all,), MB * TOK_MB, jnp.int32).at[target.reshape(-1)].set(row_ids.reshape(-1), mode='drop')
    return (target, slot_row)

def device_block(inputs, weights):
    rows_in, length_rows, picked, gate_rows = inputs
    attn_g, qkv_w, out_w, ffn_g, exp_in, exp_out = weights
    row_count = rows_in.shape[0]
    q_dim = HEADS * HEAD
    kv_dim = KV_HEADS * HEAD
    segment, position = layout_rows(length_rows)
    scale_one = lax.rsqrt(lax.optimization_barrier(jnp.mean(rows_in * rows_in, axis=1, keepdims=True)) + epsilon)
    normed = low(rows_in * scale_one * attn_g)
    projected = low_back(jnp.dot(normed, qkv_w, precision=highest))
    cosine_table, sine_table = rope_tables(position)
    queries = low(rotate(projected[:, :q_dim].reshape(row_count, HEADS, HEAD), cosine_table, sine_table))
    key_rows = low(rotate(projected[:, q_dim:q_dim + kv_dim].reshape(row_count, KV_HEADS, HEAD), cosine_table, sine_table))
    value_rows = low(projected[:, q_dim + kv_dim:].reshape(row_count, KV_HEADS, HEAD))
    groups_per = HEADS // KV_HEADS
    grouped = queries.reshape(row_count, KV_HEADS, groups_per, HEAD)
    scores = low_back(jnp.einsum('qhgd,khd->hgqk', grouped, key_rows, precision=highest) * HEAD ** (-0.5))
    allowed = (segment[:, None] == segment[None, :]) & (position[:, None] >= position[None, :])
    masked = jnp.where(allowed, scores, -1e+30)
    weights_exp = jnp.exp(masked - lax.optimization_barrier(jnp.max(masked, axis=-1, keepdims=True)))
    probabilities = low(weights_exp / lax.optimization_barrier(jnp.sum(weights_exp, axis=-1, keepdims=True)))
    mixed_rows = jnp.einsum('hgqk,khd->qhgd', probabilities, value_rows, precision=highest).reshape(row_count, q_dim)
    mixed_rows = low(low_back(mixed_rows))
    attended = low_back(jnp.dot(mixed_rows, out_w, precision=highest))
    residual = rows_in + attended
    scale_two = lax.rsqrt(lax.optimization_barrier(jnp.mean(residual * residual, axis=1, keepdims=True)) + epsilon)
    normed_two = low(residual * scale_two * ffn_g)
    target, slot_row = assign(picked)
    padded = jnp.concatenate([normed_two, jnp.zeros((1, D), normed_two.dtype)], axis=0)
    dispatched = low_back(jnp.take(padded, slot_row, axis=0)).reshape(EXPERTS, MB * CAP, D)
    gate_up = low_back(jnp.einsum('ecd,dgef->ecgf', dispatched, exp_in.reshape(D, 2, EXPERTS, FF_E), precision=highest))
    hidden = low(jax.nn.silu(gate_up[:, :, 0]) * gate_up[:, :, 1])
    produced = low_back(low(jnp.einsum('ecf,efd->ecd', hidden, exp_out.reshape(EXPERTS, FF_E, D), precision=highest)))
    padded_back = jnp.concatenate([produced.reshape(EXPERTS * MB * CAP, D), jnp.zeros((1, D), produced.dtype)], axis=0)
    combined = lax.optimization_barrier(jnp.sum(gate_rows[:, :, None] * jnp.take(padded_back, target, axis=0), axis=1))
    return residual + combined

def reference(tokens, cotangent, permutation, lengths, expert_ids, gate_weights, attn_gain, qkv_weight, out_weight, ffn_gain, expert_in, expert_out):
    device_count = N_DP * N_EXPERT
    inverse = jnp.zeros((TOKENS,), jnp.int32).at[permutation].set(jnp.arange(TOKENS, dtype=jnp.int32))
    length_blocks = lengths.reshape(device_count, MB, SEQS)
    id_blocks = expert_ids.reshape(device_count, TOK_DEV, TOPK)
    gate_blocks = gate_weights.astype(jnp.float32).reshape(device_count, TOK_DEV, TOPK)

    def forward(inputs, attn_g, qkv_w, out_w, ffn_g, exp_in, exp_out):
        dealt = jnp.take(inputs, permutation, axis=0).reshape(device_count, TOK_DEV, D)
        weights = (attn_g, qkv_w, out_w, ffn_g, exp_in, exp_out)
        checked = jax.checkpoint(device_block)
        result = lax.map(lambda block: checked(block, weights), (dealt, length_blocks, id_blocks, gate_blocks))
        return jnp.take(result.reshape(TOKENS, D), inverse, axis=0)
    output, pullback = jax.vjp(forward, tokens.astype(jnp.float32), attn_gain.astype(jnp.float32), qkv_weight.astype(jnp.float32), out_weight.astype(jnp.float32), ffn_gain.astype(jnp.float32), expert_in.astype(jnp.float32), expert_out.astype(jnp.float32))
    grads = pullback(cotangent.astype(jnp.float32))
    return (output.astype(jnp.bfloat16), grads[0].astype(jnp.bfloat16), grads[1], grads[2], grads[3], grads[4], grads[5], grads[6])
```

```python
import jax
import jax.numpy as jnp
from jax import lax
from jax.sharding import PartitionSpec as P

HEADS = 24
KV_HEADS = 8
HEAD = 64
FF_E = 512
TOPK = 8
MB = 2
SEQS = 4
TOK_MB = 256
ALL = ("hi", "lo", "core")


epsilon = 1e-05
theta_base = 10000.0


def layout_rows(length_rows):
    seq_ends = jnp.cumsum(length_rows, axis=1, dtype=jnp.int32)
    starts = seq_ends - length_rows
    within = jnp.arange(TOK_MB, dtype=jnp.int32)
    segment = jnp.sum(
        (within[None, :, None] >= seq_ends[:, None, :]).astype(jnp.int32), axis=2, dtype=jnp.int32
    )
    chosen = segment[:, :, None] == jnp.arange(SEQS, dtype=jnp.int32)[None, None, :]
    seq_begin = jnp.sum(jnp.where(chosen, starts[:, None, :], 0), axis=2, dtype=jnp.int32)
    position = within[None, :] - seq_begin
    segment = segment + jnp.arange(MB, dtype=jnp.int32)[:, None] * SEQS
    return (segment.reshape(-1), position.reshape(-1))


def rope_tables(position):
    half_width = HEAD // 2
    frequency = theta_base ** (-(2.0 / HEAD) * jnp.arange(half_width, dtype=jnp.float32))
    angles = position.astype(jnp.float32)[:, None] * frequency[None, :]
    return (jnp.cos(angles), jnp.sin(angles))


def rotate(values, cosine_table, sine_table):
    half_width = HEAD // 2
    front_half = values[..., :half_width]
    behind = values[..., half_width:]
    cosine_part = cosine_table[:, None, :]
    sine_part = sine_table[:, None, :]
    return jnp.concatenate(
        [
            front_half * cosine_part - behind * sine_part,
            behind * cosine_part + front_half * sine_part,
        ],
        axis=-1,
    )


def slot_tables(ids, gates, experts, capacity):
    count = experts.shape[0]
    named = ids[..., None] == experts
    picked = jnp.any(named, axis=2)
    weight = jnp.sum(jnp.where(named, gates[..., None], 0.0), axis=2)
    rows = jnp.arange(TOK_MB, dtype=jnp.int32)
    below = (rows[:, None] > rows[None, :]).astype(jnp.bfloat16)
    shaped = picked.reshape(-1, TOK_MB, count)
    slot = jnp.einsum(
        "rq,bqe->ber", below, shaped.astype(jnp.bfloat16), preferred_element_type=jnp.float32
    ).astype(jnp.int32)
    kept = jnp.transpose(shaped, (0, 2, 1))
    hit = kept[:, :, None, :] & (
        slot[:, :, None, :] == jnp.arange(capacity, dtype=jnp.int32)[None, None, :, None]
    )
    weight = jnp.transpose(weight.reshape(-1, TOK_MB, count), (0, 2, 1))
    slot_gate = jnp.sum(jnp.where(hit, weight[:, :, None, :], 0.0), axis=3)
    return hit.astype(jnp.bfloat16), slot_gate


def block_scores(queries, key_rows, segment, position):
    row_count = queries.shape[0]
    grouped = queries.reshape(row_count, KV_HEADS, HEADS // KV_HEADS, HEAD)
    scores = jnp.einsum(
        "qhgd,khd->hgqk", grouped, key_rows, preferred_element_type=jnp.float32
    ) * HEAD ** (-0.5)
    allowed = (segment[:, None] == segment[None, :]) & (position[:, None] >= position[None, :])
    return (jnp.where(allowed, scores, -1e30), grouped)


def attend_block(queries, key_rows, value_rows, segment, position):
    row_count = queries.shape[0]
    masked, grouped = block_scores(queries, key_rows, segment, position)
    row_peak = jnp.max(masked, axis=-1, keepdims=True)
    weights_exp = jnp.exp(masked - row_peak)
    row_total = jnp.sum(weights_exp, axis=-1, keepdims=True)
    probabilities = (weights_exp / row_total).astype(jnp.bfloat16)
    mixed_rows = jnp.einsum(
        "hgqk,khd->qhgd", probabilities, value_rows, preferred_element_type=jnp.float32
    )
    return (mixed_rows.reshape(row_count, HEADS * HEAD), row_peak + jnp.log(row_total))


def attend_back(queries, key_rows, value_rows, segment, position, logsum, grad_mixed):
    row_count = queries.shape[0]
    masked, grouped = block_scores(queries, key_rows, segment, position)
    exact_probs = jnp.exp(masked - logsum)
    probabilities = exact_probs.astype(jnp.bfloat16)
    grad_heads = grad_mixed.reshape(row_count, KV_HEADS, HEADS // KV_HEADS, HEAD)
    grad_probs = jnp.einsum(
        "qhgd,khd->hgqk", grad_heads, value_rows, preferred_element_type=jnp.float32
    )
    grad_values = jnp.einsum(
        "hgqk,qhgd->khd", probabilities, grad_heads, preferred_element_type=jnp.float32
    )
    grad_scores = (
        exact_probs * (grad_probs - jnp.sum(grad_probs * exact_probs, axis=-1, keepdims=True))
    ).astype(jnp.bfloat16)
    grad_queries = jnp.einsum(
        "hgqk,khd->qhgd", grad_scores, key_rows, preferred_element_type=jnp.float32
    ) * HEAD ** (-0.5)
    grad_keys = jnp.einsum(
        "hgqk,qhgd->khd", grad_scores, grouped, preferred_element_type=jnp.float32
    ) * HEAD ** (-0.5)
    return (grad_queries.reshape(row_count, HEADS, HEAD), grad_keys, grad_values)


def norm_back(values, scale, gain, grad_normed):
    scaled_grad = grad_normed * gain
    grad_gain = jnp.sum(grad_normed * values * scale, axis=0)
    grad_values = scale * scaled_grad - values * scale * scale * scale * jnp.mean(
        scaled_grad * values, axis=1, keepdims=True
    )
    return (grad_gain, grad_values)


def shards(
    tokens,
    cotangent,
    permutation,
    lengths,
    expert_ids,
    gate_weights,
    attn_gain,
    qkv_weight,
    out_weight,
    ffn_gain,
    expert_in,
    expert_out,
):
    device_count = lax.axis_size(ALL)
    hi_count = lax.axis_size("hi")
    lo_count = lax.axis_size("lo")
    tok_dev = permutation.shape[0]
    model_width = tokens.shape[1]
    peer_rows = tok_dev // device_count
    q_dim = HEADS * HEAD
    kv_dim = KV_HEADS * HEAD
    positions = jnp.arange(tok_dev, dtype=jnp.int32)
    expert_count = expert_in.shape[2] * device_count // FF_E
    capacity = TOK_MB * TOPK // expert_count
    source = permutation // tok_dev
    local_row = permutation % tok_dev
    from_source = (source[:, None] == jnp.arange(device_count, dtype=jnp.int32)[None, :]).astype(
        jnp.int32
    )
    earlier = jnp.cumsum(from_source, axis=0, dtype=jnp.int32) - from_source
    arrival = source * peer_rows + jnp.sum(earlier * from_source, axis=1, dtype=jnp.int32)
    arrival_match = arrival[:, None] == positions[None, :]
    wanted = jnp.sum(jnp.where(arrival_match, local_row[:, None], 0), axis=0, dtype=jnp.int32)
    by_arrival = jnp.sum(jnp.where(arrival_match, positions[:, None], 0), axis=0, dtype=jnp.int32)
    asked_rows = lax.all_to_all(
        wanted.reshape(device_count, peer_rows),
        ALL,
        split_axis=0,
        concat_axis=0,
        tiled=True,
    ).reshape(tok_dev)
    asked_match = asked_rows[:, None] == positions[None, :]
    by_asked = jnp.sum(jnp.where(asked_match, positions[:, None], 0), axis=0, dtype=jnp.int32)
    outgoing = (
        jnp.take(tokens, asked_rows, axis=0).reshape(device_count, peer_rows, model_width),
        jnp.take(cotangent, asked_rows, axis=0).reshape(device_count, peer_rows, model_width),
    )
    got_rows, got_grad = (
        lax.all_to_all(outgoing[0], ALL, split_axis=0, concat_axis=0, tiled=True),
        lax.all_to_all(outgoing[1], ALL, split_axis=0, concat_axis=0, tiled=True),
    )
    rows_in = jnp.take(got_rows.reshape(tok_dev, model_width), arrival, axis=0).astype(jnp.float32)
    grad_bf = jnp.take(got_grad.reshape(tok_dev, model_width), arrival, axis=0)
    grad_output = grad_bf.astype(jnp.float32)
    gains = jnp.concatenate(
        [attn_gain[:, None], ffn_gain[:, None], jnp.zeros((attn_gain.shape[0], 126), jnp.bfloat16)],
        axis=1,
    )
    packed_qkv = lax.all_gather(
        jnp.concatenate([qkv_weight, gains], axis=1), ALL, axis=0, tiled=True
    )
    qkv_full = packed_qkv[:, : qkv_weight.shape[1]]
    gain_pair = packed_qkv[:, qkv_weight.shape[1] :].astype(jnp.float32)
    gain_one = gain_pair[:, 0]
    gain_two = gain_pair[:, 1]
    out_full = lax.all_gather(out_weight, ALL, axis=0, tiled=True)
    shard_cols = expert_in.shape[2]
    weights_in = lax.all_gather(
        expert_in.reshape(model_width, 2 * shard_cols), ("hi", "core"), axis=0
    ).reshape(hi_count, 2, model_width, 2 * shard_cols)
    weights_out = lax.all_gather(expert_out, ("hi", "core"), axis=0).reshape(
        hi_count, 2, shard_cols, model_width
    )
    segment, position = layout_rows(lengths)
    scale_one = lax.rsqrt(jnp.mean(rows_in * rows_in, axis=1, keepdims=True) + epsilon)
    normed = (rows_in * scale_one * gain_one).astype(jnp.bfloat16)
    projected = jnp.dot(normed, qkv_full, preferred_element_type=jnp.float32)
    cosine_table, sine_table = rope_tables(position)
    queries = rotate(
        projected[:, :q_dim].reshape(tok_dev, HEADS, HEAD), cosine_table, sine_table
    ).astype(jnp.bfloat16)
    key_rows = rotate(
        projected[:, q_dim : q_dim + kv_dim].reshape(tok_dev, KV_HEADS, HEAD),
        cosine_table,
        sine_table,
    ).astype(jnp.bfloat16)
    value_rows = (
        projected[:, q_dim + kv_dim :].reshape(tok_dev, KV_HEADS, HEAD).astype(jnp.bfloat16)
    )
    block_rows = min(tok_dev, max(TOK_MB, 512))
    mixed_part, logsum = attend_block(queries, key_rows, value_rows, segment, position)
    logsums = [logsum]
    mixed_rows = mixed_part.astype(jnp.bfloat16)
    attended = jnp.dot(mixed_rows, out_full, preferred_element_type=jnp.float32)
    residual = rows_in + attended
    scale_two = lax.rsqrt(jnp.mean(residual * residual, axis=1, keepdims=True) + epsilon)
    normed_two = (residual * scale_two * gain_two).astype(jnp.bfloat16)
    home = lax.axis_index("lo")

    def spread(block):
        return [block] + [swap(block, step) for step in range(1, lo_count)]

    def swap(block, step):
        return lax.ppermute(block, "lo", [(i, i ^ step) for i in range(lo_count)])

    ids_all = jnp.stack(spread(expert_ids))
    gates_all = jnp.stack(spread(gate_weights))
    choose, slot_gate = slot_tables(
        ids_all.reshape(-1, TOK_MB, TOPK),
        gates_all.reshape(-1, TOK_MB, TOPK),
        home + lo_count * jnp.arange(hi_count, dtype=jnp.int32),
        capacity,
    )
    rows_all = jnp.stack(spread(normed_two)).reshape(lo_count * MB, TOK_MB, model_width)
    grads_all = jnp.stack(spread(grad_bf)).reshape(lo_count * MB, TOK_MB, model_width)
    expert_rows = jnp.einsum(
        "becr,brd->ebcd", choose, rows_all, preferred_element_type=jnp.float32
    ).astype(jnp.bfloat16).reshape(hi_count, -1, model_width)
    gate_up = jnp.einsum(
        "erd,ekdf->ekrf", expert_rows, weights_in, preferred_element_type=jnp.float32
    )
    gate_part = gate_up[..., :shard_cols]
    up_part = gate_up[..., shard_cols:]
    sigmoid_gate = jax.nn.sigmoid(gate_part)
    hidden = (gate_part * sigmoid_gate * up_part).astype(jnp.bfloat16)
    slot_weight = jnp.transpose(slot_gate, (1, 0, 2)).reshape(hi_count, -1, 1)
    produced = (
        jnp.einsum("ekrf,ekfd->erd", hidden, weights_out, preferred_element_type=jnp.float32)
        * slot_weight
    ).astype(jnp.bfloat16)

    def collect(slot_values):
        parts = jnp.einsum(
            "becr,ebcd->brd",
            choose,
            slot_values.reshape(hi_count, lo_count * MB, capacity, model_width),
            preferred_element_type=jnp.float32,
        ).reshape(lo_count, tok_dev, model_width)
        total = parts[0]
        for step in range(1, lo_count):
            total = total + swap(parts[step].astype(jnp.bfloat16), step).astype(jnp.float32)
        return total

    output_rows = (residual + collect(produced)).astype(jnp.bfloat16)
    grad_expert = (
        jnp.einsum("becr,brd->ebcd", choose, grads_all, preferred_element_type=jnp.float32).reshape(
            hi_count, -1, model_width
        )
        * slot_weight
    ).astype(jnp.bfloat16)
    grad_hidden = jnp.einsum(
        "erd,ekfd->ekrf", grad_expert, weights_out, preferred_element_type=jnp.float32
    )
    grad_weights_out = jnp.einsum(
        "ekrf,erd->ekfd", hidden, grad_expert, preferred_element_type=jnp.float32
    )
    grad_gate = grad_hidden * up_part * sigmoid_gate * (1.0 + gate_part * (1.0 - sigmoid_gate))
    grad_up = grad_hidden * (gate_part * sigmoid_gate)
    grad_gate_up = jnp.concatenate([grad_gate, grad_up], axis=-1).astype(jnp.bfloat16)
    grad_weights_in = jnp.einsum(
        "erd,ekrf->ekdf", expert_rows, grad_gate_up, preferred_element_type=jnp.float32
    )
    grad_expert_rows = jnp.einsum(
        "ekrf,ekdf->erd", grad_gate_up, weights_in, preferred_element_type=jnp.float32
    ).astype(jnp.bfloat16)
    grad_normed_two = collect(grad_expert_rows)
    shard_out = lax.psum_scatter(
        grad_weights_out.astype(jnp.bfloat16).reshape(hi_count * 2 * shard_cols, model_width),
        ("hi", "core"),
        scatter_dimension=0,
        tiled=True,
    ).astype(jnp.float32)
    shard_in = (
        lax.psum_scatter(
            grad_weights_in.astype(jnp.bfloat16).reshape(hi_count * 2 * model_width, 2 * shard_cols),
            ("hi", "core"),
            scatter_dimension=0,
            tiled=True,
        )
        .astype(jnp.float32)
        .reshape(model_width, 2, shard_cols)
    )
    grad_gain_two, grad_from_norm = norm_back(residual, scale_two, gain_two, grad_normed_two)
    grad_residual = grad_output + grad_from_norm
    grad_attended = grad_residual.astype(jnp.bfloat16)
    grad_out_weight = jnp.einsum(
        "nq,nd->qd", mixed_rows, grad_attended, preferred_element_type=jnp.float32
    )
    grad_mixed = jnp.einsum(
        "nd,qd->nq", grad_attended, out_full, preferred_element_type=jnp.float32
    ).astype(jnp.bfloat16)
    grad_query_parts = []
    grad_key_parts = []
    grad_value_parts = []
    for block_number, block_start in enumerate(range(0, tok_dev, block_rows)):
        grad_q, grad_k, grad_v = attend_back(
            queries, key_rows, value_rows, segment, position, logsums[block_number], grad_mixed
        )
        grad_query_parts.append(grad_q)
        grad_key_parts.append(grad_k)
        grad_value_parts.append(grad_v)
    grad_queries = rotate(grad_query_parts[0], cosine_table, -sine_table)
    grad_keys = rotate(grad_key_parts[0], cosine_table, -sine_table)
    grad_values = grad_value_parts[0]
    grad_projected = jnp.concatenate(
        [
            grad_queries.reshape(tok_dev, q_dim),
            grad_keys.reshape(tok_dev, kv_dim),
            grad_values.reshape(tok_dev, kv_dim),
        ],
        axis=1,
    ).astype(jnp.bfloat16)
    grad_qkv_weight = jnp.einsum(
        "nd,nc->dc", normed, grad_projected, preferred_element_type=jnp.float32
    )
    grad_normed = jnp.einsum(
        "nc,dc->nd", grad_projected, qkv_full, preferred_element_type=jnp.float32
    )
    grad_gain_one, grad_from_first = norm_back(rows_in, scale_one, gain_one, grad_normed)
    grad_input = (grad_residual + grad_from_first).astype(jnp.bfloat16)
    def gain_column(grad_gain):
        return jnp.pad(grad_gain[:, None], ((0, 0), (0, 127)))

    packed_out = lax.psum_scatter(
        jnp.concatenate([grad_out_weight, gain_column(grad_gain_two)], axis=1),
        ALL,
        scatter_dimension=0,
        tiled=True,
    )
    shard_attn_out = packed_out[:, :model_width]
    shard_gain_two = packed_out[:, model_width]
    packed_grad = lax.psum_scatter(
        jnp.concatenate([grad_qkv_weight, gain_column(grad_gain_one)], axis=1),
        ALL,
        scatter_dimension=0,
        tiled=True,
    )
    shard_qkv = packed_grad[:, : qkv_weight.shape[1]]
    shard_gain_one = packed_grad[:, qkv_weight.shape[1]]
    leaving = (
        jnp.take(output_rows, by_arrival, axis=0).reshape(device_count, peer_rows, model_width),
        jnp.take(grad_input, by_arrival, axis=0).reshape(device_count, peer_rows, model_width),
    )
    home_out, home_grad = (
        lax.all_to_all(leaving[0], ALL, split_axis=0, concat_axis=0, tiled=True),
        lax.all_to_all(leaving[1], ALL, split_axis=0, concat_axis=0, tiled=True),
    )
    output = jnp.take(home_out.reshape(tok_dev, model_width), by_asked, axis=0)
    input_grad = jnp.take(home_grad.reshape(tok_dev, model_width), by_asked, axis=0)
    return (
        output,
        input_grad,
        shard_gain_one,
        shard_qkv,
        shard_attn_out,
        shard_gain_two,
        shard_in,
        shard_out,
    )


def solution(mesh):
    dp_count = mesh.shape["dp"]
    hi_count = 4 if dp_count % 4 == 0 else 1
    split = jax.sharding.Mesh(
        mesh.devices.reshape(hi_count, dp_count // hi_count, mesh.shape["expert"]), ALL
    )
    rows, columns = P(ALL, None), P(None, None, ALL)
    return jax.shard_map(
        shards,
        mesh=split,
        in_specs=(rows, rows, P(ALL), rows, rows, rows, P(ALL), rows, rows, P(ALL), columns, rows),
        out_specs=(rows, rows, P(ALL), rows, rows, P(ALL), columns, rows),
        check_vma=False,
    )
```

```python
import functools

import jax
import jax.numpy as jnp
from jax import lax
from jax.experimental import pallas as pl
from jax.experimental.pallas import tpu as pltpu
from jax.sharding import PartitionSpec as P

HEADS = 24
KV_HEADS = 8
HEAD = 64
FF_E = 512
TOPK = 8
MB = 2
SEQS = 4
TOK_MB = 256
ALL = ("hi", "lo", "core")


epsilon = 1e-05
theta_base = 10000.0


def layout_rows(length_rows):
    seq_ends = jnp.cumsum(length_rows, axis=1, dtype=jnp.int32)
    starts = seq_ends - length_rows
    within = jnp.arange(TOK_MB, dtype=jnp.int32)
    segment = jnp.sum(
        (within[None, :, None] >= seq_ends[:, None, :]).astype(jnp.int32), axis=2, dtype=jnp.int32
    )
    chosen = segment[:, :, None] == jnp.arange(SEQS, dtype=jnp.int32)[None, None, :]
    seq_begin = jnp.sum(jnp.where(chosen, starts[:, None, :], 0), axis=2, dtype=jnp.int32)
    position = within[None, :] - seq_begin
    segment = segment + jnp.arange(MB, dtype=jnp.int32)[:, None] * SEQS
    return (segment.reshape(-1), position.reshape(-1))


def rope_tables(position):
    half_width = HEAD // 2
    frequency = theta_base ** (-(2.0 / HEAD) * jnp.arange(half_width, dtype=jnp.float32))
    angles = position.astype(jnp.float32)[:, None] * frequency[None, :]
    return (jnp.cos(angles), jnp.sin(angles))


def rotate(values, cosine_table, sine_table):
    half_width = HEAD // 2
    front_half = values[..., :half_width]
    behind = values[..., half_width:]
    cosine_part = cosine_table[:, None, :]
    sine_part = sine_table[:, None, :]
    return jnp.concatenate(
        [
            front_half * cosine_part - behind * sine_part,
            behind * cosine_part + front_half * sine_part,
        ],
        axis=-1,
    )


def slot_tables(ids, gates, experts, capacity):
    count = experts.shape[0]
    named = ids[..., None] == experts
    picked = jnp.any(named, axis=2)
    weight = jnp.sum(jnp.where(named, gates[..., None], 0.0), axis=2)
    rows = jnp.arange(TOK_MB, dtype=jnp.int32)
    below = (rows[:, None] > rows[None, :]).astype(jnp.bfloat16)
    shaped = picked.reshape(-1, TOK_MB, count)
    slot = jnp.einsum(
        "rq,bqe->ber", below, shaped.astype(jnp.bfloat16), preferred_element_type=jnp.float32
    ).astype(jnp.int32)
    kept = jnp.transpose(shaped, (0, 2, 1))
    hit = kept[:, :, None, :] & (
        slot[:, :, None, :] == jnp.arange(capacity, dtype=jnp.int32)[None, None, :, None]
    )
    weight = jnp.transpose(weight.reshape(-1, TOK_MB, count), (0, 2, 1))
    slot_gate = jnp.sum(jnp.where(hit, weight[:, :, None, :], 0.0), axis=3)
    return hit.astype(jnp.bfloat16), slot_gate


def block_scores(queries, key_rows, segment, position):
    row_count = queries.shape[0]
    grouped = queries.reshape(row_count, KV_HEADS, HEADS // KV_HEADS, HEAD)
    scores = jnp.einsum(
        "qhgd,khd->hgqk", grouped, key_rows, preferred_element_type=jnp.float32
    ) * HEAD ** (-0.5)
    allowed = (segment[:, None] == segment[None, :]) & (position[:, None] >= position[None, :])
    return (jnp.where(allowed, scores, -1e30), grouped)


def attend_block(queries, key_rows, value_rows, segment, position):
    row_count = queries.shape[0]
    masked, grouped = block_scores(queries, key_rows, segment, position)
    row_peak = jnp.max(masked, axis=-1, keepdims=True)
    weights_exp = jnp.exp(masked - row_peak)
    row_total = jnp.sum(weights_exp, axis=-1, keepdims=True)
    probabilities = (weights_exp / row_total).astype(jnp.bfloat16)
    mixed_rows = jnp.einsum(
        "hgqk,khd->qhgd", probabilities, value_rows, preferred_element_type=jnp.float32
    )
    return (mixed_rows.reshape(row_count, HEADS * HEAD), row_peak + jnp.log(row_total))


def attend_back(queries, key_rows, value_rows, segment, position, logsum, grad_mixed):
    row_count = queries.shape[0]
    masked, grouped = block_scores(queries, key_rows, segment, position)
    exact_probs = jnp.exp(masked - logsum)
    probabilities = exact_probs.astype(jnp.bfloat16)
    grad_heads = grad_mixed.reshape(row_count, KV_HEADS, HEADS // KV_HEADS, HEAD)
    grad_probs = jnp.einsum(
        "qhgd,khd->hgqk", grad_heads, value_rows, preferred_element_type=jnp.float32
    )
    grad_values = jnp.einsum(
        "hgqk,qhgd->khd", probabilities, grad_heads, preferred_element_type=jnp.float32
    )
    grad_scores = (
        exact_probs * (grad_probs - jnp.sum(grad_probs * exact_probs, axis=-1, keepdims=True))
    ).astype(jnp.bfloat16)
    grad_queries = jnp.einsum(
        "hgqk,khd->qhgd", grad_scores, key_rows, preferred_element_type=jnp.float32
    ) * HEAD ** (-0.5)
    grad_keys = jnp.einsum(
        "hgqk,qhgd->khd", grad_scores, grouped, preferred_element_type=jnp.float32
    ) * HEAD ** (-0.5)
    return (grad_queries.reshape(row_count, HEADS, HEAD), grad_keys, grad_values)


def norm_back(values, scale, gain, grad_normed):
    scaled_grad = grad_normed * gain
    grad_gain = jnp.sum(grad_normed * values * scale, axis=0)
    grad_values = scale * scaled_grad - values * scale * scale * scale * jnp.mean(
        scaled_grad * values, axis=1, keepdims=True
    )
    return (grad_gain, grad_values)


MESH = pl.DeviceIdType.MESH


def flip(value, bits):
    bit = 1
    while bit <= bits:
        if bits & bit:
            value = value + bit * (1 - 2 * ((value // bit) % 2))
        bit *= 2
    return value


def place():
    return lax.axis_index("hi"), lax.axis_index("lo"), lax.axis_index("core")


def greet_all(sizes):
    hi_count, lo_count, _ = sizes
    count = hi_count * lo_count * 2
    hi, lo, core = place()
    me = (hi * lo_count + lo) * 2 + core
    barrier = pltpu.get_barrier_semaphore()

    def greet(step, carry):
        peer = (me + step) % count
        pl.semaphore_signal(
            barrier,
            inc=1,
            device_id=(peer // (2 * lo_count), (peer // 2) % lo_count, peer % 2),
            device_id_type=MESH,
        )
        return carry

    lax.fori_loop(1, count, greet, 0)
    pl.semaphore_wait(barrier, count - 1)


def send_rows(sizes, source, target, send_sem, recv_sem):
    hi_count, lo_count, _ = sizes
    count = hi_count * lo_count * 2
    hi, lo, core = place()
    me = (hi * lo_count + lo) * 2 + core

    def one(step, carry):
        peer = (me + step) % count
        pltpu.make_async_remote_copy(
            src_ref=source.at[peer],
            dst_ref=target.at[me],
            send_sem=send_sem,
            recv_sem=recv_sem,
            device_id=(peer // (2 * lo_count), (peer // 2) % lo_count, peer % 2),
            device_id_type=MESH,
        ).start()
        return carry

    lax.fori_loop(1, count, one, 0)


def wait_rows(source, target, send_sem, recv_sem):
    rest = pl.ds(0, source.shape[0] - 1)
    pltpu.make_async_copy(source.at[rest], source.at[rest], send_sem).wait()
    pltpu.make_async_copy(target.at[rest], target.at[rest], recv_sem).wait()


def lo_steps(lo_count, turn):
    bits = []
    bit = 1
    while bit < lo_count:
        bits.append(bit)
        bit *= 2
    if turn:
        bits = bits[::-1]
    held, steps = [0], []
    for bit in bits:
        steps.append((bit, list(held)))
        held = held + [offset ^ bit for offset in held]
    return steps


def opening_kernel(
    sizes, rows_ref, shard_ref, got_ref, full_ref, own_sem, row_sems, hi_sems, lo_sems, core_sems
):
    hi_count, lo_count, _ = sizes
    hi, lo, core = place()
    me = (hi * lo_count + lo) * 2 + core
    own = [
        pltpu.make_async_copy(shard_ref, full_ref.at[hi, lo, core], own_sem.at[0]),
        pltpu.make_async_copy(rows_ref.at[me], got_ref.at[me], own_sem.at[1]),
    ]
    for copy in own:
        copy.start()
    greet_all(sizes)

    def hop(source, at, device, sems, *index):
        return pltpu.make_async_remote_copy(
            src_ref=source,
            dst_ref=full_ref.at[at[0], at[1], at[2]],
            send_sem=sems.at[0, *index],
            recv_sem=sems.at[1, *index],
            device_id=device,
            device_id_type=MESH,
        )

    along_hi = {}
    for step in range(1, hi_count):
        along_hi[step] = hop(
            shard_ref, (hi, lo, core), (flip(hi, step), lo, core), hi_sems, step - 1
        )
        along_hi[step].start()
    send_rows(sizes, rows_ref, got_ref, row_sems.at[0], row_sems.at[1])

    def across(plane, offset, first):
        at = (flip(hi, plane), flip(lo, offset), core)
        source = shard_ref if first else full_ref.at[at[0], at[1], at[2]]
        copy = hop(source, at, (hi, lo, 1 - core), core_sems, plane, offset)
        copy.start()
        return copy

    started, waits = [], []
    for plane in range(hi_count):
        if plane:
            along_hi[plane].wait_recv()
        started.append(across(plane, 0, plane == 0))
        number = 0
        for bit, offsets in lo_steps(lo_count, plane % 2):
            for offset in offsets:
                at = (flip(hi, plane), flip(lo, offset), core)
                source = shard_ref if plane == 0 and offset == 0 else full_ref.at[at[0], at[1], at[2]]
                copy = hop(source, at, (hi, flip(lo, bit), core), lo_sems, plane, number)
                number += 1
                if offset == 0:
                    copy.start()
                    started.append(copy)
                waits.append((copy, plane, offset, bit))
    arrived = {}
    for copy, plane, offset, bit in waits:
        if offset:
            copy.start()
            started.append(copy)
        copy.wait_recv()
        started.append(across(plane, offset ^ bit, False))
    for copy in started:
        copy.wait_send()
    for step in range(1, hi_count):
        along_hi[step].wait_send()
    for plane in range(hi_count):
        for offset in range(lo_count):
            at = (flip(hi, plane), flip(lo, offset), core)
            hop(
                full_ref.at[at[0], at[1], at[2]], at, (hi, lo, 1 - core), core_sems, plane, offset
            ).wait_recv()
    wait_rows(rows_ref, got_ref, row_sems.at[0], row_sems.at[1])
    for copy in own:
        copy.wait()


def opening(sizes, rows, shard):
    hi_count, lo_count, _ = sizes
    anywhere = pl.BlockSpec(memory_space=pl.ANY)
    return pl.pallas_call(
        functools.partial(opening_kernel, sizes),
        out_shape=(
            jax.ShapeDtypeStruct(rows.shape, rows.dtype),
            jax.ShapeDtypeStruct(sizes + shard.shape, shard.dtype),
        ),
        in_specs=[anywhere] * 2,
        out_specs=(anywhere, anywhere),
        scratch_shapes=[
            pltpu.SemaphoreType.DMA((2,)),
            pltpu.SemaphoreType.DMA((2,)),
            pltpu.SemaphoreType.DMA((2, hi_count)),
            pltpu.SemaphoreType.DMA((2, hi_count, lo_count)),
            pltpu.SemaphoreType.DMA((2, hi_count, lo_count)),
        ],
        compiler_params=pltpu.CompilerParams(collective_id=0, has_side_effects=True),
        name="opening",
    )(rows, shard)


def add_blocks(target, first, second):
    rows = target.shape[0]
    tile = 16 if rows % 16 == 0 else rows

    def one(index, carry):
        at = pl.ds(index * tile, tile)
        target[at, :] = (
            first[at, :].astype(jnp.float32) + second[at, :].astype(jnp.float32)
        ).astype(target.dtype)
        return carry

    lax.fori_loop(0, rows // tile, one, 0)


def closing_kernel(
    sizes, out_ref, grad_ref, parts_ref, got_out, got_grad, sum_ref,
    from_core, from_lo, from_hi, held, own_sem, row_sems, hi_sems, lo_sems, core_sems
):
    hi_count, lo_count, _ = sizes
    hi, lo, core = place()
    me = (hi * lo_count + lo) * 2 + core
    own = [
        pltpu.make_async_copy(out_ref.at[me], got_out.at[me], own_sem.at[0]),
        pltpu.make_async_copy(grad_ref.at[me], got_grad.at[me], own_sem.at[1]),
    ]
    for copy in own:
        copy.start()
    greet_all(sizes)

    def hop(source, target, device, sems, *index):
        return pltpu.make_async_remote_copy(
            src_ref=source,
            dst_ref=target,
            send_sem=sems.at[0, *index],
            recv_sem=sems.at[1, *index],
            device_id=device,
            device_id_type=MESH,
        )

    planes = [plane for plane in range(1, hi_count)] + [0]
    across = {}
    for plane in planes:
        for offset in reversed(range(lo_count)):
            across[plane, offset] = hop(
                parts_ref.at[flip(hi, plane), flip(lo, offset), 1 - core],
                from_core.at[plane, offset],
                (hi, lo, 1 - core),
                core_sems,
                plane,
                offset,
            )
            across[plane, offset].start()
    send_rows(sizes, grad_ref, got_grad, row_sems.at[0, 0], row_sems.at[1, 0])
    send_rows(sizes, out_ref, got_out, row_sems.at[0, 1], row_sems.at[1, 1])
    started = []
    plans = {plane: lo_steps(lo_count, plane % 2)[::-1] for plane in planes}
    moves = {}
    for depth in range(len(plans[0])):
        for plane in planes:
            bit, kept = plans[plane][depth]
            base = lo_count - 2 * len(kept)
            if depth == 0:
                for offset in [keep ^ bit for keep in kept] + kept:
                    across[plane, offset].wait_recv()
                    add_blocks(
                        held.at[plane, offset],
                        parts_ref.at[flip(hi, plane), flip(lo, offset), core],
                        from_core.at[plane, offset],
                    )
            else:
                before = plans[plane][depth - 1]
                for number, offset in enumerate(before[1]):
                    copy, spot = moves[plane, depth - 1, offset]
                    copy.wait_recv()
                    add_blocks(held.at[plane, offset], held.at[plane, offset], from_lo.at[plane, spot])
            for number, offset in enumerate(kept):
                spot = base + number
                copy = hop(
                    held.at[plane, offset ^ bit],
                    from_lo.at[plane, spot],
                    (hi, flip(lo, bit), core),
                    lo_sems,
                    plane,
                    spot,
                )
                copy.start()
                started.append(copy)
                moves[plane, depth, offset] = (copy, spot)
    last = len(plans[0]) - 1
    along = {}
    for plane in planes:
        copy, spot = moves[plane, last, 0]
        copy.wait_recv()
        add_blocks(held.at[plane, 0], held.at[plane, 0], from_lo.at[plane, spot])
        if plane:
            along[plane] = hop(
                held.at[plane, 0],
                from_hi.at[plane],
                (flip(hi, plane), lo, core),
                hi_sems,
                plane,
            )
            along[plane].start()
            started.append(along[plane])
    for plane in range(1, hi_count):
        along[plane].wait_recv()
    rows = sum_ref.shape[0]
    tile = 16 if rows % 16 == 0 else rows

    def total(index, carry):
        at = pl.ds(index * tile, tile)
        value = held[0, 0, at, :].astype(jnp.float32)
        for plane in range(1, hi_count):
            value = value + from_hi[plane, at, :].astype(jnp.float32)
        sum_ref[at, :] = value
        return carry

    lax.fori_loop(0, rows // tile, total, 0)
    for copy in started:
        copy.wait_send()
    for copy in across.values():
        copy.wait_send()
    wait_rows(grad_ref, got_grad, row_sems.at[0, 0], row_sems.at[1, 0])
    wait_rows(out_ref, got_out, row_sems.at[0, 1], row_sems.at[1, 1])
    for copy in own:
        copy.wait()


def closing(sizes, out_rows, grad_rows, parts):
    hi_count, lo_count, _ = sizes
    block = parts.shape[3:]
    anywhere = pl.BlockSpec(memory_space=pl.ANY)
    near = pl.BlockSpec(memory_space=pltpu.VMEM)
    return pl.pallas_call(
        functools.partial(closing_kernel, sizes),
        out_shape=(
            jax.ShapeDtypeStruct(out_rows.shape, out_rows.dtype),
            jax.ShapeDtypeStruct(grad_rows.shape, grad_rows.dtype),
            jax.ShapeDtypeStruct(block, jnp.float32),
        ),
        in_specs=[anywhere, anywhere, near],
        out_specs=(anywhere, anywhere, near),
        scratch_shapes=[
            pltpu.VMEM((hi_count, lo_count) + block, jnp.bfloat16),
            pltpu.VMEM((hi_count, lo_count) + block, jnp.bfloat16),
            pltpu.VMEM((hi_count,) + block, jnp.bfloat16),
            pltpu.VMEM((hi_count, lo_count) + block, jnp.bfloat16),
            pltpu.SemaphoreType.DMA((2,)),
            pltpu.SemaphoreType.DMA((2, 2)),
            pltpu.SemaphoreType.DMA((2, hi_count)),
            pltpu.SemaphoreType.DMA((2, hi_count, lo_count)),
            pltpu.SemaphoreType.DMA((2, hi_count, lo_count)),
        ],
        compiler_params=pltpu.CompilerParams(
            collective_id=1, has_side_effects=True, vmem_limit_bytes=60 << 20
        ),
        name="closing",
    )(out_rows, grad_rows, parts)


def shards(
    tokens,
    cotangent,
    permutation,
    lengths,
    expert_ids,
    gate_weights,
    attn_gain,
    qkv_weight,
    out_weight,
    ffn_gain,
    expert_in,
    expert_out,
):
    device_count = lax.axis_size(ALL)
    hi_count = lax.axis_size("hi")
    lo_count = lax.axis_size("lo")
    tok_dev = permutation.shape[0]
    model_width = tokens.shape[1]
    peer_rows = tok_dev // device_count
    q_dim = HEADS * HEAD
    kv_dim = KV_HEADS * HEAD
    positions = jnp.arange(tok_dev, dtype=jnp.int32)
    expert_count = expert_in.shape[2] * device_count // FF_E
    capacity = TOK_MB * TOPK // expert_count
    source = permutation // tok_dev
    local_row = permutation % tok_dev
    from_source = (source[:, None] == jnp.arange(device_count, dtype=jnp.int32)[None, :]).astype(
        jnp.int32
    )
    earlier = jnp.cumsum(from_source, axis=0, dtype=jnp.int32) - from_source
    arrival = source * peer_rows + jnp.sum(earlier * from_source, axis=1, dtype=jnp.int32)
    arrival_match = arrival[:, None] == positions[None, :]
    wanted = jnp.sum(jnp.where(arrival_match, local_row[:, None], 0), axis=0, dtype=jnp.int32)
    by_arrival = jnp.sum(jnp.where(arrival_match, positions[:, None], 0), axis=0, dtype=jnp.int32)
    asked_rows = lax.all_to_all(
        wanted.reshape(device_count, peer_rows),
        ALL,
        split_axis=0,
        concat_axis=0,
        tiled=True,
    ).reshape(tok_dev)
    asked_match = asked_rows[:, None] == positions[None, :]
    by_asked = jnp.sum(jnp.where(asked_match, positions[:, None], 0), axis=0, dtype=jnp.int32)
    sizes = (hi_count, lo_count, 2)
    shard_rows = qkv_weight.shape[0]
    qkv_cols = qkv_weight.shape[1]
    weight_shard = jnp.concatenate(
        [
            qkv_weight,
            out_weight,
            attn_gain[:, None],
            ffn_gain[:, None],
            jnp.zeros((shard_rows, 126), jnp.bfloat16),
        ],
        axis=1,
    )
    asked_tokens = jnp.take(tokens, asked_rows, axis=0).reshape(device_count, peer_rows, model_width)
    asked_grads = jnp.take(cotangent, asked_rows, axis=0).reshape(
        device_count, peer_rows, model_width
    )
    got_rows, packed = opening(sizes, asked_tokens, weight_shard)
    packed = packed.reshape(model_width, -1)
    got_rows, asked_grads = lax.optimization_barrier((got_rows, asked_grads))
    got_grad = lax.all_to_all(asked_grads, ALL, split_axis=0, concat_axis=0, tiled=True)
    rows_in = jnp.take(got_rows.reshape(tok_dev, model_width), arrival, axis=0).astype(jnp.float32)
    qkv_full = packed[:, :qkv_cols]
    out_full = packed[:, qkv_cols : qkv_cols + model_width]
    gain_pair = packed[:, qkv_cols + model_width :].astype(jnp.float32)
    gain_one = gain_pair[:, 0]
    gain_two = gain_pair[:, 1]
    shard_cols = expert_in.shape[2]
    weights_in = lax.all_gather(
        expert_in.reshape(model_width, 2 * shard_cols), ("hi", "core"), axis=0
    ).reshape(hi_count, 2, model_width, 2 * shard_cols)
    weights_out = lax.all_gather(expert_out, ("hi", "core"), axis=0).reshape(
        hi_count, 2, shard_cols, model_width
    )
    segment, position = layout_rows(lengths)
    scale_one = lax.rsqrt(jnp.mean(rows_in * rows_in, axis=1, keepdims=True) + epsilon)
    normed = (rows_in * scale_one * gain_one).astype(jnp.bfloat16)
    projected = jnp.dot(normed, qkv_full, preferred_element_type=jnp.float32)
    cosine_table, sine_table = rope_tables(position)
    queries = rotate(
        projected[:, :q_dim].reshape(tok_dev, HEADS, HEAD), cosine_table, sine_table
    ).astype(jnp.bfloat16)
    key_rows = rotate(
        projected[:, q_dim : q_dim + kv_dim].reshape(tok_dev, KV_HEADS, HEAD),
        cosine_table,
        sine_table,
    ).astype(jnp.bfloat16)
    value_rows = (
        projected[:, q_dim + kv_dim :].reshape(tok_dev, KV_HEADS, HEAD).astype(jnp.bfloat16)
    )
    block_rows = min(tok_dev, max(TOK_MB, 512))
    mixed_part, logsum = attend_block(queries, key_rows, value_rows, segment, position)
    logsums = [logsum]
    mixed_rows = mixed_part.astype(jnp.bfloat16)
    attended = jnp.dot(mixed_rows, out_full, preferred_element_type=jnp.float32)
    residual = rows_in + attended
    scale_two = lax.rsqrt(jnp.mean(residual * residual, axis=1, keepdims=True) + epsilon)
    normed_two = (residual * scale_two * gain_two).astype(jnp.bfloat16)
    got_grad, normed_two = lax.optimization_barrier((got_grad, normed_two))
    grad_bf = jnp.take(got_grad.reshape(tok_dev, model_width), arrival, axis=0)
    grad_output = grad_bf.astype(jnp.float32)
    home = lax.axis_index("lo")

    def spread(block):
        return [block] + [swap(block, step) for step in range(1, lo_count)]

    def swap(block, step):
        return lax.ppermute(block, "lo", [(i, i ^ step) for i in range(lo_count)])

    ids_all = jnp.stack(spread(expert_ids))
    gates_all = jnp.stack(spread(gate_weights))
    choose, slot_gate = slot_tables(
        ids_all.reshape(-1, TOK_MB, TOPK),
        gates_all.reshape(-1, TOK_MB, TOPK),
        home + lo_count * jnp.arange(hi_count, dtype=jnp.int32),
        capacity,
    )
    rows_all = jnp.stack(spread(normed_two)).reshape(lo_count * MB, TOK_MB, model_width)
    grads_all = jnp.stack(spread(grad_bf)).reshape(lo_count * MB, TOK_MB, model_width)
    expert_rows = jnp.einsum(
        "becr,brd->ebcd", choose, rows_all, preferred_element_type=jnp.float32
    ).astype(jnp.bfloat16).reshape(hi_count, -1, model_width)
    gate_up = jnp.einsum(
        "erd,ekdf->ekrf", expert_rows, weights_in, preferred_element_type=jnp.float32
    )
    gate_part = gate_up[..., :shard_cols]
    up_part = gate_up[..., shard_cols:]
    sigmoid_gate = jax.nn.sigmoid(gate_part)
    hidden = (gate_part * sigmoid_gate * up_part).astype(jnp.bfloat16)
    slot_weight = jnp.transpose(slot_gate, (1, 0, 2)).reshape(hi_count, -1, 1)
    produced = (
        jnp.einsum("ekrf,ekfd->erd", hidden, weights_out, preferred_element_type=jnp.float32)
        * slot_weight
    ).astype(jnp.bfloat16)

    def collect(slot_values):
        parts = jnp.einsum(
            "becr,ebcd->brd",
            choose,
            slot_values.reshape(hi_count, lo_count * MB, capacity, model_width),
            preferred_element_type=jnp.float32,
        ).reshape(lo_count, tok_dev, model_width)
        total = parts[0]
        for step in range(1, lo_count):
            total = total + swap(parts[step].astype(jnp.bfloat16), step).astype(jnp.float32)
        return total

    output_rows = (residual + collect(produced)).astype(jnp.bfloat16)
    grad_expert = (
        jnp.einsum("becr,brd->ebcd", choose, grads_all, preferred_element_type=jnp.float32).reshape(
            hi_count, -1, model_width
        )
        * slot_weight
    ).astype(jnp.bfloat16)
    grad_hidden = jnp.einsum(
        "erd,ekfd->ekrf", grad_expert, weights_out, preferred_element_type=jnp.float32
    )
    grad_weights_out = jnp.einsum(
        "ekrf,erd->ekfd", hidden, grad_expert, preferred_element_type=jnp.float32
    )
    grad_gate = grad_hidden * up_part * sigmoid_gate * (1.0 + gate_part * (1.0 - sigmoid_gate))
    grad_up = grad_hidden * (gate_part * sigmoid_gate)
    grad_gate_up = jnp.concatenate([grad_gate, grad_up], axis=-1).astype(jnp.bfloat16)
    grad_weights_in = jnp.einsum(
        "erd,ekrf->ekdf", expert_rows, grad_gate_up, preferred_element_type=jnp.float32
    )
    grad_expert_rows = jnp.einsum(
        "ekrf,ekdf->erd", grad_gate_up, weights_in, preferred_element_type=jnp.float32
    ).astype(jnp.bfloat16)
    grad_normed_two = collect(grad_expert_rows)
    grad_normed_two, grad_weights_in, grad_weights_out = lax.optimization_barrier(
        (
            grad_normed_two,
            grad_weights_in.astype(jnp.bfloat16),
            grad_weights_out.astype(jnp.bfloat16),
        )
    )
    shard_out = lax.psum_scatter(
        grad_weights_out.reshape(hi_count * 2 * shard_cols, model_width),
        ("hi", "core"),
        scatter_dimension=0,
        tiled=True,
    ).astype(jnp.float32)
    shard_in = (
        lax.psum_scatter(
            grad_weights_in.reshape(hi_count * 2 * model_width, 2 * shard_cols),
            ("hi", "core"),
            scatter_dimension=0,
            tiled=True,
        )
        .astype(jnp.float32)
        .reshape(model_width, 2, shard_cols)
    )
    grad_gain_two, grad_from_norm = norm_back(residual, scale_two, gain_two, grad_normed_two)
    grad_residual = grad_output + grad_from_norm
    grad_attended = grad_residual.astype(jnp.bfloat16)
    grad_out_weight = jnp.einsum(
        "nq,nd->qd", mixed_rows, grad_attended, preferred_element_type=jnp.float32
    )
    grad_mixed = jnp.einsum(
        "nd,qd->nq", grad_attended, out_full, preferred_element_type=jnp.float32
    ).astype(jnp.bfloat16)
    grad_query_parts = []
    grad_key_parts = []
    grad_value_parts = []
    for block_number, block_start in enumerate(range(0, tok_dev, block_rows)):
        grad_q, grad_k, grad_v = attend_back(
            queries, key_rows, value_rows, segment, position, logsums[block_number], grad_mixed
        )
        grad_query_parts.append(grad_q)
        grad_key_parts.append(grad_k)
        grad_value_parts.append(grad_v)
    grad_queries = rotate(grad_query_parts[0], cosine_table, -sine_table)
    grad_keys = rotate(grad_key_parts[0], cosine_table, -sine_table)
    grad_values = grad_value_parts[0]
    grad_projected = jnp.concatenate(
        [
            grad_queries.reshape(tok_dev, q_dim),
            grad_keys.reshape(tok_dev, kv_dim),
            grad_values.reshape(tok_dev, kv_dim),
        ],
        axis=1,
    ).astype(jnp.bfloat16)
    grad_qkv_weight = jnp.einsum(
        "nd,nc->dc", normed, grad_projected, preferred_element_type=jnp.float32
    )
    grad_normed = jnp.einsum(
        "nc,dc->nd", grad_projected, qkv_full, preferred_element_type=jnp.float32
    )
    grad_gain_one, grad_from_first = norm_back(rows_in, scale_one, gain_one, grad_normed)
    grad_input = (grad_residual + grad_from_first).astype(jnp.bfloat16)
    gains = jnp.pad(jnp.stack([grad_gain_one, grad_gain_two], axis=1), ((0, 0), (0, 126)))
    parts = jnp.concatenate(
        [
            grad_qkv_weight.astype(jnp.bfloat16),
            grad_out_weight.astype(jnp.bfloat16),
            gains.astype(jnp.bfloat16),
        ],
        axis=1,
    ).reshape(sizes + (shard_rows, -1))
    home_out, home_grad, sums = closing(
        sizes,
        jnp.take(output_rows, by_arrival, axis=0).reshape(device_count, peer_rows, model_width),
        jnp.take(grad_input, by_arrival, axis=0).reshape(device_count, peer_rows, model_width),
        parts,
    )
    shard_qkv = sums[:, :qkv_cols]
    shard_attn_out = sums[:, qkv_cols : qkv_cols + model_width]
    shard_gain_one = sums[:, qkv_cols + model_width]
    shard_gain_two = sums[:, qkv_cols + model_width + 1]
    output = jnp.take(home_out.reshape(tok_dev, model_width), by_asked, axis=0)
    input_grad = jnp.take(home_grad.reshape(tok_dev, model_width), by_asked, axis=0)
    return (
        output,
        input_grad,
        shard_gain_one,
        shard_qkv,
        shard_attn_out,
        shard_gain_two,
        shard_in,
        shard_out,
    )


def solution(mesh):
    dp_count = mesh.shape["dp"]
    hi_count = 4 if dp_count % 4 == 0 else 1
    split = jax.sharding.Mesh(
        mesh.devices.reshape(hi_count, dp_count // hi_count, mesh.shape["expert"]), ALL
    )
    rows, columns = P(ALL, None), P(None, None, ALL)
    return jax.shard_map(
        shards,
        mesh=split,
        in_specs=(rows, rows, P(ALL), rows, rows, rows, P(ALL), rows, rows, P(ALL), columns, rows),
        out_specs=(rows, rows, P(ALL), rows, rows, P(ALL), columns, rows),
        check_vma=False,
    )
```

```python
import functools

import jax
import jax.numpy as jnp
from jax import lax
from jax.experimental import pallas as pl
from jax.experimental.pallas import tpu as pltpu
from jax.sharding import PartitionSpec as P

HEADS = 24
KV_HEADS = 8
HEAD = 64
FF_E = 512
TOPK = 8
MB = 2
SEQS = 4
TOK_MB = 256
ALL = ("hi", "lo", "core")


epsilon = 1e-05
theta_base = 10000.0


def layout_rows(length_rows):
    seq_ends = jnp.cumsum(length_rows, axis=1, dtype=jnp.int32)
    starts = seq_ends - length_rows
    within = jnp.arange(TOK_MB, dtype=jnp.int32)
    segment = jnp.sum(
        (within[None, :, None] >= seq_ends[:, None, :]).astype(jnp.int32), axis=2, dtype=jnp.int32
    )
    chosen = segment[:, :, None] == jnp.arange(SEQS, dtype=jnp.int32)[None, None, :]
    seq_begin = jnp.sum(jnp.where(chosen, starts[:, None, :], 0), axis=2, dtype=jnp.int32)
    position = within[None, :] - seq_begin
    segment = segment + jnp.arange(MB, dtype=jnp.int32)[:, None] * SEQS
    return (segment.reshape(-1), position.reshape(-1))


def rope_tables(position):
    half_width = HEAD // 2
    frequency = theta_base ** (-(2.0 / HEAD) * jnp.arange(half_width, dtype=jnp.float32))
    angles = position.astype(jnp.float32)[:, None] * frequency[None, :]
    return (jnp.cos(angles), jnp.sin(angles))


def rotate(values, cosine_table, sine_table):
    half_width = HEAD // 2
    front_half = values[..., :half_width]
    behind = values[..., half_width:]
    cosine_part = cosine_table[:, None, :]
    sine_part = sine_table[:, None, :]
    return jnp.concatenate(
        [
            front_half * cosine_part - behind * sine_part,
            behind * cosine_part + front_half * sine_part,
        ],
        axis=-1,
    )


def slot_tables(ids, gates, experts, capacity):
    count = experts.shape[0]
    named = ids[..., None] == experts
    picked = jnp.any(named, axis=2)
    weight = jnp.sum(jnp.where(named, gates[..., None], 0.0), axis=2)
    rows = jnp.arange(TOK_MB, dtype=jnp.int32)
    below = (rows[:, None] > rows[None, :]).astype(jnp.bfloat16)
    shaped = picked.reshape(-1, TOK_MB, count)
    slot = jnp.einsum(
        "rq,bqe->ber", below, shaped.astype(jnp.bfloat16), preferred_element_type=jnp.float32
    ).astype(jnp.int32)
    kept = jnp.transpose(shaped, (0, 2, 1))
    hit = kept[:, :, None, :] & (
        slot[:, :, None, :] == jnp.arange(capacity, dtype=jnp.int32)[None, None, :, None]
    )
    weight = jnp.transpose(weight.reshape(-1, TOK_MB, count), (0, 2, 1))
    slot_gate = jnp.sum(jnp.where(hit, weight[:, :, None, :], 0.0), axis=3)
    return hit.astype(jnp.bfloat16), slot_gate


def by_batch(rows, heads):
    return rows.reshape(-1, TOK_MB, KV_HEADS, heads // KV_HEADS, HEAD)


def block_scores(queries, key_rows, segment, position):
    scores = jnp.einsum(
        "bqhgd,bkhd->bhgqk", queries, key_rows, preferred_element_type=jnp.float32
    ) * HEAD ** (-0.5)
    allowed = (segment[:, :, None] == segment[:, None, :]) & (
        position[:, :, None] >= position[:, None, :]
    )
    return jnp.where(allowed[:, None, None], scores, -1e30)


def attend_block(queries, key_rows, value_rows, segment, position):
    queries = by_batch(queries, HEADS)
    key_rows = by_batch(key_rows, KV_HEADS)[:, :, :, 0]
    value_rows = by_batch(value_rows, KV_HEADS)[:, :, :, 0]
    segment = segment.reshape(-1, TOK_MB)
    position = position.reshape(-1, TOK_MB)
    masked = block_scores(queries, key_rows, segment, position)
    row_peak = jnp.max(masked, axis=-1, keepdims=True)
    weights_exp = jnp.exp(masked - row_peak)
    row_total = jnp.sum(weights_exp, axis=-1, keepdims=True)
    probabilities = (weights_exp / row_total).astype(jnp.bfloat16)
    mixed_rows = jnp.einsum(
        "bhgqk,bkhd->bqhgd", probabilities, value_rows, preferred_element_type=jnp.float32
    )
    return (mixed_rows.reshape(-1, HEADS * HEAD), row_peak + jnp.log(row_total))


def attend_back(queries, key_rows, value_rows, segment, position, logsum, grad_mixed):
    queries = by_batch(queries, HEADS)
    key_rows = by_batch(key_rows, KV_HEADS)[:, :, :, 0]
    value_rows = by_batch(value_rows, KV_HEADS)[:, :, :, 0]
    segment = segment.reshape(-1, TOK_MB)
    position = position.reshape(-1, TOK_MB)
    masked = block_scores(queries, key_rows, segment, position)
    exact_probs = jnp.exp(masked - logsum)
    probabilities = exact_probs.astype(jnp.bfloat16)
    grad_heads = by_batch(grad_mixed, HEADS)
    grad_probs = jnp.einsum(
        "bqhgd,bkhd->bhgqk", grad_heads, value_rows, preferred_element_type=jnp.float32
    )
    grad_values = jnp.einsum(
        "bhgqk,bqhgd->bkhd", probabilities, grad_heads, preferred_element_type=jnp.float32
    )
    grad_scores = (
        exact_probs * (grad_probs - jnp.sum(grad_probs * exact_probs, axis=-1, keepdims=True))
    ).astype(jnp.bfloat16)
    grad_queries = jnp.einsum(
        "bhgqk,bkhd->bqhgd", grad_scores, key_rows, preferred_element_type=jnp.float32
    ) * HEAD ** (-0.5)
    grad_keys = jnp.einsum(
        "bhgqk,bqhgd->bkhd", grad_scores, queries, preferred_element_type=jnp.float32
    ) * HEAD ** (-0.5)
    return (
        grad_queries.reshape(-1, HEADS, HEAD),
        grad_keys.reshape(-1, KV_HEADS, HEAD),
        grad_values.reshape(-1, KV_HEADS, HEAD),
    )


def norm_back(values, scale, gain, grad_normed):
    scaled_grad = grad_normed * gain
    grad_gain = jnp.sum(grad_normed * values * scale, axis=0)
    grad_values = scale * scaled_grad - values * scale * scale * scale * jnp.mean(
        scaled_grad * values, axis=1, keepdims=True
    )
    return (grad_gain, grad_values)


MESH = pl.DeviceIdType.MESH


def flip(value, bits):
    bit = 1
    while bit <= bits:
        if bits & bit:
            value = value + bit * (1 - 2 * ((value // bit) % 2))
        bit *= 2
    return value


def place():
    return lax.axis_index("hi"), lax.axis_index("lo"), lax.axis_index("core")


def greet_all(sizes):
    hi_count, lo_count, _ = sizes
    count = hi_count * lo_count * 2
    hi, lo, core = place()
    me = (hi * lo_count + lo) * 2 + core
    barrier = pltpu.get_barrier_semaphore()

    def greet(step, carry):
        peer = (me + step) % count
        pl.semaphore_signal(
            barrier,
            inc=1,
            device_id=(peer // (2 * lo_count), (peer // 2) % lo_count, peer % 2),
            device_id_type=MESH,
        )
        return carry

    lax.fori_loop(1, count, greet, 0)
    pl.semaphore_wait(barrier, count - 1)


def send_rows(sizes, source, target, send_sem, recv_sem):
    hi_count, lo_count, _ = sizes
    count = hi_count * lo_count * 2
    hi, lo, core = place()
    me = (hi * lo_count + lo) * 2 + core

    def one(step, carry):
        peer = (me + step) % count
        pltpu.make_async_remote_copy(
            src_ref=source.at[peer],
            dst_ref=target.at[me],
            send_sem=send_sem,
            recv_sem=recv_sem,
            device_id=(peer // (2 * lo_count), (peer // 2) % lo_count, peer % 2),
            device_id_type=MESH,
        ).start()
        return carry

    lax.fori_loop(1, count, one, 0)


def wait_rows(source, target, send_sem, recv_sem):
    rest = pl.ds(0, source.shape[0] - 1)
    pltpu.make_async_copy(source.at[rest], source.at[rest], send_sem).wait()
    pltpu.make_async_copy(target.at[rest], target.at[rest], recv_sem).wait()


def lo_steps(lo_count, turn):
    bits = []
    bit = 1
    while bit < lo_count:
        bits.append(bit)
        bit *= 2
    if turn:
        bits = bits[::-1]
    held, steps = [0], []
    for bit in bits:
        steps.append((bit, list(held)))
        held = held + [offset ^ bit for offset in held]
    return steps


def opening_kernel(
    sizes, rows_ref, grads_ref, shard_ref, got_ref, got_grads_ref, full_ref,
    own_sem, row_sems, hi_sems, lo_sems, core_sems
):
    hi_count, lo_count, _ = sizes
    hi, lo, core = place()
    me = (hi * lo_count + lo) * 2 + core
    own = [
        pltpu.make_async_copy(shard_ref, full_ref.at[hi, lo, core], own_sem.at[0]),
        pltpu.make_async_copy(rows_ref.at[me], got_ref.at[me], own_sem.at[1]),
        pltpu.make_async_copy(grads_ref.at[me], got_grads_ref.at[me], own_sem.at[2]),
    ]
    for copy in own:
        copy.start()
    greet_all(sizes)

    def hop(source, at, device, sems, *index):
        return pltpu.make_async_remote_copy(
            src_ref=source,
            dst_ref=full_ref.at[at[0], at[1], at[2]],
            send_sem=sems.at[0, *index],
            recv_sem=sems.at[1, *index],
            device_id=device,
            device_id_type=MESH,
        )

    along_hi = {}
    for step in range(1, hi_count):
        along_hi[step] = hop(
            shard_ref, (hi, lo, core), (flip(hi, step), lo, core), hi_sems, step - 1
        )
        along_hi[step].start()
    send_rows(sizes, rows_ref, got_ref, row_sems.at[0, 0], row_sems.at[1, 0])
    send_rows(sizes, grads_ref, got_grads_ref, row_sems.at[0, 1], row_sems.at[1, 1])

    def across(plane, offset, first):
        at = (flip(hi, plane), flip(lo, offset), core)
        source = shard_ref if first else full_ref.at[at[0], at[1], at[2]]
        copy = hop(source, at, (hi, lo, 1 - core), core_sems, plane, offset)
        copy.start()
        return copy

    started, waits = [], []
    for plane in range(hi_count):
        if plane:
            along_hi[plane].wait_recv()
        started.append(across(plane, 0, plane == 0))
        number = 0
        for bit, offsets in lo_steps(lo_count, plane % 2):
            for offset in offsets:
                at = (flip(hi, plane), flip(lo, offset), core)
                source = shard_ref if plane == 0 and offset == 0 else full_ref.at[at[0], at[1], at[2]]
                copy = hop(source, at, (hi, flip(lo, bit), core), lo_sems, plane, number)
                number += 1
                if offset == 0:
                    copy.start()
                    started.append(copy)
                waits.append((copy, plane, offset, bit))
    arrived = {}
    for copy, plane, offset, bit in waits:
        if offset:
            copy.start()
            started.append(copy)
        copy.wait_recv()
        started.append(across(plane, offset ^ bit, False))
    for copy in started:
        copy.wait_send()
    for step in range(1, hi_count):
        along_hi[step].wait_send()
    for plane in range(hi_count):
        for offset in range(lo_count):
            at = (flip(hi, plane), flip(lo, offset), core)
            hop(
                full_ref.at[at[0], at[1], at[2]], at, (hi, lo, 1 - core), core_sems, plane, offset
            ).wait_recv()
    wait_rows(rows_ref, got_ref, row_sems.at[0, 0], row_sems.at[1, 0])
    wait_rows(grads_ref, got_grads_ref, row_sems.at[0, 1], row_sems.at[1, 1])
    for copy in own:
        copy.wait()


def opening(sizes, rows, grads, shard):
    hi_count, lo_count, _ = sizes
    anywhere = pl.BlockSpec(memory_space=pl.ANY)
    return pl.pallas_call(
        functools.partial(opening_kernel, sizes),
        out_shape=(
            jax.ShapeDtypeStruct(rows.shape, rows.dtype),
            jax.ShapeDtypeStruct(grads.shape, grads.dtype),
            jax.ShapeDtypeStruct(sizes + shard.shape, shard.dtype),
        ),
        in_specs=[anywhere] * 3,
        out_specs=(anywhere, anywhere, anywhere),
        scratch_shapes=[
            pltpu.SemaphoreType.DMA((3,)),
            pltpu.SemaphoreType.DMA((2, 2)),
            pltpu.SemaphoreType.DMA((2, hi_count)),
            pltpu.SemaphoreType.DMA((2, hi_count, lo_count)),
            pltpu.SemaphoreType.DMA((2, hi_count, lo_count)),
        ],
        compiler_params=pltpu.CompilerParams(collective_id=0, has_side_effects=True),
        name="opening",
    )(rows, grads, shard)


def add_blocks(target, first, second):
    rows = target.shape[0]
    tile = 16 if rows % 16 == 0 else rows

    def one(index, carry):
        at = pl.ds(index * tile, tile)
        target[at, :] = (
            first[at, :].astype(jnp.float32) + second[at, :].astype(jnp.float32)
        ).astype(target.dtype)
        return carry

    lax.fori_loop(0, rows // tile, one, 0)


def closing_kernel(
    sizes, out_ref, grad_ref, parts_ref, got_out, got_grad, sum_ref,
    from_core, from_lo, from_hi, held, own_sem, row_sems, hi_sems, lo_sems, core_sems
):
    hi_count, lo_count, _ = sizes
    hi, lo, core = place()
    me = (hi * lo_count + lo) * 2 + core
    own = [
        pltpu.make_async_copy(out_ref.at[me], got_out.at[me], own_sem.at[0]),
        pltpu.make_async_copy(grad_ref.at[me], got_grad.at[me], own_sem.at[1]),
    ]
    for copy in own:
        copy.start()
    greet_all(sizes)

    def hop(source, target, device, sems, *index):
        return pltpu.make_async_remote_copy(
            src_ref=source,
            dst_ref=target,
            send_sem=sems.at[0, *index],
            recv_sem=sems.at[1, *index],
            device_id=device,
            device_id_type=MESH,
        )

    planes = [plane for plane in range(1, hi_count)] + [0]
    across = {}
    for plane in planes:
        for offset in reversed(range(lo_count)):
            across[plane, offset] = hop(
                parts_ref.at[flip(hi, plane), flip(lo, offset), 1 - core],
                from_core.at[plane, offset],
                (hi, lo, 1 - core),
                core_sems,
                plane,
                offset,
            )
            across[plane, offset].start()
    send_rows(sizes, grad_ref, got_grad, row_sems.at[0, 0], row_sems.at[1, 0])
    send_rows(sizes, out_ref, got_out, row_sems.at[0, 1], row_sems.at[1, 1])
    started = []
    plans = {plane: lo_steps(lo_count, plane % 2)[::-1] for plane in planes}
    moves = {}
    for depth in range(len(plans[0])):
        for plane in planes:
            bit, kept = plans[plane][depth]
            base = lo_count - 2 * len(kept)
            if depth == 0:
                for offset in [keep ^ bit for keep in kept] + kept:
                    across[plane, offset].wait_recv()
                    add_blocks(
                        held.at[plane, offset],
                        parts_ref.at[flip(hi, plane), flip(lo, offset), core],
                        from_core.at[plane, offset],
                    )
            else:
                before = plans[plane][depth - 1]
                for number, offset in enumerate(before[1]):
                    copy, spot = moves[plane, depth - 1, offset]
                    copy.wait_recv()
                    add_blocks(held.at[plane, offset], held.at[plane, offset], from_lo.at[plane, spot])
            for number, offset in enumerate(kept):
                spot = base + number
                copy = hop(
                    held.at[plane, offset ^ bit],
                    from_lo.at[plane, spot],
                    (hi, flip(lo, bit), core),
                    lo_sems,
                    plane,
                    spot,
                )
                copy.start()
                started.append(copy)
                moves[plane, depth, offset] = (copy, spot)
    last = len(plans[0]) - 1
    along = {}
    for plane in planes:
        copy, spot = moves[plane, last, 0]
        copy.wait_recv()
        add_blocks(held.at[plane, 0], held.at[plane, 0], from_lo.at[plane, spot])
        if plane:
            along[plane] = hop(
                held.at[plane, 0],
                from_hi.at[plane],
                (flip(hi, plane), lo, core),
                hi_sems,
                plane,
            )
            along[plane].start()
            started.append(along[plane])
    for plane in range(1, hi_count):
        along[plane].wait_recv()
    rows = sum_ref.shape[0]
    tile = 16 if rows % 16 == 0 else rows

    def total(index, carry):
        at = pl.ds(index * tile, tile)
        value = held[0, 0, at, :].astype(jnp.float32)
        for plane in range(1, hi_count):
            value = value + from_hi[plane, at, :].astype(jnp.float32)
        sum_ref[at, :] = value
        return carry

    lax.fori_loop(0, rows // tile, total, 0)
    for copy in started:
        copy.wait_send()
    for copy in across.values():
        copy.wait_send()
    wait_rows(grad_ref, got_grad, row_sems.at[0, 0], row_sems.at[1, 0])
    wait_rows(out_ref, got_out, row_sems.at[0, 1], row_sems.at[1, 1])
    for copy in own:
        copy.wait()


def closing(sizes, out_rows, grad_rows, parts):
    hi_count, lo_count, _ = sizes
    block = parts.shape[3:]
    anywhere = pl.BlockSpec(memory_space=pl.ANY)
    near = pl.BlockSpec(memory_space=pltpu.VMEM)
    return pl.pallas_call(
        functools.partial(closing_kernel, sizes),
        out_shape=(
            jax.ShapeDtypeStruct(out_rows.shape, out_rows.dtype),
            jax.ShapeDtypeStruct(grad_rows.shape, grad_rows.dtype),
            jax.ShapeDtypeStruct(block, jnp.float32),
        ),
        in_specs=[anywhere, anywhere, near],
        out_specs=(anywhere, anywhere, near),
        scratch_shapes=[
            pltpu.VMEM((hi_count, lo_count) + block, jnp.bfloat16),
            pltpu.VMEM((hi_count, lo_count) + block, jnp.bfloat16),
            pltpu.VMEM((hi_count,) + block, jnp.bfloat16),
            pltpu.VMEM((hi_count, lo_count) + block, jnp.bfloat16),
            pltpu.SemaphoreType.DMA((2,)),
            pltpu.SemaphoreType.DMA((2, 2)),
            pltpu.SemaphoreType.DMA((2, hi_count)),
            pltpu.SemaphoreType.DMA((2, hi_count, lo_count)),
            pltpu.SemaphoreType.DMA((2, hi_count, lo_count)),
        ],
        compiler_params=pltpu.CompilerParams(
            collective_id=1, has_side_effects=True, vmem_limit_bytes=60 << 20
        ),
        name="closing",
    )(out_rows, grad_rows, parts)


def dispatch_kernel(weighted, choose_ref, rows_ref, *refs):
    slots = jnp.dot(choose_ref[0, 0], rows_ref[...], preferred_element_type=jnp.float32)
    if weighted:
        slots = slots * refs[0][0, 0]
    refs[-1][0, 0] = slots.astype(jnp.bfloat16)


def dispatch(choose, rows, step, slots, weight):
    _, count, capacity, _ = choose.shape
    width = rows.shape[1]
    first = step * MB
    operands = [choose, rows]
    in_specs = [
        pl.BlockSpec((1, 1, capacity, TOK_MB), lambda b, e: (first + b, e, 0, 0)),
        pl.BlockSpec((TOK_MB, width), lambda b, e: (b, 0)),
    ]
    if weight is not None:
        operands.append(weight)
        in_specs.append(pl.BlockSpec((1, 1, capacity, 1), lambda b, e: (e, first + b, 0, 0)))
    aliases = {}
    if slots is not None:
        aliases = {len(operands): 0}
        operands.append(slots)
        in_specs.append(pl.BlockSpec(memory_space=pl.ANY))
    return pl.pallas_call(
        functools.partial(dispatch_kernel, weight is not None),
        grid=(MB, count),
        out_shape=jax.ShapeDtypeStruct((count, choose.shape[0], capacity, width), jnp.bfloat16),
        in_specs=in_specs,
        out_specs=pl.BlockSpec((1, 1, capacity, width), lambda b, e: (e, first + b, 0, 0)),
        input_output_aliases=aliases,
        name="dispatch",
    )(*operands)


def shards(
    tokens,
    cotangent,
    permutation,
    lengths,
    expert_ids,
    gate_weights,
    attn_gain,
    qkv_weight,
    out_weight,
    ffn_gain,
    expert_in,
    expert_out,
):
    device_count = lax.axis_size(ALL)
    hi_count = lax.axis_size("hi")
    lo_count = lax.axis_size("lo")
    tok_dev = permutation.shape[0]
    model_width = tokens.shape[1]
    peer_rows = tok_dev // device_count
    q_dim = HEADS * HEAD
    kv_dim = KV_HEADS * HEAD
    positions = jnp.arange(tok_dev, dtype=jnp.int32)
    expert_count = expert_in.shape[2] * device_count // FF_E
    capacity = TOK_MB * TOPK // expert_count
    source = permutation // tok_dev
    local_row = permutation % tok_dev
    from_source = (source[:, None] == jnp.arange(device_count, dtype=jnp.int32)[None, :]).astype(
        jnp.int32
    )
    earlier = jnp.cumsum(from_source, axis=0, dtype=jnp.int32) - from_source
    arrival = source * peer_rows + jnp.sum(earlier * from_source, axis=1, dtype=jnp.int32)
    arrival_match = arrival[:, None] == positions[None, :]
    wanted = jnp.sum(jnp.where(arrival_match, local_row[:, None], 0), axis=0, dtype=jnp.int32)
    by_arrival = jnp.sum(jnp.where(arrival_match, positions[:, None], 0), axis=0, dtype=jnp.int32)
    def swap(block, step):
        return lax.ppermute(block, "lo", [(i, i ^ step) for i in range(lo_count)])

    def spread(block):
        return [block] + [swap(block, step) for step in range(1, lo_count)]

    ids_all = jnp.stack(spread(expert_ids))
    gates_all = jnp.stack(spread(gate_weights))
    asked_rows = lax.all_to_all(
        wanted.reshape(device_count, peer_rows),
        ALL,
        split_axis=0,
        concat_axis=0,
        tiled=True,
    ).reshape(tok_dev)
    asked_rows, ids_all, gates_all = lax.optimization_barrier((asked_rows, ids_all, gates_all))
    asked_match = asked_rows[:, None] == positions[None, :]
    by_asked = jnp.sum(jnp.where(asked_match, positions[:, None], 0), axis=0, dtype=jnp.int32)
    sizes = (hi_count, lo_count, 2)
    shard_rows = qkv_weight.shape[0]
    qkv_cols = qkv_weight.shape[1]
    weight_shard = jnp.concatenate(
        [
            qkv_weight,
            out_weight,
            attn_gain[:, None],
            ffn_gain[:, None],
            jnp.zeros((shard_rows, 126), jnp.bfloat16),
        ],
        axis=1,
    )
    asked_tokens = jnp.take(tokens, asked_rows, axis=0).reshape(device_count, peer_rows, model_width)
    asked_grads = jnp.take(cotangent, asked_rows, axis=0).reshape(
        device_count, peer_rows, model_width
    )
    got_rows, got_grad, packed = opening(sizes, asked_tokens, asked_grads, weight_shard)
    packed = packed.reshape(model_width, -1)
    grad_bf = jnp.take(got_grad.reshape(tok_dev, model_width), arrival, axis=0)
    grad_blocks = spread(grad_bf)
    rows_in = jnp.take(got_rows.reshape(tok_dev, model_width), arrival, axis=0).astype(jnp.float32)
    qkv_full = packed[:, :qkv_cols]
    out_full = packed[:, qkv_cols : qkv_cols + model_width]
    gain_pair = packed[:, qkv_cols + model_width :].astype(jnp.float32)
    gain_one = gain_pair[:, 0]
    gain_two = gain_pair[:, 1]
    shard_cols = expert_in.shape[2]
    weights_in = lax.all_gather(
        expert_in.reshape(model_width, 2 * shard_cols), ("hi", "core"), axis=0
    ).reshape(hi_count, 2, model_width, 2 * shard_cols)
    weights_out = lax.all_gather(expert_out, ("hi", "core"), axis=0).reshape(
        hi_count, 2, shard_cols, model_width
    )
    segment, position = layout_rows(lengths)
    scale_one = lax.rsqrt(jnp.mean(rows_in * rows_in, axis=1, keepdims=True) + epsilon)
    normed = (rows_in * scale_one * gain_one).astype(jnp.bfloat16)
    projected = jnp.dot(normed, qkv_full, preferred_element_type=jnp.float32)
    cosine_table, sine_table = rope_tables(position)
    queries = rotate(
        projected[:, :q_dim].reshape(tok_dev, HEADS, HEAD), cosine_table, sine_table
    ).astype(jnp.bfloat16)
    key_rows = rotate(
        projected[:, q_dim : q_dim + kv_dim].reshape(tok_dev, KV_HEADS, HEAD),
        cosine_table,
        sine_table,
    ).astype(jnp.bfloat16)
    value_rows = (
        projected[:, q_dim + kv_dim :].reshape(tok_dev, KV_HEADS, HEAD).astype(jnp.bfloat16)
    )
    mixed_part, logsum = attend_block(queries, key_rows, value_rows, segment, position)
    mixed_rows = mixed_part.astype(jnp.bfloat16)
    attended = jnp.dot(mixed_rows, out_full, preferred_element_type=jnp.float32)
    residual = rows_in + attended
    scale_two = lax.rsqrt(jnp.mean(residual * residual, axis=1, keepdims=True) + epsilon)
    normed_two = (residual * scale_two * gain_two).astype(jnp.bfloat16)
    grad_output = grad_bf.astype(jnp.float32)
    home = lax.axis_index("lo")
    row_blocks = spread(normed_two)
    normed_two, *grad_blocks = lax.optimization_barrier((normed_two, *grad_blocks))
    choose, slot_gate = slot_tables(
        ids_all.reshape(-1, TOK_MB, TOPK),
        gates_all.reshape(-1, TOK_MB, TOPK),
        home + lo_count * jnp.arange(hi_count, dtype=jnp.int32),
        capacity,
    )
    slot_weight = jnp.transpose(slot_gate, (1, 0, 2))[..., None]
    grad_expert = None
    for step in range(lo_count):
        grad_expert = dispatch(choose, grad_blocks[step], step, grad_expert, slot_weight)
    grad_expert = grad_expert.reshape(hi_count, -1, model_width)
    grad_hidden = jnp.einsum(
        "erd,ekfd->ekrf", grad_expert, weights_out, preferred_element_type=jnp.float32
    ).astype(jnp.bfloat16)
    grad_hidden, *others = lax.optimization_barrier((grad_hidden, *row_blocks[1:]))
    row_blocks = [normed_two] + others
    expert_rows = None
    for step in range(lo_count):
        expert_rows = dispatch(choose, row_blocks[step], step, expert_rows, None)
    expert_rows = expert_rows.reshape(hi_count, -1, model_width)
    gate_up = jnp.einsum(
        "erd,ekdf->ekrf", expert_rows, weights_in, preferred_element_type=jnp.float32
    )
    gate_part = gate_up[..., :shard_cols]
    up_part = gate_up[..., shard_cols:]
    sigmoid_gate = jax.nn.sigmoid(gate_part)
    hidden = (gate_part * sigmoid_gate * up_part).astype(jnp.bfloat16)
    grad_gate = grad_hidden * up_part * sigmoid_gate * (1.0 + gate_part * (1.0 - sigmoid_gate))
    grad_up = grad_hidden * (gate_part * sigmoid_gate)
    grad_gate_up = jnp.concatenate([grad_gate, grad_up], axis=-1).astype(jnp.bfloat16)
    grad_expert_rows = jnp.einsum(
        "ekrf,ekdf->erd", grad_gate_up, weights_in, preferred_element_type=jnp.float32
    ).astype(jnp.bfloat16)

    def split_back(slot_values):
        return (
            jnp.einsum(
                "becr,ebcd->brd",
                choose,
                slot_values.reshape(hi_count, lo_count * MB, capacity, model_width),
                preferred_element_type=jnp.float32,
            )
            .astype(jnp.bfloat16)
            .reshape(lo_count, tok_dev, model_width)
        )

    def total_of(parts):
        total = parts[0].astype(jnp.float32)
        for part in parts[1:]:
            total = total + part.astype(jnp.float32)
        return total

    back = split_back(grad_expert_rows)
    back_parts = [back[0]] + [swap(back[step], step) for step in range(1, lo_count)]
    back, hidden, expert_rows, grad_gate_up, grad_expert = lax.optimization_barrier(
        (back, hidden, expert_rows, grad_gate_up, grad_expert)
    )
    grad_weights_out = jnp.einsum(
        "ekrf,erd->ekfd", hidden, grad_expert, preferred_element_type=jnp.float32
    ).astype(jnp.bfloat16)
    grad_weights_in = jnp.einsum(
        "ekrf,erd->ekfd", grad_gate_up, expert_rows, preferred_element_type=jnp.float32
    ).astype(jnp.bfloat16)
    produced = (
        jnp.einsum("ekrf,ekfd->erd", hidden, weights_out, preferred_element_type=jnp.float32)
        * slot_weight.reshape(hi_count, -1, 1)
    ).astype(jnp.bfloat16)
    ahead = split_back(produced)
    ahead, grad_weights_in, grad_weights_out, *back_parts = lax.optimization_barrier(
        (ahead, grad_weights_in, grad_weights_out, *back_parts)
    )
    ahead_parts = [ahead[0]] + [swap(ahead[step], step) for step in range(1, lo_count)]
    grad_normed_two = total_of(back_parts)
    shard_out = lax.psum_scatter(
        grad_weights_out.reshape(hi_count * 2 * shard_cols, model_width),
        ("hi", "core"),
        scatter_dimension=0,
        tiled=True,
    ).astype(jnp.float32)
    shard_in = lax.psum_scatter(
        grad_weights_in.reshape(hi_count * 2 * 2 * shard_cols, model_width),
        ("hi", "core"),
        scatter_dimension=0,
        tiled=True,
    )
    shard_in = shard_in.T.astype(jnp.float32).reshape(model_width, 2, shard_cols)
    grad_gain_two, grad_from_norm = norm_back(residual, scale_two, gain_two, grad_normed_two)
    grad_residual = grad_output + grad_from_norm
    grad_attended = grad_residual.astype(jnp.bfloat16)
    grad_out_weight = jnp.einsum(
        "nq,nd->qd", mixed_rows, grad_attended, preferred_element_type=jnp.float32
    )
    grad_mixed = jnp.einsum(
        "nd,qd->nq", grad_attended, out_full, preferred_element_type=jnp.float32
    ).astype(jnp.bfloat16)
    grad_queries, grad_keys, grad_values = attend_back(
        queries, key_rows, value_rows, segment, position, logsum, grad_mixed
    )
    grad_queries = rotate(grad_queries, cosine_table, -sine_table)
    grad_keys = rotate(grad_keys, cosine_table, -sine_table)
    grad_projected = jnp.concatenate(
        [
            grad_queries.reshape(tok_dev, q_dim),
            grad_keys.reshape(tok_dev, kv_dim),
            grad_values.reshape(tok_dev, kv_dim),
        ],
        axis=1,
    ).astype(jnp.bfloat16)
    grad_projected, *ahead_parts = lax.optimization_barrier((grad_projected, *ahead_parts))
    output_rows = (residual + total_of(ahead_parts)).astype(jnp.bfloat16)
    grad_qkv_weight = jnp.einsum(
        "nd,nc->dc", normed, grad_projected, preferred_element_type=jnp.float32
    )
    grad_normed = jnp.einsum(
        "nc,dc->nd", grad_projected, qkv_full, preferred_element_type=jnp.float32
    )
    grad_gain_one, grad_from_first = norm_back(rows_in, scale_one, gain_one, grad_normed)
    grad_input = (grad_residual + grad_from_first).astype(jnp.bfloat16)
    gains = jnp.pad(jnp.stack([grad_gain_one, grad_gain_two], axis=1), ((0, 0), (0, 126)))
    parts = jnp.concatenate(
        [
            grad_qkv_weight.astype(jnp.bfloat16),
            grad_out_weight.astype(jnp.bfloat16),
            gains.astype(jnp.bfloat16),
        ],
        axis=1,
    ).reshape(sizes + (shard_rows, -1))
    home_out, home_grad, sums = closing(
        sizes,
        jnp.take(output_rows, by_arrival, axis=0).reshape(device_count, peer_rows, model_width),
        jnp.take(grad_input, by_arrival, axis=0).reshape(device_count, peer_rows, model_width),
        parts,
    )
    shard_qkv = sums[:, :qkv_cols]
    shard_attn_out = sums[:, qkv_cols : qkv_cols + model_width]
    shard_gain_one = sums[:, qkv_cols + model_width]
    shard_gain_two = sums[:, qkv_cols + model_width + 1]
    output = jnp.take(home_out.reshape(tok_dev, model_width), by_asked, axis=0)
    input_grad = jnp.take(home_grad.reshape(tok_dev, model_width), by_asked, axis=0)
    return (
        output,
        input_grad,
        shard_gain_one,
        shard_qkv,
        shard_attn_out,
        shard_gain_two,
        shard_in,
        shard_out,
    )


def solution(mesh):
    dp_count = mesh.shape["dp"]
    hi_count = 4 if dp_count % 4 == 0 else 1
    split = jax.sharding.Mesh(
        mesh.devices.reshape(hi_count, dp_count // hi_count, mesh.shape["expert"]), ALL
    )
    rows, columns = P(ALL, None), P(None, None, ALL)
    return jax.shard_map(
        shards,
        mesh=split,
        in_specs=(rows, rows, P(ALL), rows, rows, rows, P(ALL), rows, rows, P(ALL), columns, rows),
        out_specs=(rows, rows, P(ALL), rows, rows, P(ALL), columns, rows),
        check_vma=False,
    )
```

```python
import functools

import jax
import jax.numpy as jnp
from jax import lax
from jax.experimental import pallas as pl
from jax.experimental.pallas import tpu as pltpu
from jax.sharding import PartitionSpec as P

HEADS = 24
KV_HEADS = 8
HEAD = 64
FF_E = 512
TOPK = 8
MB = 2
SEQS = 4
TOK_MB = 256
ALL = ("hi", "lo", "core")


epsilon = 1e-05
theta_base = 10000.0


def layout_rows(length_rows):
    seq_ends = jnp.cumsum(length_rows, axis=1, dtype=jnp.int32)
    starts = seq_ends - length_rows
    within = jnp.arange(TOK_MB, dtype=jnp.int32)
    segment = jnp.sum(
        (within[None, :, None] >= seq_ends[:, None, :]).astype(jnp.int32), axis=2, dtype=jnp.int32
    )
    chosen = segment[:, :, None] == jnp.arange(SEQS, dtype=jnp.int32)[None, None, :]
    seq_begin = jnp.sum(jnp.where(chosen, starts[:, None, :], 0), axis=2, dtype=jnp.int32)
    position = within[None, :] - seq_begin
    segment = segment + jnp.arange(MB, dtype=jnp.int32)[:, None] * SEQS
    return (segment.reshape(-1), position.reshape(-1))


def rope_tables(position):
    half_width = HEAD // 2
    frequency = theta_base ** (-(2.0 / HEAD) * jnp.arange(half_width, dtype=jnp.float32))
    angles = position.astype(jnp.float32)[:, None] * frequency[None, :]
    return (jnp.cos(angles), jnp.sin(angles))


def rotate(values, cosine_table, sine_table):
    half_width = HEAD // 2
    front_half = values[..., :half_width]
    behind = values[..., half_width:]
    cosine_part = cosine_table[:, None, :]
    sine_part = sine_table[:, None, :]
    return jnp.concatenate(
        [
            front_half * cosine_part - behind * sine_part,
            behind * cosine_part + front_half * sine_part,
        ],
        axis=-1,
    )


def slot_tables(ids, gates, experts, capacity):
    count = experts.shape[0]
    named = ids[..., None] == experts
    picked = jnp.any(named, axis=2)
    weight = jnp.sum(jnp.where(named, gates[..., None], 0.0), axis=2)
    rows = jnp.arange(TOK_MB, dtype=jnp.int32)
    below = (rows[:, None] > rows[None, :]).astype(jnp.bfloat16)
    shaped = picked.reshape(-1, TOK_MB, count)
    slot = jnp.einsum(
        "rq,bqe->ber", below, shaped.astype(jnp.bfloat16), preferred_element_type=jnp.float32
    ).astype(jnp.int32)
    kept = jnp.transpose(shaped, (0, 2, 1))
    hit = kept[:, :, None, :] & (
        slot[:, :, None, :] == jnp.arange(capacity, dtype=jnp.int32)[None, None, :, None]
    )
    weight = jnp.transpose(weight.reshape(-1, TOK_MB, count), (0, 2, 1))
    slot_gate = jnp.sum(jnp.where(hit, weight[:, :, None, :], 0.0), axis=3)
    return hit.astype(jnp.bfloat16), slot_gate


def by_batch(rows, heads):
    return rows.reshape(-1, TOK_MB, KV_HEADS, heads // KV_HEADS, HEAD)


def block_scores(queries, key_rows, segment, position):
    scores = jnp.einsum(
        "bqhgd,bkhd->bhgqk", queries, key_rows, preferred_element_type=jnp.float32
    ) * HEAD ** (-0.5)
    allowed = (segment[:, :, None] == segment[:, None, :]) & (
        position[:, :, None] >= position[:, None, :]
    )
    return jnp.where(allowed[:, None, None], scores, -1e30)


def attend_block(queries, key_rows, value_rows, segment, position):
    queries = by_batch(queries, HEADS)
    key_rows = by_batch(key_rows, KV_HEADS)[:, :, :, 0]
    value_rows = by_batch(value_rows, KV_HEADS)[:, :, :, 0]
    segment = segment.reshape(-1, TOK_MB)
    position = position.reshape(-1, TOK_MB)
    masked = block_scores(queries, key_rows, segment, position)
    row_peak = jnp.max(masked, axis=-1, keepdims=True)
    weights_exp = jnp.exp(masked - row_peak)
    row_total = jnp.sum(weights_exp, axis=-1, keepdims=True)
    probabilities = (weights_exp / row_total).astype(jnp.bfloat16)
    mixed_rows = jnp.einsum(
        "bhgqk,bkhd->bqhgd", probabilities, value_rows, preferred_element_type=jnp.float32
    )
    return (mixed_rows.reshape(-1, HEADS * HEAD), row_peak + jnp.log(row_total))


def attend_back(queries, key_rows, value_rows, segment, position, logsum, grad_mixed):
    queries = by_batch(queries, HEADS)
    key_rows = by_batch(key_rows, KV_HEADS)[:, :, :, 0]
    value_rows = by_batch(value_rows, KV_HEADS)[:, :, :, 0]
    segment = segment.reshape(-1, TOK_MB)
    position = position.reshape(-1, TOK_MB)
    masked = block_scores(queries, key_rows, segment, position)
    exact_probs = jnp.exp(masked - logsum)
    probabilities = exact_probs.astype(jnp.bfloat16)
    grad_heads = by_batch(grad_mixed, HEADS)
    grad_probs = jnp.einsum(
        "bqhgd,bkhd->bhgqk", grad_heads, value_rows, preferred_element_type=jnp.float32
    )
    grad_values = jnp.einsum(
        "bhgqk,bqhgd->bkhd", probabilities, grad_heads, preferred_element_type=jnp.float32
    )
    grad_scores = (
        exact_probs * (grad_probs - jnp.sum(grad_probs * exact_probs, axis=-1, keepdims=True))
    ).astype(jnp.bfloat16)
    grad_queries = jnp.einsum(
        "bhgqk,bkhd->bqhgd", grad_scores, key_rows, preferred_element_type=jnp.float32
    ) * HEAD ** (-0.5)
    grad_keys = jnp.einsum(
        "bhgqk,bqhgd->bkhd", grad_scores, queries, preferred_element_type=jnp.float32
    ) * HEAD ** (-0.5)
    return (
        grad_queries.reshape(-1, HEADS, HEAD),
        grad_keys.reshape(-1, KV_HEADS, HEAD),
        grad_values.reshape(-1, KV_HEADS, HEAD),
    )


def norm_back(values, scale, gain, grad_normed):
    scaled_grad = grad_normed * gain
    grad_gain = jnp.sum(grad_normed * values * scale, axis=0)
    grad_values = scale * scaled_grad - values * scale * scale * scale * jnp.mean(
        scaled_grad * values, axis=1, keepdims=True
    )
    return (grad_gain, grad_values)


MESH = pl.DeviceIdType.MESH


def flip(value, bits):
    bit = 1
    while bit <= bits:
        if bits & bit:
            value = value + bit * (1 - 2 * ((value // bit) % 2))
        bit *= 2
    return value


def place():
    return lax.axis_index("hi"), lax.axis_index("lo"), lax.axis_index("core")


def greet_all(sizes):
    hi_count, lo_count, _ = sizes
    count = hi_count * lo_count * 2
    hi, lo, core = place()
    me = (hi * lo_count + lo) * 2 + core
    barrier = pltpu.get_barrier_semaphore()

    def greet(step, carry):
        peer = (me + step) % count
        pl.semaphore_signal(
            barrier,
            inc=1,
            device_id=(peer // (2 * lo_count), (peer // 2) % lo_count, peer % 2),
            device_id_type=MESH,
        )
        return carry

    lax.fori_loop(1, count, greet, 0)
    pl.semaphore_wait(barrier, count - 1)


def send_rows(sizes, source, target, send_sem, recv_sem):
    hi_count, lo_count, _ = sizes
    count = hi_count * lo_count * 2
    hi, lo, core = place()
    me = (hi * lo_count + lo) * 2 + core

    def one(step, carry):
        peer = (me + step) % count
        pltpu.make_async_remote_copy(
            src_ref=source.at[peer],
            dst_ref=target.at[me],
            send_sem=send_sem,
            recv_sem=recv_sem,
            device_id=(peer // (2 * lo_count), (peer // 2) % lo_count, peer % 2),
            device_id_type=MESH,
        ).start()
        return carry

    lax.fori_loop(1, count, one, 0)


def wait_rows(source, target, send_sem, recv_sem):
    rest = pl.ds(0, source.shape[0] - 1)
    pltpu.make_async_copy(source.at[rest], source.at[rest], send_sem).wait()
    pltpu.make_async_copy(target.at[rest], target.at[rest], recv_sem).wait()


def lo_steps(lo_count, turn):
    bits = []
    bit = 1
    while bit < lo_count:
        bits.append(bit)
        bit *= 2
    if turn:
        bits = bits[::-1]
    held, steps = [0], []
    for bit in bits:
        steps.append((bit, list(held)))
        held = held + [offset ^ bit for offset in held]
    return steps


def opening_kernel(
    sizes, rows_ref, grads_ref, shard_ref, got_ref, got_grads_ref, full_ref,
    own_sem, row_sems, hi_sems, lo_sems, core_sems
):
    hi_count, lo_count, _ = sizes
    hi, lo, core = place()
    me = (hi * lo_count + lo) * 2 + core
    own = [
        pltpu.make_async_copy(shard_ref, full_ref.at[hi, lo, core], own_sem.at[0]),
        pltpu.make_async_copy(rows_ref.at[me], got_ref.at[me], own_sem.at[1]),
        pltpu.make_async_copy(grads_ref.at[me], got_grads_ref.at[me], own_sem.at[2]),
    ]
    for copy in own:
        copy.start()
    greet_all(sizes)

    def hop(source, at, device, sems, *index):
        return pltpu.make_async_remote_copy(
            src_ref=source,
            dst_ref=full_ref.at[at[0], at[1], at[2]],
            send_sem=sems.at[0, *index],
            recv_sem=sems.at[1, *index],
            device_id=device,
            device_id_type=MESH,
        )

    along_hi = {}
    for step in range(1, hi_count):
        along_hi[step] = hop(
            shard_ref, (hi, lo, core), (flip(hi, step), lo, core), hi_sems, step - 1
        )
        along_hi[step].start()
    send_rows(sizes, rows_ref, got_ref, row_sems.at[0, 0], row_sems.at[1, 0])
    send_rows(sizes, grads_ref, got_grads_ref, row_sems.at[0, 1], row_sems.at[1, 1])

    def across(plane, offset, first):
        at = (flip(hi, plane), flip(lo, offset), core)
        source = shard_ref if first else full_ref.at[at[0], at[1], at[2]]
        copy = hop(source, at, (hi, lo, 1 - core), core_sems, plane, offset)
        copy.start()
        return copy

    started, waits = [], []
    for plane in range(hi_count):
        if plane:
            along_hi[plane].wait_recv()
        started.append(across(plane, 0, plane == 0))
        number = 0
        for bit, offsets in lo_steps(lo_count, plane % 2):
            for offset in offsets:
                at = (flip(hi, plane), flip(lo, offset), core)
                source = shard_ref if plane == 0 and offset == 0 else full_ref.at[at[0], at[1], at[2]]
                copy = hop(source, at, (hi, flip(lo, bit), core), lo_sems, plane, number)
                number += 1
                if offset == 0:
                    copy.start()
                    started.append(copy)
                waits.append((copy, plane, offset, bit))
    arrived = {}
    for copy, plane, offset, bit in waits:
        if offset:
            copy.start()
            started.append(copy)
        copy.wait_recv()
        started.append(across(plane, offset ^ bit, False))
    for copy in started:
        copy.wait_send()
    for step in range(1, hi_count):
        along_hi[step].wait_send()
    for plane in range(hi_count):
        for offset in range(lo_count):
            at = (flip(hi, plane), flip(lo, offset), core)
            hop(
                full_ref.at[at[0], at[1], at[2]], at, (hi, lo, 1 - core), core_sems, plane, offset
            ).wait_recv()
    wait_rows(rows_ref, got_ref, row_sems.at[0, 0], row_sems.at[1, 0])
    wait_rows(grads_ref, got_grads_ref, row_sems.at[0, 1], row_sems.at[1, 1])
    for copy in own:
        copy.wait()


def opening(sizes, rows, grads, shard):
    hi_count, lo_count, _ = sizes
    anywhere = pl.BlockSpec(memory_space=pl.ANY)
    return pl.pallas_call(
        functools.partial(opening_kernel, sizes),
        out_shape=(
            jax.ShapeDtypeStruct(rows.shape, rows.dtype),
            jax.ShapeDtypeStruct(grads.shape, grads.dtype),
            jax.ShapeDtypeStruct(sizes + shard.shape, shard.dtype),
        ),
        in_specs=[anywhere] * 3,
        out_specs=(anywhere, anywhere, anywhere),
        scratch_shapes=[
            pltpu.SemaphoreType.DMA((3,)),
            pltpu.SemaphoreType.DMA((2, 2)),
            pltpu.SemaphoreType.DMA((2, hi_count)),
            pltpu.SemaphoreType.DMA((2, hi_count, lo_count)),
            pltpu.SemaphoreType.DMA((2, hi_count, lo_count)),
        ],
        compiler_params=pltpu.CompilerParams(collective_id=0, has_side_effects=True),
        name="opening",
    )(rows, grads, shard)


def add_blocks(target, first, second):
    rows = target.shape[0]
    tile = 16 if rows % 16 == 0 else rows

    def one(index, carry):
        at = pl.ds(index * tile, tile)
        target[at, :] = (
            first[at, :].astype(jnp.float32) + second[at, :].astype(jnp.float32)
        ).astype(target.dtype)
        return carry

    lax.fori_loop(0, rows // tile, one, 0)


def closing_kernel(
    sizes, out_ref, grad_ref, parts_ref, got_out, got_grad, sum_ref,
    from_core, from_lo, from_hi, held, own_sem, row_sems, hi_sems, lo_sems, core_sems
):
    hi_count, lo_count, _ = sizes
    hi, lo, core = place()
    me = (hi * lo_count + lo) * 2 + core
    own = [
        pltpu.make_async_copy(out_ref.at[me], got_out.at[me], own_sem.at[0]),
        pltpu.make_async_copy(grad_ref.at[me], got_grad.at[me], own_sem.at[1]),
    ]
    for copy in own:
        copy.start()
    greet_all(sizes)

    def hop(source, target, device, sems, *index):
        return pltpu.make_async_remote_copy(
            src_ref=source,
            dst_ref=target,
            send_sem=sems.at[0, *index],
            recv_sem=sems.at[1, *index],
            device_id=device,
            device_id_type=MESH,
        )

    planes = [plane for plane in range(1, hi_count)] + [0]
    across = {}
    for plane in planes:
        for offset in reversed(range(lo_count)):
            across[plane, offset] = hop(
                parts_ref.at[flip(hi, plane), flip(lo, offset), 1 - core],
                from_core.at[plane, offset],
                (hi, lo, 1 - core),
                core_sems,
                plane,
                offset,
            )
            across[plane, offset].start()
    send_rows(sizes, grad_ref, got_grad, row_sems.at[0, 0], row_sems.at[1, 0])
    send_rows(sizes, out_ref, got_out, row_sems.at[0, 1], row_sems.at[1, 1])
    started = []
    plans = {plane: lo_steps(lo_count, plane % 2)[::-1] for plane in planes}
    moves = {}
    for depth in range(len(plans[0])):
        for plane in planes:
            bit, kept = plans[plane][depth]
            base = lo_count - 2 * len(kept)
            if depth == 0:
                for offset in [keep ^ bit for keep in kept] + kept:
                    across[plane, offset].wait_recv()
                    add_blocks(
                        held.at[plane, offset],
                        parts_ref.at[flip(hi, plane), flip(lo, offset), core],
                        from_core.at[plane, offset],
                    )
            else:
                before = plans[plane][depth - 1]
                for number, offset in enumerate(before[1]):
                    copy, spot = moves[plane, depth - 1, offset]
                    copy.wait_recv()
                    add_blocks(held.at[plane, offset], held.at[plane, offset], from_lo.at[plane, spot])
            for number, offset in enumerate(kept):
                spot = base + number
                copy = hop(
                    held.at[plane, offset ^ bit],
                    from_lo.at[plane, spot],
                    (hi, flip(lo, bit), core),
                    lo_sems,
                    plane,
                    spot,
                )
                copy.start()
                started.append(copy)
                moves[plane, depth, offset] = (copy, spot)
    last = len(plans[0]) - 1
    along = {}
    for plane in planes:
        copy, spot = moves[plane, last, 0]
        copy.wait_recv()
        add_blocks(held.at[plane, 0], held.at[plane, 0], from_lo.at[plane, spot])
        if plane:
            along[plane] = hop(
                held.at[plane, 0],
                from_hi.at[plane],
                (flip(hi, plane), lo, core),
                hi_sems,
                plane,
            )
            along[plane].start()
            started.append(along[plane])
    for plane in range(1, hi_count):
        along[plane].wait_recv()
    rows = sum_ref.shape[0]
    tile = 16 if rows % 16 == 0 else rows

    def total(index, carry):
        at = pl.ds(index * tile, tile)
        value = held[0, 0, at, :].astype(jnp.float32)
        for plane in range(1, hi_count):
            value = value + from_hi[plane, at, :].astype(jnp.float32)
        sum_ref[at, :] = value
        return carry

    lax.fori_loop(0, rows // tile, total, 0)
    for copy in started:
        copy.wait_send()
    for copy in across.values():
        copy.wait_send()
    wait_rows(grad_ref, got_grad, row_sems.at[0, 0], row_sems.at[1, 0])
    wait_rows(out_ref, got_out, row_sems.at[0, 1], row_sems.at[1, 1])
    for copy in own:
        copy.wait()


def closing(sizes, out_rows, grad_rows, parts):
    hi_count, lo_count, _ = sizes
    block = parts.shape[3:]
    anywhere = pl.BlockSpec(memory_space=pl.ANY)
    near = pl.BlockSpec(memory_space=pltpu.VMEM)
    return pl.pallas_call(
        functools.partial(closing_kernel, sizes),
        out_shape=(
            jax.ShapeDtypeStruct(out_rows.shape, out_rows.dtype),
            jax.ShapeDtypeStruct(grad_rows.shape, grad_rows.dtype),
            jax.ShapeDtypeStruct(block, jnp.float32),
        ),
        in_specs=[anywhere, anywhere, near],
        out_specs=(anywhere, anywhere, near),
        scratch_shapes=[
            pltpu.VMEM((hi_count, lo_count) + block, jnp.bfloat16),
            pltpu.VMEM((hi_count, lo_count) + block, jnp.bfloat16),
            pltpu.VMEM((hi_count,) + block, jnp.bfloat16),
            pltpu.VMEM((hi_count, lo_count) + block, jnp.bfloat16),
            pltpu.SemaphoreType.DMA((2,)),
            pltpu.SemaphoreType.DMA((2, 2)),
            pltpu.SemaphoreType.DMA((2, hi_count)),
            pltpu.SemaphoreType.DMA((2, hi_count, lo_count)),
            pltpu.SemaphoreType.DMA((2, hi_count, lo_count)),
        ],
        compiler_params=pltpu.CompilerParams(
            collective_id=1, has_side_effects=True, vmem_limit_bytes=60 << 20
        ),
        name="closing",
    )(out_rows, grad_rows, parts)


def dispatch_kernel(weighted, choose_ref, rows_ref, *refs):
    count, capacity, rows = choose_ref.shape[1:]
    chosen = choose_ref[0].reshape(count * capacity, rows)
    width = rows_ref.shape[1]
    tile = 256 if width % 256 == 0 else width
    for start in range(0, width, tile):
        at = pl.ds(start, tile)
        slots = jnp.dot(chosen, rows_ref[:, at], preferred_element_type=jnp.float32)
        slots = slots.reshape(count, capacity, tile)
        if weighted:
            slots = slots * refs[0][:, 0]
        refs[-1][:, 0, :, at] = slots.astype(jnp.bfloat16)


def dispatch(choose, rows, step, slots, weight):
    _, count, capacity, _ = choose.shape
    width = rows.shape[1]
    first = step * MB
    operands = [choose, rows]
    in_specs = [
        pl.BlockSpec((1, count, capacity, TOK_MB), lambda b: (first + b, 0, 0, 0)),
        pl.BlockSpec((TOK_MB, width), lambda b: (b, 0)),
    ]
    if weight is not None:
        operands.append(weight)
        in_specs.append(pl.BlockSpec((count, 1, capacity, 1), lambda b: (0, first + b, 0, 0)))
    aliases = {}
    if slots is not None:
        aliases = {len(operands): 0}
        operands.append(slots)
        in_specs.append(pl.BlockSpec(memory_space=pl.ANY))
    return pl.pallas_call(
        functools.partial(dispatch_kernel, weight is not None),
        grid=(MB,),
        out_shape=jax.ShapeDtypeStruct((count, choose.shape[0], capacity, width), jnp.bfloat16),
        in_specs=in_specs,
        out_specs=pl.BlockSpec((count, 1, capacity, width), lambda b: (0, first + b, 0, 0)),
        input_output_aliases=aliases,
        name="dispatch",
    )(*operands)


def shards(
    tokens,
    cotangent,
    permutation,
    lengths,
    expert_ids,
    gate_weights,
    attn_gain,
    qkv_weight,
    out_weight,
    ffn_gain,
    expert_in,
    expert_out,
):
    device_count = lax.axis_size(ALL)
    hi_count = lax.axis_size("hi")
    lo_count = lax.axis_size("lo")
    tok_dev = permutation.shape[0]
    model_width = tokens.shape[1]
    peer_rows = tok_dev // device_count
    q_dim = HEADS * HEAD
    kv_dim = KV_HEADS * HEAD
    positions = jnp.arange(tok_dev, dtype=jnp.int32)
    expert_count = expert_in.shape[2] * device_count // FF_E
    capacity = TOK_MB * TOPK // expert_count
    source = permutation // tok_dev
    local_row = permutation % tok_dev
    from_source = (source[:, None] == jnp.arange(device_count, dtype=jnp.int32)[None, :]).astype(
        jnp.int32
    )
    earlier = jnp.cumsum(from_source, axis=0, dtype=jnp.int32) - from_source
    arrival = source * peer_rows + jnp.sum(earlier * from_source, axis=1, dtype=jnp.int32)
    arrival_match = arrival[:, None] == positions[None, :]
    wanted = jnp.sum(jnp.where(arrival_match, local_row[:, None], 0), axis=0, dtype=jnp.int32)
    by_arrival = jnp.sum(jnp.where(arrival_match, positions[:, None], 0), axis=0, dtype=jnp.int32)
    def swap(block, step):
        return lax.ppermute(block, "lo", [(i, i ^ step) for i in range(lo_count)])

    def spread(block):
        return [block] + [swap(block, step) for step in range(1, lo_count)]

    ids_all = jnp.stack(spread(expert_ids))
    gates_all = jnp.stack(spread(gate_weights))
    asked_rows = lax.all_to_all(
        wanted.reshape(device_count, peer_rows),
        ALL,
        split_axis=0,
        concat_axis=0,
        tiled=True,
    ).reshape(tok_dev)
    asked_rows, ids_all, gates_all = lax.optimization_barrier((asked_rows, ids_all, gates_all))
    asked_match = asked_rows[:, None] == positions[None, :]
    by_asked = jnp.sum(jnp.where(asked_match, positions[:, None], 0), axis=0, dtype=jnp.int32)
    sizes = (hi_count, lo_count, 2)
    shard_rows = qkv_weight.shape[0]
    qkv_cols = qkv_weight.shape[1]
    weight_shard = jnp.concatenate(
        [
            qkv_weight,
            out_weight,
            attn_gain[:, None],
            ffn_gain[:, None],
            jnp.zeros((shard_rows, 126), jnp.bfloat16),
        ],
        axis=1,
    )
    asked_tokens = jnp.take(tokens, asked_rows, axis=0).reshape(device_count, peer_rows, model_width)
    asked_grads = jnp.take(cotangent, asked_rows, axis=0).reshape(
        device_count, peer_rows, model_width
    )
    got_rows, got_grad, packed = opening(sizes, asked_tokens, asked_grads, weight_shard)
    got_rows, packed, expert_in = lax.optimization_barrier((got_rows, packed, expert_in))
    packed = packed.reshape(model_width, -1)
    grad_bf = jnp.take(got_grad.reshape(tok_dev, model_width), arrival, axis=0)
    grad_blocks = spread(grad_bf)
    rows_in = jnp.take(got_rows.reshape(tok_dev, model_width), arrival, axis=0).astype(jnp.float32)
    qkv_full = packed[:, :qkv_cols]
    out_full = packed[:, qkv_cols : qkv_cols + model_width]
    gain_pair = packed[:, qkv_cols + model_width :].astype(jnp.float32)
    gain_one = gain_pair[:, 0]
    gain_two = gain_pair[:, 1]
    shard_cols = expert_in.shape[2]
    weights_in = lax.all_gather(
        expert_in.reshape(model_width, 2 * shard_cols), ("hi", "core"), axis=0
    ).reshape(hi_count, 2, model_width, 2 * shard_cols)
    weights_out = lax.all_gather(expert_out, ("hi", "core"), axis=0).reshape(
        hi_count, 2, shard_cols, model_width
    )
    segment, position = layout_rows(lengths)
    scale_one = lax.rsqrt(jnp.mean(rows_in * rows_in, axis=1, keepdims=True) + epsilon)
    normed = (rows_in * scale_one * gain_one).astype(jnp.bfloat16)
    projected = jnp.dot(normed, qkv_full, preferred_element_type=jnp.float32)
    cosine_table, sine_table = rope_tables(position)
    queries = rotate(
        projected[:, :q_dim].reshape(tok_dev, HEADS, HEAD), cosine_table, sine_table
    ).astype(jnp.bfloat16)
    key_rows = rotate(
        projected[:, q_dim : q_dim + kv_dim].reshape(tok_dev, KV_HEADS, HEAD),
        cosine_table,
        sine_table,
    ).astype(jnp.bfloat16)
    value_rows = (
        projected[:, q_dim + kv_dim :].reshape(tok_dev, KV_HEADS, HEAD).astype(jnp.bfloat16)
    )
    mixed_part, logsum = attend_block(queries, key_rows, value_rows, segment, position)
    mixed_rows = mixed_part.astype(jnp.bfloat16)
    attended = jnp.dot(mixed_rows, out_full, preferred_element_type=jnp.float32)
    residual = rows_in + attended
    scale_two = lax.rsqrt(jnp.mean(residual * residual, axis=1, keepdims=True) + epsilon)
    normed_two = (residual * scale_two * gain_two).astype(jnp.bfloat16)
    grad_output = grad_bf.astype(jnp.float32)
    home = lax.axis_index("lo")
    row_blocks = spread(normed_two)
    normed_two, *grad_blocks = lax.optimization_barrier((normed_two, *grad_blocks))
    choose, slot_gate = slot_tables(
        ids_all.reshape(-1, TOK_MB, TOPK),
        gates_all.reshape(-1, TOK_MB, TOPK),
        home + lo_count * jnp.arange(hi_count, dtype=jnp.int32),
        capacity,
    )
    slot_weight = jnp.transpose(slot_gate, (1, 0, 2))[..., None]
    grad_expert = None
    for step in range(lo_count):
        grad_expert = dispatch(choose, grad_blocks[step], step, grad_expert, slot_weight)
    grad_expert = grad_expert.reshape(hi_count, -1, model_width)
    grad_hidden = jnp.einsum(
        "erd,ekfd->ekrf", grad_expert, weights_out, preferred_element_type=jnp.float32
    ).astype(jnp.bfloat16)
    grad_hidden, *others = lax.optimization_barrier((grad_hidden, *row_blocks[1:]))
    row_blocks = [normed_two] + others
    expert_rows = None
    for step in range(lo_count):
        expert_rows = dispatch(choose, row_blocks[step], step, expert_rows, None)
    expert_rows = expert_rows.reshape(hi_count, -1, model_width)
    gate_up = jnp.einsum(
        "erd,ekdf->ekrf", expert_rows, weights_in, preferred_element_type=jnp.float32
    )
    gate_part = gate_up[..., :shard_cols]
    up_part = gate_up[..., shard_cols:]
    sigmoid_gate = jax.nn.sigmoid(gate_part)
    hidden = (gate_part * sigmoid_gate * up_part).astype(jnp.bfloat16)
    grad_gate = grad_hidden * up_part * sigmoid_gate * (1.0 + gate_part * (1.0 - sigmoid_gate))
    grad_up = grad_hidden * (gate_part * sigmoid_gate)
    grad_gate_up = jnp.concatenate([grad_gate, grad_up], axis=-1).astype(jnp.bfloat16)
    grad_weights_out = jnp.einsum(
        "ekrf,erd->ekfd", hidden, grad_expert, preferred_element_type=jnp.float32
    ).astype(jnp.bfloat16)
    grad_weights_out, grad_gate_up = lax.optimization_barrier((grad_weights_out, grad_gate_up))
    shard_out = lax.psum_scatter(
        grad_weights_out.reshape(hi_count * 2 * shard_cols, model_width),
        ("hi", "core"),
        scatter_dimension=0,
        tiled=True,
    ).astype(jnp.float32)
    grad_expert_rows = jnp.einsum(
        "ekrf,ekdf->erd", grad_gate_up, weights_in, preferred_element_type=jnp.float32
    ).astype(jnp.bfloat16)

    def split_back(slot_values):
        return (
            jnp.einsum(
                "becr,ebcd->brd",
                choose,
                slot_values.reshape(hi_count, lo_count * MB, capacity, model_width),
                preferred_element_type=jnp.float32,
            )
            .astype(jnp.bfloat16)
            .reshape(lo_count, tok_dev, model_width)
        )

    def total_of(parts):
        total = parts[0].astype(jnp.float32)
        for part in parts[1:]:
            total = total + part.astype(jnp.float32)
        return total

    back = split_back(grad_expert_rows)
    back_parts = [back[0]] + [swap(back[step], step) for step in range(1, lo_count)]
    back, hidden, expert_rows, grad_gate_up = lax.optimization_barrier(
        (back, hidden, expert_rows, grad_gate_up)
    )
    grad_weights_in = jnp.einsum(
        "ekrf,erd->ekfd", grad_gate_up, expert_rows, preferred_element_type=jnp.float32
    ).astype(jnp.bfloat16)
    grad_weights_in, hidden = lax.optimization_barrier((grad_weights_in, hidden))
    shard_in = lax.psum_scatter(
        grad_weights_in.reshape(hi_count * 2 * 2 * shard_cols, model_width),
        ("hi", "core"),
        scatter_dimension=0,
        tiled=True,
    )
    shard_in = shard_in.T.astype(jnp.float32).reshape(model_width, 2, shard_cols)
    produced = (
        jnp.einsum("ekrf,ekfd->erd", hidden, weights_out, preferred_element_type=jnp.float32)
        * slot_weight.reshape(hi_count, -1, 1)
    ).astype(jnp.bfloat16)
    ahead = split_back(produced)
    ahead, *back_parts = lax.optimization_barrier((ahead, *back_parts))
    ahead_parts = [ahead[0]] + [swap(ahead[step], step) for step in range(1, lo_count)]
    grad_normed_two = total_of(back_parts)
    grad_gain_two, grad_from_norm = norm_back(residual, scale_two, gain_two, grad_normed_two)
    grad_residual = grad_output + grad_from_norm
    grad_attended = grad_residual.astype(jnp.bfloat16)
    grad_out_weight = jnp.einsum(
        "nq,nd->qd", mixed_rows, grad_attended, preferred_element_type=jnp.float32
    )
    grad_mixed = jnp.einsum(
        "nd,qd->nq", grad_attended, out_full, preferred_element_type=jnp.float32
    ).astype(jnp.bfloat16)
    grad_queries, grad_keys, grad_values = attend_back(
        queries, key_rows, value_rows, segment, position, logsum, grad_mixed
    )
    grad_queries = rotate(grad_queries, cosine_table, -sine_table)
    grad_keys = rotate(grad_keys, cosine_table, -sine_table)
    grad_projected = jnp.concatenate(
        [
            grad_queries.reshape(tok_dev, q_dim),
            grad_keys.reshape(tok_dev, kv_dim),
            grad_values.reshape(tok_dev, kv_dim),
        ],
        axis=1,
    ).astype(jnp.bfloat16)
    grad_projected, *ahead_parts = lax.optimization_barrier((grad_projected, *ahead_parts))
    output_rows = (residual + total_of(ahead_parts)).astype(jnp.bfloat16)
    grad_qkv_weight = jnp.einsum(
        "nd,nc->dc", normed, grad_projected, preferred_element_type=jnp.float32
    )
    grad_normed = jnp.einsum(
        "nc,dc->nd", grad_projected, qkv_full, preferred_element_type=jnp.float32
    )
    grad_gain_one, grad_from_first = norm_back(rows_in, scale_one, gain_one, grad_normed)
    grad_input = (grad_residual + grad_from_first).astype(jnp.bfloat16)
    gains = jnp.pad(jnp.stack([grad_gain_one, grad_gain_two], axis=1), ((0, 0), (0, 126)))
    parts = jnp.concatenate(
        [
            grad_qkv_weight.astype(jnp.bfloat16),
            grad_out_weight.astype(jnp.bfloat16),
            gains.astype(jnp.bfloat16),
        ],
        axis=1,
    ).reshape(sizes + (shard_rows, -1))
    home_out, home_grad, sums = closing(
        sizes,
        jnp.take(output_rows, by_arrival, axis=0).reshape(device_count, peer_rows, model_width),
        jnp.take(grad_input, by_arrival, axis=0).reshape(device_count, peer_rows, model_width),
        parts,
    )
    shard_qkv = sums[:, :qkv_cols]
    shard_attn_out = sums[:, qkv_cols : qkv_cols + model_width]
    shard_gain_one = sums[:, qkv_cols + model_width]
    shard_gain_two = sums[:, qkv_cols + model_width + 1]
    output = jnp.take(home_out.reshape(tok_dev, model_width), by_asked, axis=0)
    input_grad = jnp.take(home_grad.reshape(tok_dev, model_width), by_asked, axis=0)
    return (
        output,
        input_grad,
        shard_gain_one,
        shard_qkv,
        shard_attn_out,
        shard_gain_two,
        shard_in,
        shard_out,
    )


def solution(mesh):
    dp_count = mesh.shape["dp"]
    hi_count = 4 if dp_count % 4 == 0 else 1
    split = jax.sharding.Mesh(
        mesh.devices.reshape(hi_count, dp_count // hi_count, mesh.shape["expert"]), ALL
    )
    rows, columns = P(ALL, None), P(None, None, ALL)
    return jax.shard_map(
        shards,
        mesh=split,
        in_specs=(rows, rows, P(ALL), rows, rows, rows, P(ALL), rows, rows, P(ALL), columns, rows),
        out_specs=(rows, rows, P(ALL), rows, rows, P(ALL), columns, rows),
        check_vma=False,
    )
```

```python
import functools

import jax
import jax.numpy as jnp
from jax import lax
from jax.experimental import pallas as pl
from jax.experimental.pallas import tpu as pltpu
from jax.sharding import PartitionSpec as P

HEADS = 24
KV_HEADS = 8
HEAD = 64
FF_E = 512
TOPK = 8
MB = 2
SEQS = 4
TOK_MB = 256
ALL = ("hi", "lo", "core")


epsilon = 1e-05
theta_base = 10000.0


def layout_rows(length_rows):
    seq_ends = jnp.cumsum(length_rows, axis=1, dtype=jnp.int32)
    starts = seq_ends - length_rows
    within = jnp.arange(TOK_MB, dtype=jnp.int32)
    segment = jnp.sum(
        (within[None, :, None] >= seq_ends[:, None, :]).astype(jnp.int32), axis=2, dtype=jnp.int32
    )
    chosen = segment[:, :, None] == jnp.arange(SEQS, dtype=jnp.int32)[None, None, :]
    seq_begin = jnp.sum(jnp.where(chosen, starts[:, None, :], 0), axis=2, dtype=jnp.int32)
    position = within[None, :] - seq_begin
    segment = segment + jnp.arange(MB, dtype=jnp.int32)[:, None] * SEQS
    return (segment.reshape(-1), position.reshape(-1))


def rope_tables(position):
    half_width = HEAD // 2
    frequency = theta_base ** (-(2.0 / HEAD) * jnp.arange(half_width, dtype=jnp.float32))
    angles = position.astype(jnp.float32)[:, None] * frequency[None, :]
    return (jnp.cos(angles), jnp.sin(angles))


def rotate(values, cosine_table, sine_table):
    half_width = HEAD // 2
    front_half = values[..., :half_width]
    behind = values[..., half_width:]
    cosine_part = cosine_table[:, None, :]
    sine_part = sine_table[:, None, :]
    return jnp.concatenate(
        [
            front_half * cosine_part - behind * sine_part,
            behind * cosine_part + front_half * sine_part,
        ],
        axis=-1,
    )


def slot_tables(ids, gates, experts, capacity):
    count = experts.shape[0]
    named = ids[..., None] == experts
    picked = jnp.any(named, axis=2)
    weight = jnp.sum(jnp.where(named, gates[..., None], 0.0), axis=2)
    rows = jnp.arange(TOK_MB, dtype=jnp.int32)
    below = (rows[:, None] > rows[None, :]).astype(jnp.bfloat16)
    shaped = picked.reshape(-1, TOK_MB, count)
    slot = jnp.einsum(
        "rq,bqe->ber", below, shaped.astype(jnp.bfloat16), preferred_element_type=jnp.float32
    ).astype(jnp.int32)
    kept = jnp.transpose(shaped, (0, 2, 1))
    hit = kept[:, :, None, :] & (
        slot[:, :, None, :] == jnp.arange(capacity, dtype=jnp.int32)[None, None, :, None]
    )
    weight = jnp.transpose(weight.reshape(-1, TOK_MB, count), (0, 2, 1))
    slot_gate = jnp.sum(jnp.where(hit, weight[:, :, None, :], 0.0), axis=3)
    return hit.astype(jnp.bfloat16), slot_gate


def by_batch(rows, heads):
    return rows.reshape(-1, TOK_MB, KV_HEADS, heads // KV_HEADS, HEAD)


def block_scores(queries, key_rows, segment, position):
    scores = jnp.einsum(
        "bqhgd,bkhd->bhgqk", queries, key_rows, preferred_element_type=jnp.float32
    ) * HEAD ** (-0.5)
    allowed = (segment[:, :, None] == segment[:, None, :]) & (
        position[:, :, None] >= position[:, None, :]
    )
    return jnp.where(allowed[:, None, None], scores, -1e30)


def attend_block(queries, key_rows, value_rows, segment, position):
    queries = by_batch(queries, HEADS)
    key_rows = by_batch(key_rows, KV_HEADS)[:, :, :, 0]
    value_rows = by_batch(value_rows, KV_HEADS)[:, :, :, 0]
    segment = segment.reshape(-1, TOK_MB)
    position = position.reshape(-1, TOK_MB)
    masked = block_scores(queries, key_rows, segment, position)
    row_peak = jnp.max(masked, axis=-1, keepdims=True)
    weights_exp = jnp.exp(masked - row_peak)
    row_total = jnp.sum(weights_exp, axis=-1, keepdims=True)
    probabilities = (weights_exp / row_total).astype(jnp.bfloat16)
    mixed_rows = jnp.einsum(
        "bhgqk,bkhd->bqhgd", probabilities, value_rows, preferred_element_type=jnp.float32
    )
    return (mixed_rows.reshape(-1, HEADS * HEAD), row_peak + jnp.log(row_total))


def attend_back(queries, key_rows, value_rows, segment, position, logsum, grad_mixed):
    queries = by_batch(queries, HEADS)
    key_rows = by_batch(key_rows, KV_HEADS)[:, :, :, 0]
    value_rows = by_batch(value_rows, KV_HEADS)[:, :, :, 0]
    segment = segment.reshape(-1, TOK_MB)
    position = position.reshape(-1, TOK_MB)
    masked = block_scores(queries, key_rows, segment, position)
    exact_probs = jnp.exp(masked - logsum)
    probabilities = exact_probs.astype(jnp.bfloat16)
    grad_heads = by_batch(grad_mixed, HEADS)
    grad_probs = jnp.einsum(
        "bqhgd,bkhd->bhgqk", grad_heads, value_rows, preferred_element_type=jnp.float32
    )
    grad_values = jnp.einsum(
        "bhgqk,bqhgd->bkhd", probabilities, grad_heads, preferred_element_type=jnp.float32
    )
    grad_scores = (
        exact_probs * (grad_probs - jnp.sum(grad_probs * exact_probs, axis=-1, keepdims=True))
    ).astype(jnp.bfloat16)
    grad_queries = jnp.einsum(
        "bhgqk,bkhd->bqhgd", grad_scores, key_rows, preferred_element_type=jnp.float32
    ) * HEAD ** (-0.5)
    grad_keys = jnp.einsum(
        "bhgqk,bqhgd->bkhd", grad_scores, queries, preferred_element_type=jnp.float32
    ) * HEAD ** (-0.5)
    return (
        grad_queries.reshape(-1, HEADS, HEAD),
        grad_keys.reshape(-1, KV_HEADS, HEAD),
        grad_values.reshape(-1, KV_HEADS, HEAD),
    )


def pick(rows, index):
    return jnp.take(rows, index, axis=0, mode="clip")


def hold(value, *after):
    anywhere = pl.BlockSpec(memory_space=pl.ANY)
    return pl.pallas_call(
        lambda *refs: None,
        out_shape=jax.ShapeDtypeStruct(value.shape, value.dtype),
        in_specs=[anywhere] * (1 + len(after)),
        out_specs=anywhere,
        input_output_aliases={0: 0},
        name="hold",
    )(value, *after)


def norm_back(values, scale, gain, grad_normed):
    scaled_grad = grad_normed * gain
    grad_gain = jnp.sum(grad_normed * values * scale, axis=0)
    grad_values = scale * scaled_grad - values * scale * scale * scale * jnp.mean(
        scaled_grad * values, axis=1, keepdims=True
    )
    return (grad_gain, grad_values)


MESH = pl.DeviceIdType.MESH


def flip(value, bits):
    bit = 1
    while bit <= bits:
        if bits & bit:
            value = value + bit * (1 - 2 * ((value // bit) % 2))
        bit *= 2
    return value


def place():
    return lax.axis_index("hi"), lax.axis_index("lo"), lax.axis_index("core")


def greet_all(sizes):
    hi_count, lo_count, _ = sizes
    count = hi_count * lo_count * 2
    hi, lo, core = place()
    me = (hi * lo_count + lo) * 2 + core
    barrier = pltpu.get_barrier_semaphore()

    def greet(step, carry):
        peer = (me + step) % count
        pl.semaphore_signal(
            barrier,
            inc=1,
            device_id=(peer // (2 * lo_count), (peer // 2) % lo_count, peer % 2),
            device_id_type=MESH,
        )
        return carry

    lax.fori_loop(1, count, greet, 0)
    pl.semaphore_wait(barrier, count - 1)


def send_rows(sizes, source, target, send_sem, recv_sem):
    hi_count, lo_count, _ = sizes
    count = hi_count * lo_count * 2
    hi, lo, core = place()
    me = (hi * lo_count + lo) * 2 + core

    def one(step, carry):
        peer = (me + step) % count
        pltpu.make_async_remote_copy(
            src_ref=source.at[peer],
            dst_ref=target.at[me],
            send_sem=send_sem,
            recv_sem=recv_sem,
            device_id=(peer // (2 * lo_count), (peer // 2) % lo_count, peer % 2),
            device_id_type=MESH,
        ).start()
        return carry

    lax.fori_loop(1, count, one, 0)


def wait_rows(source, target, send_sem, recv_sem):
    rest = pl.ds(0, source.shape[0] - 1)
    pltpu.make_async_copy(source.at[rest], source.at[rest], send_sem).wait()
    pltpu.make_async_copy(target.at[rest], target.at[rest], recv_sem).wait()


def lo_steps(lo_count, turn):
    bits = []
    bit = 1
    while bit < lo_count:
        bits.append(bit)
        bit *= 2
    if turn:
        bits = bits[::-1]
    held, steps = [0], []
    for bit in bits:
        steps.append((bit, list(held)))
        held = held + [offset ^ bit for offset in held]
    return steps


def opening_kernel(
    sizes, rows_ref, grads_ref, shard_ref, got_ref, got_grads_ref, full_ref,
    own_sem, row_sems, hi_sems, lo_sems, core_sems
):
    hi_count, lo_count, _ = sizes
    hi, lo, core = place()
    me = (hi * lo_count + lo) * 2 + core
    own = [
        pltpu.make_async_copy(shard_ref, full_ref.at[hi, lo, core], own_sem.at[0]),
        pltpu.make_async_copy(rows_ref.at[me], got_ref.at[me], own_sem.at[1]),
        pltpu.make_async_copy(grads_ref.at[me], got_grads_ref.at[me], own_sem.at[2]),
    ]
    for copy in own:
        copy.start()
    greet_all(sizes)

    def hop(source, at, device, sems, *index):
        return pltpu.make_async_remote_copy(
            src_ref=source,
            dst_ref=full_ref.at[at[0], at[1], at[2]],
            send_sem=sems.at[0, *index],
            recv_sem=sems.at[1, *index],
            device_id=device,
            device_id_type=MESH,
        )

    along_hi = {}
    for step in range(1, hi_count):
        along_hi[step] = hop(
            shard_ref, (hi, lo, core), (flip(hi, step), lo, core), hi_sems, step - 1
        )
        along_hi[step].start()
    send_rows(sizes, rows_ref, got_ref, row_sems.at[0, 0], row_sems.at[1, 0])
    send_rows(sizes, grads_ref, got_grads_ref, row_sems.at[0, 1], row_sems.at[1, 1])

    def across(plane, offset, first):
        at = (flip(hi, plane), flip(lo, offset), core)
        source = shard_ref if first else full_ref.at[at[0], at[1], at[2]]
        copy = hop(source, at, (hi, lo, 1 - core), core_sems, plane, offset)
        copy.start()
        return copy

    started, waits = [], []
    for plane in range(hi_count):
        if plane:
            along_hi[plane].wait_recv()
        started.append(across(plane, 0, plane == 0))
        number = 0
        for bit, offsets in lo_steps(lo_count, plane % 2):
            for offset in offsets:
                at = (flip(hi, plane), flip(lo, offset), core)
                source = shard_ref if plane == 0 and offset == 0 else full_ref.at[at[0], at[1], at[2]]
                copy = hop(source, at, (hi, flip(lo, bit), core), lo_sems, plane, number)
                number += 1
                if offset == 0:
                    copy.start()
                    started.append(copy)
                waits.append((copy, plane, offset, bit))
    arrived = {}
    for copy, plane, offset, bit in waits:
        if offset:
            copy.start()
            started.append(copy)
        copy.wait_recv()
        started.append(across(plane, offset ^ bit, False))
    for copy in started:
        copy.wait_send()
    for step in range(1, hi_count):
        along_hi[step].wait_send()
    for plane in range(hi_count):
        for offset in range(lo_count):
            at = (flip(hi, plane), flip(lo, offset), core)
            hop(
                full_ref.at[at[0], at[1], at[2]], at, (hi, lo, 1 - core), core_sems, plane, offset
            ).wait_recv()
    wait_rows(rows_ref, got_ref, row_sems.at[0, 0], row_sems.at[1, 0])
    wait_rows(grads_ref, got_grads_ref, row_sems.at[0, 1], row_sems.at[1, 1])
    for copy in own:
        copy.wait()


def opening(sizes, rows, grads, shard):
    hi_count, lo_count, _ = sizes
    anywhere = pl.BlockSpec(memory_space=pl.ANY)
    return pl.pallas_call(
        functools.partial(opening_kernel, sizes),
        out_shape=(
            jax.ShapeDtypeStruct(rows.shape, rows.dtype),
            jax.ShapeDtypeStruct(grads.shape, grads.dtype),
            jax.ShapeDtypeStruct(sizes + shard.shape, shard.dtype),
        ),
        in_specs=[anywhere] * 3,
        out_specs=(anywhere, anywhere, anywhere),
        scratch_shapes=[
            pltpu.SemaphoreType.DMA((3,)),
            pltpu.SemaphoreType.DMA((2, 2)),
            pltpu.SemaphoreType.DMA((2, hi_count)),
            pltpu.SemaphoreType.DMA((2, hi_count, lo_count)),
            pltpu.SemaphoreType.DMA((2, hi_count, lo_count)),
        ],
        compiler_params=pltpu.CompilerParams(collective_id=0, has_side_effects=True),
        name="opening",
    )(rows, grads, shard)


def add_blocks(target, first, second):
    rows = target.shape[0]
    tile = 16 if rows % 16 == 0 else rows

    def one(index, carry):
        at = pl.ds(index * tile, tile)
        target[at, :] = (
            first[at, :].astype(jnp.float32) + second[at, :].astype(jnp.float32)
        ).astype(target.dtype)
        return carry

    lax.fori_loop(0, rows // tile, one, 0)


def closing_kernel(
    sizes, out_ref, grad_ref, parts_ref, got_out, got_grad, sum_ref,
    from_core, from_lo, from_hi, held, own_sem, row_sems, hi_sems, lo_sems, core_sems
):
    hi_count, lo_count, _ = sizes
    hi, lo, core = place()
    me = (hi * lo_count + lo) * 2 + core
    own = [
        pltpu.make_async_copy(out_ref.at[me], got_out.at[me], own_sem.at[0]),
        pltpu.make_async_copy(grad_ref.at[me], got_grad.at[me], own_sem.at[1]),
    ]
    for copy in own:
        copy.start()
    greet_all(sizes)

    def hop(source, target, device, sems, *index):
        return pltpu.make_async_remote_copy(
            src_ref=source,
            dst_ref=target,
            send_sem=sems.at[0, *index],
            recv_sem=sems.at[1, *index],
            device_id=device,
            device_id_type=MESH,
        )

    planes = [plane for plane in range(1, hi_count)] + [0]
    across = {}
    for plane in planes:
        for offset in reversed(range(lo_count)):
            across[plane, offset] = hop(
                parts_ref.at[flip(hi, plane), flip(lo, offset), 1 - core],
                from_core.at[plane, offset],
                (hi, lo, 1 - core),
                core_sems,
                plane,
                offset,
            )
            across[plane, offset].start()
    send_rows(sizes, grad_ref, got_grad, row_sems.at[0, 0], row_sems.at[1, 0])
    send_rows(sizes, out_ref, got_out, row_sems.at[0, 1], row_sems.at[1, 1])
    started = []
    plans = {plane: lo_steps(lo_count, plane % 2)[::-1] for plane in planes}
    moves = {}
    for depth in range(len(plans[0])):
        for plane in planes:
            bit, kept = plans[plane][depth]
            base = lo_count - 2 * len(kept)
            if depth == 0:
                for offset in [keep ^ bit for keep in kept] + kept:
                    across[plane, offset].wait_recv()
                    add_blocks(
                        held.at[plane, offset],
                        parts_ref.at[flip(hi, plane), flip(lo, offset), core],
                        from_core.at[plane, offset],
                    )
            else:
                before = plans[plane][depth - 1]
                for number, offset in enumerate(before[1]):
                    copy, spot = moves[plane, depth - 1, offset]
                    copy.wait_recv()
                    add_blocks(held.at[plane, offset], held.at[plane, offset], from_lo.at[plane, spot])
            for number, offset in enumerate(kept):
                spot = base + number
                copy = hop(
                    held.at[plane, offset ^ bit],
                    from_lo.at[plane, spot],
                    (hi, flip(lo, bit), core),
                    lo_sems,
                    plane,
                    spot,
                )
                copy.start()
                started.append(copy)
                moves[plane, depth, offset] = (copy, spot)
    last = len(plans[0]) - 1
    along = {}
    for plane in planes:
        copy, spot = moves[plane, last, 0]
        copy.wait_recv()
        add_blocks(held.at[plane, 0], held.at[plane, 0], from_lo.at[plane, spot])
        if plane:
            along[plane] = hop(
                held.at[plane, 0],
                from_hi.at[plane],
                (flip(hi, plane), lo, core),
                hi_sems,
                plane,
            )
            along[plane].start()
            started.append(along[plane])
    for plane in range(1, hi_count):
        along[plane].wait_recv()
    rows = sum_ref.shape[0]
    tile = 16 if rows % 16 == 0 else rows

    def total(index, carry):
        at = pl.ds(index * tile, tile)
        value = held[0, 0, at, :].astype(jnp.float32)
        for plane in range(1, hi_count):
            value = value + from_hi[plane, at, :].astype(jnp.float32)
        sum_ref[at, :] = value
        return carry

    lax.fori_loop(0, rows // tile, total, 0)
    for copy in started:
        copy.wait_send()
    for copy in across.values():
        copy.wait_send()
    wait_rows(grad_ref, got_grad, row_sems.at[0, 0], row_sems.at[1, 0])
    wait_rows(out_ref, got_out, row_sems.at[0, 1], row_sems.at[1, 1])
    for copy in own:
        copy.wait()


def closing(sizes, out_rows, grad_rows, parts):
    hi_count, lo_count, _ = sizes
    block = parts.shape[3:]
    anywhere = pl.BlockSpec(memory_space=pl.ANY)
    near = pl.BlockSpec(memory_space=pltpu.VMEM)
    return pl.pallas_call(
        functools.partial(closing_kernel, sizes),
        out_shape=(
            jax.ShapeDtypeStruct(out_rows.shape, out_rows.dtype),
            jax.ShapeDtypeStruct(grad_rows.shape, grad_rows.dtype),
            jax.ShapeDtypeStruct(block, jnp.float32),
        ),
        in_specs=[anywhere, anywhere, near],
        out_specs=(anywhere, anywhere, near),
        scratch_shapes=[
            pltpu.VMEM((hi_count, lo_count) + block, jnp.bfloat16),
            pltpu.VMEM((hi_count, lo_count) + block, jnp.bfloat16),
            pltpu.VMEM((hi_count,) + block, jnp.bfloat16),
            pltpu.VMEM((hi_count, lo_count) + block, jnp.bfloat16),
            pltpu.SemaphoreType.DMA((2,)),
            pltpu.SemaphoreType.DMA((2, 2)),
            pltpu.SemaphoreType.DMA((2, hi_count)),
            pltpu.SemaphoreType.DMA((2, hi_count, lo_count)),
            pltpu.SemaphoreType.DMA((2, hi_count, lo_count)),
        ],
        compiler_params=pltpu.CompilerParams(
            collective_id=1, has_side_effects=True, vmem_limit_bytes=60 << 20
        ),
        name="closing",
    )(out_rows, grad_rows, parts)


def dispatch_kernel(weighted, choose_ref, rows_ref, *refs):
    count, capacity, rows = choose_ref.shape[1:]
    chosen = choose_ref[0].reshape(count * capacity, rows)
    width = rows_ref.shape[1]
    tile = 256 if width % 256 == 0 else width
    for start in range(0, width, tile):
        at = pl.ds(start, tile)
        slots = jnp.dot(chosen, rows_ref[:, at], preferred_element_type=jnp.float32)
        slots = slots.reshape(count, capacity, tile)
        if weighted:
            slots = slots * refs[0][:, 0]
        refs[-1][:, 0, :, at] = slots.astype(jnp.bfloat16)


def dispatch(choose, rows, first, stride, slots, weight):
    _, count, capacity, _ = choose.shape
    width = rows.shape[1]
    operands = [choose, rows]
    in_specs = [
        pl.BlockSpec((1, count, capacity, TOK_MB), lambda b: (first + b * stride, 0, 0, 0)),
        pl.BlockSpec((TOK_MB, width), lambda b: (b, 0)),
    ]
    if weight is not None:
        operands.append(weight)
        in_specs.append(pl.BlockSpec((count, 1, capacity, 1), lambda b: (0, first + b * stride, 0, 0)))
    aliases = {}
    if slots is not None:
        aliases = {len(operands): 0}
        operands.append(slots)
        in_specs.append(pl.BlockSpec(memory_space=pl.ANY))
    return pl.pallas_call(
        functools.partial(dispatch_kernel, weight is not None),
        grid=(rows.shape[0] // TOK_MB,),
        out_shape=jax.ShapeDtypeStruct((count, choose.shape[0], capacity, width), jnp.bfloat16),
        in_specs=in_specs,
        out_specs=pl.BlockSpec((count, 1, capacity, width), lambda b: (0, first + b * stride, 0, 0)),
        input_output_aliases=aliases,
        name="dispatch",
    )(*operands)


def shards(
    tokens,
    cotangent,
    permutation,
    lengths,
    expert_ids,
    gate_weights,
    attn_gain,
    qkv_weight,
    out_weight,
    ffn_gain,
    expert_in,
    expert_out,
):
    device_count = lax.axis_size(ALL)
    hi_count = lax.axis_size("hi")
    lo_count = lax.axis_size("lo")
    tok_dev = permutation.shape[0]
    model_width = tokens.shape[1]
    peer_rows = tok_dev // device_count
    q_dim = HEADS * HEAD
    kv_dim = KV_HEADS * HEAD
    positions = jnp.arange(tok_dev, dtype=jnp.int32)
    expert_count = expert_in.shape[2] * device_count // FF_E
    capacity = TOK_MB * TOPK // expert_count
    source = permutation // tok_dev
    local_row = permutation % tok_dev
    from_source = (source[:, None] == jnp.arange(device_count, dtype=jnp.int32)[None, :]).astype(
        jnp.int32
    )
    earlier = jnp.cumsum(from_source, axis=0, dtype=jnp.int32) - from_source
    arrival = source * peer_rows + jnp.sum(earlier * from_source, axis=1, dtype=jnp.int32)
    arrival_match = arrival[:, None] == positions[None, :]
    wanted = jnp.sum(jnp.where(arrival_match, local_row[:, None], 0), axis=0, dtype=jnp.int32)
    by_arrival = jnp.sum(jnp.where(arrival_match, positions[:, None], 0), axis=0, dtype=jnp.int32)
    def swap(block, step):
        return lax.ppermute(block, "lo", [(i, i ^ step) for i in range(lo_count)])

    def spread(block):
        if lo_count != 4:
            return [[block]] + [[swap(block, step)] for step in range(1, lo_count)]
        half = block.shape[0] // 2
        one, two = swap(block, 1), swap(block, 2)
        return [[block], [one], [two], [swap(one[:half], 2), swap(two[half:], 1)]]

    if lo_count == 4:
        order = [(0, 0), (0, 1), (1, 0), (3, 0), (2, 1), (3, 1), (1, 1), (2, 0)]
    else:
        order = [(step, batch) for step in range(lo_count) for batch in range(MB)]
    routing = jnp.concatenate([expert_ids.astype(jnp.float32), gate_weights], axis=1)
    routing_all = [routing] + [swap(routing, step) for step in range(1, lo_count)]
    routing_all = jnp.stack(
        [routing_all[step][batch * TOK_MB : (batch + 1) * TOK_MB] for step, batch in order]
    )
    asked_rows = lax.all_to_all(
        wanted.reshape(device_count, peer_rows),
        ALL,
        split_axis=0,
        concat_axis=0,
        tiled=True,
    ).reshape(tok_dev)
    asked_rows, routing_all = lax.optimization_barrier((asked_rows, routing_all))
    asked_match = asked_rows[:, None] == positions[None, :]
    by_asked = jnp.sum(jnp.where(asked_match, positions[:, None], 0), axis=0, dtype=jnp.int32)
    sizes = (hi_count, lo_count, 2)
    shard_rows = qkv_weight.shape[0]
    qkv_cols = qkv_weight.shape[1]
    weight_shard = jnp.concatenate(
        [
            qkv_weight,
            out_weight,
            attn_gain[:, None],
            ffn_gain[:, None],
            jnp.zeros((shard_rows, 126), jnp.bfloat16),
        ],
        axis=1,
    )
    asked_tokens = pick(tokens, asked_rows).reshape(device_count, peer_rows, model_width)
    asked_grads = pick(cotangent, asked_rows).reshape(
        device_count, peer_rows, model_width
    )
    got_rows, got_grad, packed = opening(sizes, asked_tokens, asked_grads, weight_shard)
    got_rows, packed, expert_in = lax.optimization_barrier((got_rows, packed, expert_in))
    packed = packed.reshape(model_width, -1)
    grad_bf = pick(got_grad.reshape(tok_dev, model_width), arrival)
    got_rows = hold(got_rows, grad_bf)
    grad_blocks = spread(grad_bf)
    rows_in = pick(got_rows.reshape(tok_dev, model_width), arrival).astype(jnp.float32)
    qkv_full = packed[:, :qkv_cols]
    out_full = packed[:, qkv_cols : qkv_cols + model_width]
    gain_pair = packed[:, qkv_cols + model_width :].astype(jnp.float32)
    gain_one = gain_pair[:, 0]
    gain_two = gain_pair[:, 1]
    shard_cols = expert_in.shape[2]
    weights_in = lax.all_gather(
        expert_in.reshape(model_width, 2 * shard_cols), ("hi", "core"), axis=0
    ).reshape(hi_count, 2, model_width, 2 * shard_cols)
    weights_out = lax.all_gather(expert_out, ("hi", "core"), axis=0).reshape(
        hi_count, 2, shard_cols, model_width
    )
    segment, position = layout_rows(lengths)
    scale_one = lax.rsqrt(jnp.mean(rows_in * rows_in, axis=1, keepdims=True) + epsilon)
    normed = (rows_in * scale_one * gain_one).astype(jnp.bfloat16)
    projected = jnp.dot(normed, qkv_full, preferred_element_type=jnp.float32)
    cosine_table, sine_table = rope_tables(position)
    queries = rotate(
        projected[:, :q_dim].reshape(tok_dev, HEADS, HEAD), cosine_table, sine_table
    ).astype(jnp.bfloat16)
    key_rows = rotate(
        projected[:, q_dim : q_dim + kv_dim].reshape(tok_dev, KV_HEADS, HEAD),
        cosine_table,
        sine_table,
    ).astype(jnp.bfloat16)
    value_rows = (
        projected[:, q_dim + kv_dim :].reshape(tok_dev, KV_HEADS, HEAD).astype(jnp.bfloat16)
    )
    mixed_part, logsum = attend_block(queries, key_rows, value_rows, segment, position)
    mixed_rows = mixed_part.astype(jnp.bfloat16)
    if lo_count == 4:
        mixed_rows = hold(mixed_rows, grad_blocks[1][0], grad_blocks[2][0])
    attended = jnp.dot(mixed_rows, out_full, preferred_element_type=jnp.float32)
    residual = rows_in + attended
    scale_two = lax.rsqrt(jnp.mean(residual * residual, axis=1, keepdims=True) + epsilon)
    normed_two = (residual * scale_two * gain_two).astype(jnp.bfloat16)
    grad_output = grad_bf.astype(jnp.float32)
    home = lax.axis_index("lo")
    row_blocks = spread(normed_two)
    normed_two, grad_blocks = lax.optimization_barrier((normed_two, grad_blocks))
    choose, slot_gate = slot_tables(
        routing_all[..., :TOPK].astype(jnp.int32),
        routing_all[..., TOPK:],
        home + lo_count * jnp.arange(hi_count, dtype=jnp.int32),
        capacity,
    )
    slot_weight = jnp.transpose(slot_gate, (1, 0, 2))[..., None]
    place_of = {name: number for number, name in enumerate(order)}

    def fill(blocks, slots, weight):
        for step, pieces in blocks:
            batch = 0
            for piece in pieces:
                first = place_of[step, batch]
                stride = place_of[step, MB - 1] - place_of[step, 0]
                slots = dispatch(choose, piece, first, stride, slots, weight)
                batch += piece.shape[0] // TOK_MB
        return slots

    grad_expert = fill(list(enumerate(grad_blocks)), None, slot_weight)
    grad_expert = grad_expert.reshape(hi_count, -1, model_width)
    grad_hidden = jnp.einsum(
        "erd,ekfd->ekrf", grad_expert, weights_out, preferred_element_type=jnp.float32
    ).astype(jnp.bfloat16)
    expert_rows = fill([(0, [normed_two])], None, None)
    grad_hidden, expert_rows, others = lax.optimization_barrier(
        (grad_hidden, expert_rows, row_blocks[1:])
    )
    expert_rows = fill(list(enumerate(others, 1)), expert_rows, None)
    expert_rows = expert_rows.reshape(hi_count, -1, model_width)
    gate_up = jnp.einsum(
        "erd,ekdf->ekrf", expert_rows, weights_in, preferred_element_type=jnp.float32
    )
    gate_part = gate_up[..., :shard_cols]
    up_part = gate_up[..., shard_cols:]
    sigmoid_gate = jax.nn.sigmoid(gate_part)
    hidden = (gate_part * sigmoid_gate * up_part).astype(jnp.bfloat16)
    grad_gate = grad_hidden * up_part * sigmoid_gate * (1.0 + gate_part * (1.0 - sigmoid_gate))
    grad_up = grad_hidden * (gate_part * sigmoid_gate)
    grad_gate_up = jnp.concatenate([grad_gate, grad_up], axis=-1).astype(jnp.bfloat16)
    grad_weights_out = jnp.einsum(
        "ekrf,erd->ekfd", hidden, grad_expert, preferred_element_type=jnp.float32
    ).astype(jnp.bfloat16)
    grad_weights_out, grad_gate_up = lax.optimization_barrier((grad_weights_out, grad_gate_up))
    shard_out = lax.psum_scatter(
        grad_weights_out.reshape(hi_count * 2 * shard_cols, model_width),
        ("hi", "core"),
        scatter_dimension=0,
        tiled=True,
    ).astype(jnp.float32)
    grad_expert_rows = jnp.einsum(
        "ekrf,ekdf->erd", grad_gate_up, weights_in, preferred_element_type=jnp.float32
    ).astype(jnp.bfloat16)

    def split_back(slot_values):
        return jnp.einsum(
            "becr,ebcd->brd",
            choose,
            slot_values.reshape(hi_count, lo_count * MB, capacity, model_width),
            preferred_element_type=jnp.float32,
        ).astype(jnp.bfloat16)

    def wide(value):
        return value.astype(jnp.float32)

    def bring_back(parts):
        if lo_count != 4:
            parts = parts.reshape(lo_count, tok_dev, model_width)
            return [parts[0]] + [swap(parts[step], step) for step in range(1, lo_count)]
        one = swap(parts[2:4], 1)
        two = swap(parts[4:6], 2)
        for_one = (wide(parts[6]) + wide(two[1])).astype(jnp.bfloat16)
        for_two = (wide(parts[7]) + wide(one[1])).astype(jnp.bfloat16)
        return [parts[:2], one, two, swap(for_two, 2), swap(for_one, 1)]

    def total_of(terms):
        if lo_count != 4:
            total = wide(terms[0])
            for term in terms[1:]:
                total = total + wide(term)
            return total
        own, one, two, last_two, last_one = terms
        return jnp.concatenate(
            [
                wide(own[0]) + wide(one[0]) + wide(last_two),
                wide(own[1]) + wide(two[0]) + wide(last_one),
            ],
            axis=0,
        )

    back = split_back(grad_expert_rows)
    back_parts = bring_back(back)
    grad_gate_up = hold(grad_gate_up, *back_parts[1:3])
    grad_weights_in = jnp.einsum(
        "ekrf,erd->ekfd", grad_gate_up, expert_rows, preferred_element_type=jnp.float32
    ).astype(jnp.bfloat16)
    grad_weights_in, hidden = lax.optimization_barrier((grad_weights_in, hidden))
    shard_in = lax.psum_scatter(
        grad_weights_in.reshape(hi_count * 2 * 2 * shard_cols, model_width),
        ("hi", "core"),
        scatter_dimension=0,
        tiled=True,
    )
    shard_in = shard_in.T.astype(jnp.float32).reshape(model_width, 2, shard_cols)
    produced = (
        jnp.einsum("ekrf,ekfd->erd", hidden, weights_out, preferred_element_type=jnp.float32)
        * slot_weight.reshape(hi_count, -1, 1)
    ).astype(jnp.bfloat16)
    ahead = split_back(produced)
    ahead, back_parts = lax.optimization_barrier((ahead, back_parts))
    ahead_parts = bring_back(ahead)
    grad_normed_two = total_of(back_parts)
    grad_gain_two, grad_from_norm = norm_back(residual, scale_two, gain_two, grad_normed_two)
    grad_residual = grad_output + grad_from_norm
    grad_attended = grad_residual.astype(jnp.bfloat16)
    grad_out_weight = jnp.einsum(
        "nq,nd->qd", mixed_rows, grad_attended, preferred_element_type=jnp.float32
    )
    grad_mixed = jnp.einsum(
        "nd,qd->nq", grad_attended, out_full, preferred_element_type=jnp.float32
    ).astype(jnp.bfloat16)
    grad_queries, grad_keys, grad_values = attend_back(
        queries, key_rows, value_rows, segment, position, logsum, grad_mixed
    )
    grad_queries = rotate(grad_queries, cosine_table, -sine_table)
    grad_keys = rotate(grad_keys, cosine_table, -sine_table)
    grad_projected = jnp.concatenate(
        [
            grad_queries.reshape(tok_dev, q_dim),
            grad_keys.reshape(tok_dev, kv_dim),
            grad_values.reshape(tok_dev, kv_dim),
        ],
        axis=1,
    ).astype(jnp.bfloat16)
    if lo_count == 4:
        normed = hold(normed, *ahead_parts[1:3])
    grad_qkv_weight = jnp.einsum(
        "nd,nc->dc", normed, grad_projected, preferred_element_type=jnp.float32
    )
    grad_normed = jnp.einsum(
        "nc,dc->nd", grad_projected, qkv_full, preferred_element_type=jnp.float32
    )
    grad_gain_one, grad_from_first = norm_back(rows_in, scale_one, gain_one, grad_normed)
    grad_input = (grad_residual + grad_from_first).astype(jnp.bfloat16)
    gains = jnp.pad(jnp.stack([grad_gain_one, grad_gain_two], axis=1), ((0, 0), (0, 126)))
    parts = jnp.concatenate(
        [
            grad_qkv_weight.astype(jnp.bfloat16),
            grad_out_weight.astype(jnp.bfloat16),
            gains.astype(jnp.bfloat16),
        ],
        axis=1,
    ).reshape(sizes + (shard_rows, -1))
    parts, shard_in, shard_out, ahead_parts = lax.optimization_barrier(
        (parts, shard_in, shard_out, ahead_parts)
    )
    output_rows = (residual + total_of(ahead_parts)).astype(jnp.bfloat16)
    home_out, home_grad, sums = closing(
        sizes,
        pick(output_rows, by_arrival).reshape(device_count, peer_rows, model_width),
        pick(grad_input, by_arrival).reshape(device_count, peer_rows, model_width),
        parts,
    )
    shard_qkv = sums[:, :qkv_cols]
    shard_attn_out = sums[:, qkv_cols : qkv_cols + model_width]
    shard_gain_one = sums[:, qkv_cols + model_width]
    shard_gain_two = sums[:, qkv_cols + model_width + 1]
    output = pick(home_out.reshape(tok_dev, model_width), by_asked)
    input_grad = pick(home_grad.reshape(tok_dev, model_width), by_asked)
    return (
        output,
        input_grad,
        shard_gain_one,
        shard_qkv,
        shard_attn_out,
        shard_gain_two,
        shard_in,
        shard_out,
    )


def solution(mesh):
    dp_count = mesh.shape["dp"]
    hi_count = 4 if dp_count % 4 == 0 else 1
    split = jax.sharding.Mesh(
        mesh.devices.reshape(hi_count, dp_count // hi_count, mesh.shape["expert"]), ALL
    )
    rows, columns = P(ALL, None), P(None, None, ALL)
    return jax.shard_map(
        shards,
        mesh=split,
        in_specs=(rows, rows, P(ALL), rows, rows, rows, P(ALL), rows, rows, P(ALL), columns, rows),
        out_specs=(rows, rows, P(ALL), rows, rows, P(ALL), columns, rows),
        check_vma=False,
    )
```

```python
import functools

import jax
import jax.numpy as jnp
from jax import lax
from jax.experimental import pallas as pl
from jax.experimental.pallas import tpu as pltpu
from jax.sharding import PartitionSpec as P

HEADS = 24
KV_HEADS = 8
HEAD = 64
FF_E = 512
TOPK = 8
MB = 2
SEQS = 4
TOK_MB = 256
ALL = ("hi", "lo", "core")


epsilon = 1e-05
theta_base = 10000.0


def layout_rows(length_rows):
    seq_ends = jnp.cumsum(length_rows, axis=1, dtype=jnp.int32)
    starts = seq_ends - length_rows
    within = jnp.arange(TOK_MB, dtype=jnp.int32)
    segment = jnp.sum(
        (within[None, :, None] >= seq_ends[:, None, :]).astype(jnp.int32), axis=2, dtype=jnp.int32
    )
    chosen = segment[:, :, None] == jnp.arange(SEQS, dtype=jnp.int32)[None, None, :]
    seq_begin = jnp.sum(jnp.where(chosen, starts[:, None, :], 0), axis=2, dtype=jnp.int32)
    position = within[None, :] - seq_begin
    segment = segment + jnp.arange(MB, dtype=jnp.int32)[:, None] * SEQS
    return (segment.reshape(-1), position.reshape(-1))


def rope_tables(position):
    half_width = HEAD // 2
    frequency = theta_base ** (-(2.0 / HEAD) * jnp.arange(half_width, dtype=jnp.float32))
    angles = position.astype(jnp.float32)[:, None] * frequency[None, :]
    return (jnp.cos(angles), jnp.sin(angles))


def rotate(values, cosine_table, sine_table):
    half_width = HEAD // 2
    front_half = values[..., :half_width]
    behind = values[..., half_width:]
    cosine_part = cosine_table[:, None, :]
    sine_part = sine_table[:, None, :]
    return jnp.concatenate(
        [
            front_half * cosine_part - behind * sine_part,
            behind * cosine_part + front_half * sine_part,
        ],
        axis=-1,
    )


def slot_tables(ids, gates, experts, capacity):
    count = experts.shape[0]
    named = ids[..., None] == experts
    picked = jnp.any(named, axis=2)
    weight = jnp.sum(jnp.where(named, gates[..., None], 0.0), axis=2)
    rows = jnp.arange(TOK_MB, dtype=jnp.int32)
    below = (rows[:, None] > rows[None, :]).astype(jnp.bfloat16)
    shaped = picked.reshape(-1, TOK_MB, count)
    slot = jnp.einsum(
        "rq,bqe->ber", below, shaped.astype(jnp.bfloat16), preferred_element_type=jnp.float32
    ).astype(jnp.int32)
    kept = jnp.transpose(shaped, (0, 2, 1))
    hit = kept[:, :, None, :] & (
        slot[:, :, None, :] == jnp.arange(capacity, dtype=jnp.int32)[None, None, :, None]
    )
    weight = jnp.transpose(weight.reshape(-1, TOK_MB, count), (0, 2, 1))
    slot_gate = jnp.sum(jnp.where(hit, weight[:, :, None, :], 0.0), axis=3)
    return hit.astype(jnp.bfloat16), slot_gate


def by_batch(rows, heads):
    return rows.reshape(-1, TOK_MB, KV_HEADS, heads // KV_HEADS, HEAD)


def block_scores(queries, key_rows, segment, position):
    scores = jnp.einsum(
        "bqhgd,bkhd->bhgqk", queries, key_rows, preferred_element_type=jnp.float32
    ) * HEAD ** (-0.5)
    allowed = (segment[:, :, None] == segment[:, None, :]) & (
        position[:, :, None] >= position[:, None, :]
    )
    return jnp.where(allowed[:, None, None], scores, -1e30)


def attend_block(queries, key_rows, value_rows, segment, position):
    queries = by_batch(queries, HEADS)
    key_rows = by_batch(key_rows, KV_HEADS)[:, :, :, 0]
    value_rows = by_batch(value_rows, KV_HEADS)[:, :, :, 0]
    segment = segment.reshape(-1, TOK_MB)
    position = position.reshape(-1, TOK_MB)
    masked = block_scores(queries, key_rows, segment, position)
    row_peak = jnp.max(masked, axis=-1, keepdims=True)
    weights_exp = jnp.exp(masked - row_peak)
    row_total = jnp.sum(weights_exp, axis=-1, keepdims=True)
    probabilities = (weights_exp / row_total).astype(jnp.bfloat16)
    mixed_rows = jnp.einsum(
        "bhgqk,bkhd->bqhgd", probabilities, value_rows, preferred_element_type=jnp.float32
    )
    return (mixed_rows.reshape(-1, HEADS * HEAD), row_peak + jnp.log(row_total))


def attend_back(queries, key_rows, value_rows, segment, position, logsum, grad_mixed):
    queries = by_batch(queries, HEADS)
    key_rows = by_batch(key_rows, KV_HEADS)[:, :, :, 0]
    value_rows = by_batch(value_rows, KV_HEADS)[:, :, :, 0]
    segment = segment.reshape(-1, TOK_MB)
    position = position.reshape(-1, TOK_MB)
    masked = block_scores(queries, key_rows, segment, position)
    exact_probs = jnp.exp(masked - logsum)
    probabilities = exact_probs.astype(jnp.bfloat16)
    grad_heads = by_batch(grad_mixed, HEADS)
    grad_probs = jnp.einsum(
        "bqhgd,bkhd->bhgqk", grad_heads, value_rows, preferred_element_type=jnp.float32
    )
    grad_values = jnp.einsum(
        "bhgqk,bqhgd->bkhd", probabilities, grad_heads, preferred_element_type=jnp.float32
    )
    grad_scores = (
        exact_probs * (grad_probs - jnp.sum(grad_probs * exact_probs, axis=-1, keepdims=True))
    ).astype(jnp.bfloat16)
    grad_queries = jnp.einsum(
        "bhgqk,bkhd->bqhgd", grad_scores, key_rows, preferred_element_type=jnp.float32
    ) * HEAD ** (-0.5)
    grad_keys = jnp.einsum(
        "bhgqk,bqhgd->bkhd", grad_scores, queries, preferred_element_type=jnp.float32
    ) * HEAD ** (-0.5)
    return (
        grad_queries.reshape(-1, HEADS, HEAD),
        grad_keys.reshape(-1, KV_HEADS, HEAD),
        grad_values.reshape(-1, KV_HEADS, HEAD),
    )


def pick(rows, index):
    return jnp.take(rows, index, axis=0, mode="clip")


def hold(value, *after):
    anywhere = pl.BlockSpec(memory_space=pl.ANY)
    return pl.pallas_call(
        lambda *refs: None,
        out_shape=jax.ShapeDtypeStruct(value.shape, value.dtype),
        in_specs=[anywhere] * (1 + len(after)),
        out_specs=anywhere,
        input_output_aliases={0: 0},
        name="hold",
    )(value, *after)


def norm_back(values, scale, gain, grad_normed):
    scaled_grad = grad_normed * gain
    grad_gain = jnp.sum(grad_normed * values * scale, axis=0)
    grad_values = scale * scaled_grad - values * scale * scale * scale * jnp.mean(
        scaled_grad * values, axis=1, keepdims=True
    )
    return (grad_gain, grad_values)


MESH = pl.DeviceIdType.MESH


def flip(value, bits):
    bit = 1
    while bit <= bits:
        if bits & bit:
            value = value + bit * (1 - 2 * ((value // bit) % 2))
        bit *= 2
    return value


def place():
    return lax.axis_index("hi"), lax.axis_index("lo"), lax.axis_index("core")


def greet_all(sizes):
    hi_count, lo_count, _ = sizes
    count = hi_count * lo_count * 2
    hi, lo, core = place()
    me = (hi * lo_count + lo) * 2 + core
    barrier = pltpu.get_barrier_semaphore()

    def greet(step, carry):
        peer = (me + step) % count
        pl.semaphore_signal(
            barrier,
            inc=1,
            device_id=(peer // (2 * lo_count), (peer // 2) % lo_count, peer % 2),
            device_id_type=MESH,
        )
        return carry

    lax.fori_loop(1, count, greet, 0)
    pl.semaphore_wait(barrier, count - 1)


def send_rows(sizes, source, target, send_sem, recv_sem):
    hi_count, lo_count, _ = sizes
    count = hi_count * lo_count * 2
    hi, lo, core = place()
    me = (hi * lo_count + lo) * 2 + core

    def one(step, carry):
        peer = (me + step) % count
        pltpu.make_async_remote_copy(
            src_ref=source.at[peer],
            dst_ref=target.at[me],
            send_sem=send_sem,
            recv_sem=recv_sem,
            device_id=(peer // (2 * lo_count), (peer // 2) % lo_count, peer % 2),
            device_id_type=MESH,
        ).start()
        return carry

    lax.fori_loop(1, count, one, 0)


def wait_rows(source, target, send_sem, recv_sem):
    rest = pl.ds(0, source.shape[0] - 1)
    pltpu.make_async_copy(source.at[rest], source.at[rest], send_sem).wait()
    pltpu.make_async_copy(target.at[rest], target.at[rest], recv_sem).wait()


def lo_steps(lo_count, turn):
    bits = []
    bit = 1
    while bit < lo_count:
        bits.append(bit)
        bit *= 2
    if turn:
        bits = bits[::-1]
    held, steps = [0], []
    for bit in bits:
        steps.append((bit, list(held)))
        held = held + [offset ^ bit for offset in held]
    return steps


def opening_kernel(
    sizes, rows_ref, grads_ref, shard_ref, got_ref, got_grads_ref, full_ref,
    own_sem, row_sems, hi_sems, lo_sems, core_sems
):
    hi_count, lo_count, _ = sizes
    hi, lo, core = place()
    me = (hi * lo_count + lo) * 2 + core
    own = [
        pltpu.make_async_copy(shard_ref, full_ref.at[hi, lo, core], own_sem.at[0]),
        pltpu.make_async_copy(rows_ref.at[me], got_ref.at[me], own_sem.at[1]),
        pltpu.make_async_copy(grads_ref.at[me], got_grads_ref.at[me], own_sem.at[2]),
    ]
    for copy in own:
        copy.start()
    greet_all(sizes)

    def hop(source, at, device, sems, *index):
        return pltpu.make_async_remote_copy(
            src_ref=source,
            dst_ref=full_ref.at[at[0], at[1], at[2]],
            send_sem=sems.at[0, *index],
            recv_sem=sems.at[1, *index],
            device_id=device,
            device_id_type=MESH,
        )

    along_hi = {}
    for step in range(1, hi_count):
        along_hi[step] = hop(
            shard_ref, (hi, lo, core), (flip(hi, step), lo, core), hi_sems, step - 1
        )
        along_hi[step].start()
    send_rows(sizes, rows_ref, got_ref, row_sems.at[0, 0], row_sems.at[1, 0])
    send_rows(sizes, grads_ref, got_grads_ref, row_sems.at[0, 1], row_sems.at[1, 1])

    def across(plane, offset, first):
        at = (flip(hi, plane), flip(lo, offset), core)
        source = shard_ref if first else full_ref.at[at[0], at[1], at[2]]
        copy = hop(source, at, (hi, lo, 1 - core), core_sems, plane, offset)
        copy.start()
        return copy

    started, waits = [], []
    for plane in range(hi_count):
        if plane:
            along_hi[plane].wait_recv()
        started.append(across(plane, 0, plane == 0))
        number = 0
        for bit, offsets in lo_steps(lo_count, plane % 2):
            for offset in offsets:
                at = (flip(hi, plane), flip(lo, offset), core)
                source = shard_ref if plane == 0 and offset == 0 else full_ref.at[at[0], at[1], at[2]]
                copy = hop(source, at, (hi, flip(lo, bit), core), lo_sems, plane, number)
                number += 1
                if offset == 0:
                    copy.start()
                    started.append(copy)
                waits.append((copy, plane, offset, bit))
    arrived = {}
    for copy, plane, offset, bit in waits:
        if offset:
            copy.start()
            started.append(copy)
        copy.wait_recv()
        started.append(across(plane, offset ^ bit, False))
    for copy in started:
        copy.wait_send()
    for step in range(1, hi_count):
        along_hi[step].wait_send()
    for plane in range(hi_count):
        for offset in range(lo_count):
            at = (flip(hi, plane), flip(lo, offset), core)
            hop(
                full_ref.at[at[0], at[1], at[2]], at, (hi, lo, 1 - core), core_sems, plane, offset
            ).wait_recv()
    wait_rows(rows_ref, got_ref, row_sems.at[0, 0], row_sems.at[1, 0])
    wait_rows(grads_ref, got_grads_ref, row_sems.at[0, 1], row_sems.at[1, 1])
    for copy in own:
        copy.wait()


def opening(sizes, rows, grads, shard):
    hi_count, lo_count, _ = sizes
    anywhere = pl.BlockSpec(memory_space=pl.ANY)
    return pl.pallas_call(
        functools.partial(opening_kernel, sizes),
        out_shape=(
            jax.ShapeDtypeStruct(rows.shape, rows.dtype),
            jax.ShapeDtypeStruct(grads.shape, grads.dtype),
            jax.ShapeDtypeStruct(sizes + shard.shape, shard.dtype),
        ),
        in_specs=[anywhere] * 3,
        out_specs=(anywhere, anywhere, anywhere),
        scratch_shapes=[
            pltpu.SemaphoreType.DMA((3,)),
            pltpu.SemaphoreType.DMA((2, 2)),
            pltpu.SemaphoreType.DMA((2, hi_count)),
            pltpu.SemaphoreType.DMA((2, hi_count, lo_count)),
            pltpu.SemaphoreType.DMA((2, hi_count, lo_count)),
        ],
        compiler_params=pltpu.CompilerParams(collective_id=0, has_side_effects=True),
        name="opening",
    )(rows, grads, shard)


def add_blocks(target, first, second):
    rows = target.shape[0]
    tile = 16 if rows % 16 == 0 else rows

    def one(index, carry):
        at = pl.ds(index * tile, tile)
        target[at, :] = (
            first[at, :].astype(jnp.float32) + second[at, :].astype(jnp.float32)
        ).astype(target.dtype)
        return carry

    lax.fori_loop(0, rows // tile, one, 0)


def closing_kernel(
    sizes, out_ref, grad_ref, parts_ref, got_out, got_grad, sum_ref,
    from_core, from_lo, from_hi, held, own_sem, row_sems, hi_sems, lo_sems, core_sems
):
    hi_count, lo_count, _ = sizes
    hi, lo, core = place()
    me = (hi * lo_count + lo) * 2 + core
    own = [
        pltpu.make_async_copy(out_ref.at[me], got_out.at[me], own_sem.at[0]),
        pltpu.make_async_copy(grad_ref.at[me], got_grad.at[me], own_sem.at[1]),
    ]
    for copy in own:
        copy.start()
    greet_all(sizes)

    def hop(source, target, device, sems, *index):
        return pltpu.make_async_remote_copy(
            src_ref=source,
            dst_ref=target,
            send_sem=sems.at[0, *index],
            recv_sem=sems.at[1, *index],
            device_id=device,
            device_id_type=MESH,
        )

    planes = [plane for plane in range(1, hi_count)] + [0]
    across = {}
    for plane in planes:
        for offset in reversed(range(lo_count)):
            across[plane, offset] = hop(
                parts_ref.at[flip(hi, plane), flip(lo, offset), 1 - core],
                from_core.at[plane, offset],
                (hi, lo, 1 - core),
                core_sems,
                plane,
                offset,
            )
            across[plane, offset].start()
    send_rows(sizes, grad_ref, got_grad, row_sems.at[0, 0], row_sems.at[1, 0])
    send_rows(sizes, out_ref, got_out, row_sems.at[0, 1], row_sems.at[1, 1])
    started = []
    plans = {plane: lo_steps(lo_count, plane % 2)[::-1] for plane in planes}
    moves = {}
    for depth in range(len(plans[0])):
        for plane in planes:
            bit, kept = plans[plane][depth]
            base = lo_count - 2 * len(kept)
            if depth == 0:
                for offset in [keep ^ bit for keep in kept] + kept:
                    across[plane, offset].wait_recv()
                    add_blocks(
                        held.at[plane, offset],
                        parts_ref.at[flip(hi, plane), flip(lo, offset), core],
                        from_core.at[plane, offset],
                    )
            else:
                before = plans[plane][depth - 1]
                for number, offset in enumerate(before[1]):
                    copy, spot = moves[plane, depth - 1, offset]
                    copy.wait_recv()
                    add_blocks(held.at[plane, offset], held.at[plane, offset], from_lo.at[plane, spot])
            for number, offset in enumerate(kept):
                spot = base + number
                copy = hop(
                    held.at[plane, offset ^ bit],
                    from_lo.at[plane, spot],
                    (hi, flip(lo, bit), core),
                    lo_sems,
                    plane,
                    spot,
                )
                copy.start()
                started.append(copy)
                moves[plane, depth, offset] = (copy, spot)
    last = len(plans[0]) - 1
    along = {}
    for plane in planes:
        copy, spot = moves[plane, last, 0]
        copy.wait_recv()
        add_blocks(held.at[plane, 0], held.at[plane, 0], from_lo.at[plane, spot])
        if plane:
            along[plane] = hop(
                held.at[plane, 0],
                from_hi.at[plane],
                (flip(hi, plane), lo, core),
                hi_sems,
                plane,
            )
            along[plane].start()
            started.append(along[plane])
    for plane in range(1, hi_count):
        along[plane].wait_recv()
    rows = sum_ref.shape[0]
    tile = 16 if rows % 16 == 0 else rows

    def total(index, carry):
        at = pl.ds(index * tile, tile)
        value = held[0, 0, at, :].astype(jnp.float32)
        for plane in range(1, hi_count):
            value = value + from_hi[plane, at, :].astype(jnp.float32)
        sum_ref[at, :] = value
        return carry

    lax.fori_loop(0, rows // tile, total, 0)
    for copy in started:
        copy.wait_send()
    for copy in across.values():
        copy.wait_send()
    wait_rows(grad_ref, got_grad, row_sems.at[0, 0], row_sems.at[1, 0])
    wait_rows(out_ref, got_out, row_sems.at[0, 1], row_sems.at[1, 1])
    for copy in own:
        copy.wait()


def closing(sizes, out_rows, grad_rows, parts):
    hi_count, lo_count, _ = sizes
    block = parts.shape[3:]
    anywhere = pl.BlockSpec(memory_space=pl.ANY)
    near = pl.BlockSpec(memory_space=pltpu.VMEM)
    return pl.pallas_call(
        functools.partial(closing_kernel, sizes),
        out_shape=(
            jax.ShapeDtypeStruct(out_rows.shape, out_rows.dtype),
            jax.ShapeDtypeStruct(grad_rows.shape, grad_rows.dtype),
            jax.ShapeDtypeStruct(block, jnp.float32),
        ),
        in_specs=[anywhere, anywhere, near],
        out_specs=(anywhere, anywhere, near),
        scratch_shapes=[
            pltpu.VMEM((hi_count, lo_count) + block, jnp.bfloat16),
            pltpu.VMEM((hi_count, lo_count) + block, jnp.bfloat16),
            pltpu.VMEM((hi_count,) + block, jnp.bfloat16),
            pltpu.VMEM((hi_count, lo_count) + block, jnp.bfloat16),
            pltpu.SemaphoreType.DMA((2,)),
            pltpu.SemaphoreType.DMA((2, 2)),
            pltpu.SemaphoreType.DMA((2, hi_count)),
            pltpu.SemaphoreType.DMA((2, hi_count, lo_count)),
            pltpu.SemaphoreType.DMA((2, hi_count, lo_count)),
        ],
        compiler_params=pltpu.CompilerParams(
            collective_id=1, has_side_effects=True, vmem_limit_bytes=60 << 20
        ),
        name="closing",
    )(out_rows, grad_rows, parts)


def dispatch_kernel(weighted, choose_ref, rows_ref, *refs):
    count, capacity, rows = choose_ref.shape[1:]
    chosen = choose_ref[0].reshape(count * capacity, rows)
    width = rows_ref.shape[1]
    tile = 256 if width % 256 == 0 else width
    for start in range(0, width, tile):
        at = pl.ds(start, tile)
        slots = jnp.dot(chosen, rows_ref[:, at], preferred_element_type=jnp.float32)
        slots = slots.reshape(count, capacity, tile)
        if weighted:
            slots = slots * refs[0][:, 0]
        refs[-1][:, 0, :, at] = slots.astype(jnp.bfloat16)


def dispatch(choose, rows, first, stride, slots, weight):
    _, count, capacity, _ = choose.shape
    width = rows.shape[1]
    operands = [choose, rows]
    in_specs = [
        pl.BlockSpec((1, count, capacity, TOK_MB), lambda b: (first + b * stride, 0, 0, 0)),
        pl.BlockSpec((TOK_MB, width), lambda b: (b, 0)),
    ]
    if weight is not None:
        operands.append(weight)
        in_specs.append(pl.BlockSpec((count, 1, capacity, 1), lambda b: (0, first + b * stride, 0, 0)))
    aliases = {}
    if slots is not None:
        aliases = {len(operands): 0}
        operands.append(slots)
        in_specs.append(pl.BlockSpec(memory_space=pl.ANY))
    return pl.pallas_call(
        functools.partial(dispatch_kernel, weight is not None),
        grid=(rows.shape[0] // TOK_MB,),
        out_shape=jax.ShapeDtypeStruct((count, choose.shape[0], capacity, width), jnp.bfloat16),
        in_specs=in_specs,
        out_specs=pl.BlockSpec((count, 1, capacity, width), lambda b: (0, first + b * stride, 0, 0)),
        input_output_aliases=aliases,
        name="dispatch",
    )(*operands)


def middle_kernel(rows_ref, weight_ref, grad_ref, hidden_ref, grad_out_ref):
    half = grad_ref.shape[3]
    for part in range(weight_ref.shape[1]):
        gate_up = jnp.dot(rows_ref[0], weight_ref[0, part], preferred_element_type=jnp.float32)
        gate, up = gate_up[:, :half], gate_up[:, half:]
        sigmoid_gate = jax.nn.sigmoid(gate)
        active = gate * sigmoid_gate
        grad_hidden = grad_ref[0, part].astype(jnp.float32)
        hidden_ref[0, part] = (active * up).astype(jnp.bfloat16)
        slope = sigmoid_gate * (1.0 + gate * (1.0 - sigmoid_gate))
        grad_out_ref[0, part, :, :half] = (grad_hidden * up * slope).astype(jnp.bfloat16)
        grad_out_ref[0, part, :, half:] = (grad_hidden * active).astype(jnp.bfloat16)


def middle(expert_rows, weights_in, grad_hidden):
    count, row_count, width = expert_rows.shape
    parts, both = weights_in.shape[1], weights_in.shape[3]
    tile = 512 if row_count % 512 == 0 else row_count
    return pl.pallas_call(
        middle_kernel,
        grid=(count, row_count // tile),
        out_shape=(
            jax.ShapeDtypeStruct((count, parts, row_count, both // 2), jnp.bfloat16),
            jax.ShapeDtypeStruct((count, parts, row_count, both), jnp.bfloat16),
        ),
        in_specs=[
            pl.BlockSpec((1, tile, width), lambda e, t: (e, t, 0)),
            pl.BlockSpec((1, parts, width, both), lambda e, t: (e, 0, 0, 0)),
            pl.BlockSpec((1, parts, tile, both // 2), lambda e, t: (e, 0, t, 0)),
        ],
        out_specs=(
            pl.BlockSpec((1, parts, tile, both // 2), lambda e, t: (e, 0, t, 0)),
            pl.BlockSpec((1, parts, tile, both), lambda e, t: (e, 0, t, 0)),
        ),
        name="middle",
    )(expert_rows, weights_in, grad_hidden)


def shards(
    tokens,
    cotangent,
    permutation,
    lengths,
    expert_ids,
    gate_weights,
    attn_gain,
    qkv_weight,
    out_weight,
    ffn_gain,
    expert_in,
    expert_out,
):
    device_count = lax.axis_size(ALL)
    hi_count = lax.axis_size("hi")
    lo_count = lax.axis_size("lo")
    tok_dev = permutation.shape[0]
    model_width = tokens.shape[1]
    peer_rows = tok_dev // device_count
    q_dim = HEADS * HEAD
    kv_dim = KV_HEADS * HEAD
    positions = jnp.arange(tok_dev, dtype=jnp.int32)
    expert_count = expert_in.shape[2] * device_count // FF_E
    capacity = TOK_MB * TOPK // expert_count
    source = permutation // tok_dev
    local_row = permutation % tok_dev
    from_source = (source[:, None] == jnp.arange(device_count, dtype=jnp.int32)[None, :]).astype(
        jnp.int32
    )
    earlier = jnp.cumsum(from_source, axis=0, dtype=jnp.int32) - from_source
    arrival = source * peer_rows + jnp.sum(earlier * from_source, axis=1, dtype=jnp.int32)
    arrival_match = arrival[:, None] == positions[None, :]
    wanted = jnp.sum(jnp.where(arrival_match, local_row[:, None], 0), axis=0, dtype=jnp.int32)
    by_arrival = jnp.sum(jnp.where(arrival_match, positions[:, None], 0), axis=0, dtype=jnp.int32)
    def swap(block, step):
        return lax.ppermute(block, "lo", [(i, i ^ step) for i in range(lo_count)])

    def spread(block):
        if lo_count != 4:
            return [[block]] + [[swap(block, step)] for step in range(1, lo_count)]
        half = block.shape[0] // 2
        one, two = swap(block, 1), swap(block, 2)
        return [[block], [one], [two], [swap(one[:half], 2), swap(two[half:], 1)]]

    if lo_count == 4:
        order = [(0, 0), (0, 1), (1, 0), (3, 0), (2, 1), (3, 1), (1, 1), (2, 0)]
    else:
        order = [(step, batch) for step in range(lo_count) for batch in range(MB)]
    routing = jnp.concatenate([expert_ids.astype(jnp.float32), gate_weights], axis=1)
    routing_all = [routing] + [swap(routing, step) for step in range(1, lo_count)]
    routing_all = jnp.stack(
        [routing_all[step][batch * TOK_MB : (batch + 1) * TOK_MB] for step, batch in order]
    )
    asked_rows = lax.all_to_all(
        wanted.reshape(device_count, peer_rows),
        ALL,
        split_axis=0,
        concat_axis=0,
        tiled=True,
    ).reshape(tok_dev)
    asked_rows, routing_all = lax.optimization_barrier((asked_rows, routing_all))
    asked_match = asked_rows[:, None] == positions[None, :]
    by_asked = jnp.sum(jnp.where(asked_match, positions[:, None], 0), axis=0, dtype=jnp.int32)
    sizes = (hi_count, lo_count, 2)
    shard_rows = qkv_weight.shape[0]
    qkv_cols = qkv_weight.shape[1]
    weight_shard = jnp.concatenate(
        [
            qkv_weight,
            out_weight,
            attn_gain[:, None],
            ffn_gain[:, None],
            jnp.zeros((shard_rows, 126), jnp.bfloat16),
        ],
        axis=1,
    )
    asked_tokens = pick(tokens, asked_rows).reshape(device_count, peer_rows, model_width)
    asked_grads = pick(cotangent, asked_rows).reshape(
        device_count, peer_rows, model_width
    )
    got_rows, got_grad, packed = opening(sizes, asked_tokens, asked_grads, weight_shard)
    got_rows, packed, expert_in = lax.optimization_barrier((got_rows, packed, expert_in))
    packed = packed.reshape(model_width, -1)
    grad_bf = pick(got_grad.reshape(tok_dev, model_width), arrival)
    got_rows = hold(got_rows, grad_bf)
    grad_blocks = spread(grad_bf)
    rows_in = pick(got_rows.reshape(tok_dev, model_width), arrival).astype(jnp.float32)
    qkv_full = packed[:, :qkv_cols]
    out_full = packed[:, qkv_cols : qkv_cols + model_width]
    gain_pair = packed[:, qkv_cols + model_width :].astype(jnp.float32)
    gain_one = gain_pair[:, 0]
    gain_two = gain_pair[:, 1]
    shard_cols = expert_in.shape[2]
    weights_in = lax.all_gather(
        expert_in.reshape(model_width, 2 * shard_cols), ("hi", "core"), axis=0
    ).reshape(hi_count, 2, model_width, 2 * shard_cols)
    weights_out = lax.all_gather(expert_out, ("hi", "core"), axis=0).reshape(
        hi_count, 2, shard_cols, model_width
    )
    segment, position = layout_rows(lengths)
    scale_one = lax.rsqrt(jnp.mean(rows_in * rows_in, axis=1, keepdims=True) + epsilon)
    normed = (rows_in * scale_one * gain_one).astype(jnp.bfloat16)
    projected = jnp.dot(normed, qkv_full, preferred_element_type=jnp.float32)
    cosine_table, sine_table = rope_tables(position)
    if lo_count == 4:
        segment = hold(segment, grad_blocks[1][0], grad_blocks[2][0])
    queries = rotate(
        projected[:, :q_dim].reshape(tok_dev, HEADS, HEAD), cosine_table, sine_table
    ).astype(jnp.bfloat16)
    key_rows = rotate(
        projected[:, q_dim : q_dim + kv_dim].reshape(tok_dev, KV_HEADS, HEAD),
        cosine_table,
        sine_table,
    ).astype(jnp.bfloat16)
    value_rows = (
        projected[:, q_dim + kv_dim :].reshape(tok_dev, KV_HEADS, HEAD).astype(jnp.bfloat16)
    )
    mixed_part, logsum = attend_block(queries, key_rows, value_rows, segment, position)
    mixed_rows = mixed_part.astype(jnp.bfloat16)
    attended = jnp.dot(mixed_rows, out_full, preferred_element_type=jnp.float32)
    residual = rows_in + attended
    scale_two = lax.rsqrt(jnp.mean(residual * residual, axis=1, keepdims=True) + epsilon)
    normed_two = (residual * scale_two * gain_two).astype(jnp.bfloat16)
    grad_output = grad_bf.astype(jnp.float32)
    home = lax.axis_index("lo")
    if lo_count == 4:
        normed_two = hold(normed_two, *grad_blocks[3])
    row_blocks = spread(normed_two)
    normed_two, grad_blocks = lax.optimization_barrier((normed_two, grad_blocks))
    choose, slot_gate = slot_tables(
        routing_all[..., :TOPK].astype(jnp.int32),
        routing_all[..., TOPK:],
        home + lo_count * jnp.arange(hi_count, dtype=jnp.int32),
        capacity,
    )
    slot_weight = jnp.transpose(slot_gate, (1, 0, 2))[..., None]
    place_of = {name: number for number, name in enumerate(order)}

    def fill(blocks, slots, weight):
        for step, pieces in blocks:
            batch = 0
            for piece in pieces:
                first = place_of[step, batch]
                stride = place_of[step, MB - 1] - place_of[step, 0]
                slots = dispatch(choose, piece, first, stride, slots, weight)
                batch += piece.shape[0] // TOK_MB
        return slots

    grad_expert = fill(list(enumerate(grad_blocks)), None, slot_weight)
    grad_expert = grad_expert.reshape(hi_count, -1, model_width)
    grad_hidden = jnp.einsum(
        "erd,ekfd->ekrf", grad_expert, weights_out, preferred_element_type=jnp.float32
    ).astype(jnp.bfloat16)
    expert_rows = fill([(0, [normed_two])], None, None)
    grad_hidden, expert_rows, others = lax.optimization_barrier(
        (grad_hidden, expert_rows, row_blocks[1:])
    )
    expert_rows = fill(list(enumerate(others, 1)), expert_rows, None)
    expert_rows = expert_rows.reshape(hi_count, -1, model_width)
    hidden, grad_gate_up = middle(expert_rows, weights_in, grad_hidden)
    grad_weights_out = jnp.einsum(
        "ekrf,erd->ekfd", hidden, grad_expert, preferred_element_type=jnp.float32
    ).astype(jnp.bfloat16)
    grad_weights_out, grad_gate_up = lax.optimization_barrier((grad_weights_out, grad_gate_up))
    shard_out = lax.psum_scatter(
        grad_weights_out.reshape(hi_count * 2 * shard_cols, model_width),
        ("hi", "core"),
        scatter_dimension=0,
        tiled=True,
    ).astype(jnp.float32)
    grad_expert_rows = jnp.einsum(
        "ekrf,ekdf->erd", grad_gate_up, weights_in, preferred_element_type=jnp.float32
    ).astype(jnp.bfloat16)

    def split_back(slot_values):
        return jnp.einsum(
            "becr,ebcd->brd",
            choose,
            slot_values.reshape(hi_count, lo_count * MB, capacity, model_width),
            preferred_element_type=jnp.float32,
        ).astype(jnp.bfloat16)

    def wide(value):
        return value.astype(jnp.float32)

    def bring_back(parts):
        if lo_count != 4:
            parts = parts.reshape(lo_count, tok_dev, model_width)
            return [parts[0]] + [swap(parts[step], step) for step in range(1, lo_count)]
        one = swap(parts[2:4], 1)
        two = swap(parts[4:6], 2)
        for_one = (wide(parts[6]) + wide(two[1])).astype(jnp.bfloat16)
        for_two = (wide(parts[7]) + wide(one[1])).astype(jnp.bfloat16)
        return [parts[:2], one, two, swap(for_two, 2), swap(for_one, 1)]

    def total_of(terms):
        if lo_count != 4:
            total = wide(terms[0])
            for term in terms[1:]:
                total = total + wide(term)
            return total
        own, one, two, last_two, last_one = terms
        return jnp.concatenate(
            [
                wide(own[0]) + wide(one[0]) + wide(last_two),
                wide(own[1]) + wide(two[0]) + wide(last_one),
            ],
            axis=0,
        )

    back = split_back(grad_expert_rows)
    back_parts = bring_back(back)
    produced = (
        jnp.einsum("ekrf,ekfd->erd", hidden, weights_out, preferred_element_type=jnp.float32)
        * slot_weight.reshape(hi_count, -1, 1)
    ).astype(jnp.bfloat16)
    ahead = split_back(produced)
    grad_gate_up = hold(grad_gate_up, ahead, *back_parts[1:3])
    grad_weights_in = jnp.einsum(
        "ekrf,erd->ekfd", grad_gate_up, expert_rows, preferred_element_type=jnp.float32
    ).astype(jnp.bfloat16)
    shard_in = lax.psum_scatter(
        grad_weights_in.reshape(hi_count * 2 * 2 * shard_cols, model_width),
        ("hi", "core"),
        scatter_dimension=0,
        tiled=True,
    )
    shard_in = shard_in.T.astype(jnp.float32).reshape(model_width, 2, shard_cols)
    ahead, back_parts = lax.optimization_barrier((ahead, back_parts))
    ahead_parts = bring_back(ahead)
    grad_normed_two = total_of(back_parts)
    grad_gain_two, grad_from_norm = norm_back(residual, scale_two, gain_two, grad_normed_two)
    grad_residual = grad_output + grad_from_norm
    grad_attended = grad_residual.astype(jnp.bfloat16)
    grad_out_weight = jnp.einsum(
        "nq,nd->qd", mixed_rows, grad_attended, preferred_element_type=jnp.float32
    )
    grad_mixed = jnp.einsum(
        "nd,qd->nq", grad_attended, out_full, preferred_element_type=jnp.float32
    ).astype(jnp.bfloat16)
    grad_queries, grad_keys, grad_values = attend_back(
        queries, key_rows, value_rows, segment, position, logsum, grad_mixed
    )
    grad_queries = rotate(grad_queries, cosine_table, -sine_table)
    grad_keys = rotate(grad_keys, cosine_table, -sine_table)
    grad_projected = jnp.concatenate(
        [
            grad_queries.reshape(tok_dev, q_dim),
            grad_keys.reshape(tok_dev, kv_dim),
            grad_values.reshape(tok_dev, kv_dim),
        ],
        axis=1,
    ).astype(jnp.bfloat16)
    if lo_count == 4:
        normed = hold(normed, *ahead_parts[1:3])
    grad_qkv_weight = jnp.einsum(
        "nd,nc->dc", normed, grad_projected, preferred_element_type=jnp.float32
    )
    grad_normed = jnp.einsum(
        "nc,dc->nd", grad_projected, qkv_full, preferred_element_type=jnp.float32
    )
    grad_gain_one, grad_from_first = norm_back(rows_in, scale_one, gain_one, grad_normed)
    grad_input = (grad_residual + grad_from_first).astype(jnp.bfloat16)
    gains = jnp.pad(jnp.stack([grad_gain_one, grad_gain_two], axis=1), ((0, 0), (0, 126)))
    parts = jnp.concatenate(
        [
            grad_qkv_weight.astype(jnp.bfloat16),
            grad_out_weight.astype(jnp.bfloat16),
            gains.astype(jnp.bfloat16),
        ],
        axis=1,
    ).reshape(sizes + (shard_rows, -1))
    parts, shard_out, ahead_parts = lax.optimization_barrier((parts, shard_out, ahead_parts))
    output_rows = (residual + total_of(ahead_parts)).astype(jnp.bfloat16)
    home_out, home_grad, sums = closing(
        sizes,
        pick(output_rows, by_arrival).reshape(device_count, peer_rows, model_width),
        pick(grad_input, by_arrival).reshape(device_count, peer_rows, model_width),
        parts,
    )
    shard_qkv = sums[:, :qkv_cols]
    shard_attn_out = sums[:, qkv_cols : qkv_cols + model_width]
    shard_gain_one = sums[:, qkv_cols + model_width]
    shard_gain_two = sums[:, qkv_cols + model_width + 1]
    output = pick(home_out.reshape(tok_dev, model_width), by_asked)
    input_grad = pick(home_grad.reshape(tok_dev, model_width), by_asked)
    return (
        output,
        input_grad,
        shard_gain_one,
        shard_qkv,
        shard_attn_out,
        shard_gain_two,
        shard_in,
        shard_out,
    )


def solution(mesh):
    dp_count = mesh.shape["dp"]
    hi_count = 4 if dp_count % 4 == 0 else 1
    split = jax.sharding.Mesh(
        mesh.devices.reshape(hi_count, dp_count // hi_count, mesh.shape["expert"]), ALL
    )
    rows, columns = P(ALL, None), P(None, None, ALL)
    return jax.shard_map(
        shards,
        mesh=split,
        in_specs=(rows, rows, P(ALL), rows, rows, rows, P(ALL), rows, rows, P(ALL), columns, rows),
        out_specs=(rows, rows, P(ALL), rows, rows, P(ALL), columns, rows),
        check_vma=False,
    )
```

```python
import functools

import jax
import jax.numpy as jnp
from jax import lax
from jax.experimental import pallas as pl
from jax.experimental.pallas import tpu as pltpu
from jax.sharding import PartitionSpec as P

HEADS = 24
KV_HEADS = 8
HEAD = 64
FF_E = 512
TOPK = 8
MB = 2
SEQS = 4
TOK_MB = 256
ALL = ("hi", "lo", "core")


epsilon = 1e-05
theta_base = 10000.0


def layout_rows(length_rows):
    seq_ends = jnp.cumsum(length_rows, axis=1, dtype=jnp.int32)
    starts = seq_ends - length_rows
    within = jnp.arange(TOK_MB, dtype=jnp.int32)
    segment = jnp.sum(
        (within[None, :, None] >= seq_ends[:, None, :]).astype(jnp.int32), axis=2, dtype=jnp.int32
    )
    chosen = segment[:, :, None] == jnp.arange(SEQS, dtype=jnp.int32)[None, None, :]
    seq_begin = jnp.sum(jnp.where(chosen, starts[:, None, :], 0), axis=2, dtype=jnp.int32)
    position = within[None, :] - seq_begin
    segment = segment + jnp.arange(MB, dtype=jnp.int32)[:, None] * SEQS
    return (segment.reshape(-1), position.reshape(-1))


def rope_tables(position):
    half_width = HEAD // 2
    frequency = theta_base ** (-(2.0 / HEAD) * jnp.arange(half_width, dtype=jnp.float32))
    angles = position.astype(jnp.float32)[:, None] * frequency[None, :]
    return (jnp.cos(angles), jnp.sin(angles))


def slot_tables(ids, gates, experts, capacity):
    count = experts.shape[0]
    named = ids[..., None] == experts
    picked = jnp.any(named, axis=2)
    weight = jnp.sum(jnp.where(named, gates[..., None], 0.0), axis=2)
    rows = jnp.arange(TOK_MB, dtype=jnp.int32)
    below = (rows[:, None] > rows[None, :]).astype(jnp.bfloat16)
    shaped = picked.reshape(-1, TOK_MB, count)
    slot = jnp.einsum(
        "rq,bqe->ber", below, shaped.astype(jnp.bfloat16), preferred_element_type=jnp.float32
    ).astype(jnp.int32)
    kept = jnp.transpose(shaped, (0, 2, 1))
    hit = kept[:, :, None, :] & (
        slot[:, :, None, :] == jnp.arange(capacity, dtype=jnp.int32)[None, None, :, None]
    )
    weight = jnp.transpose(weight.reshape(-1, TOK_MB, count), (0, 2, 1))
    slot_gate = jnp.sum(jnp.where(hit, weight[:, :, None, :], 0.0), axis=3)
    return hit.astype(jnp.bfloat16), slot_gate


def partner(values):
    half = HEAD // 2
    lane = lax.broadcasted_iota(jnp.int32, values.shape, 1) % HEAD
    return jnp.where(
        lane < half, pltpu.roll(values, 2 * HEAD - half, 1), pltpu.roll(values, half, 1)
    )


def allowed_keys(seg_col_ref, seg_row_ref, first, count):
    keys = first + count
    rows = lax.broadcasted_iota(jnp.int32, (count, keys), 0) + first
    columns = lax.broadcasted_iota(jnp.int32, (count, keys), 1)
    same = seg_col_ref[0, first : first + count, :] == seg_row_ref[0, :, :keys]
    return same & (rows >= columns)


def soft_weights(queries, keys, allowed):
    scores = lax.dot_general(
        queries, keys, (((1,), (1,)), ((), ())), preferred_element_type=jnp.float32
    )
    scores = jnp.where(allowed, scores, -1e30)
    weights = jnp.exp(scores - jnp.max(scores, axis=-1, keepdims=True))
    return weights * (1.0 / jnp.sum(weights, axis=-1, keepdims=True))


def attend_kernel(
    q_ref, k_ref, v_ref, cos_ref, sin_ref, seg_col_ref, seg_row_ref,
    q_out, k_out, v_out, mixed_ref
):
    cosine, sine = cos_ref[...], sin_ref[...]
    pair = 2 * HEAD
    group = HEADS // KV_HEADS
    for start in range(0, q_ref.shape[1], pair):
        values = q_ref[:, start : start + pair]
        turned = (values * cosine + partner(values) * sine).astype(jnp.bfloat16)
        q_out[:, start : start + pair] = turned * jnp.bfloat16(HEAD**-0.5)
    values = k_ref[...]
    k_out[...] = (values * cosine + partner(values) * sine).astype(jnp.bfloat16)
    v_out[...] = v_ref[...].astype(jnp.bfloat16)
    block = TOK_MB // 2
    for first in range(0, TOK_MB, block):
        rows, keys = slice(first, first + block), slice(0, first + block)
        allowed = allowed_keys(seg_col_ref, seg_row_ref, first, block)
        for one in range(2):
            lanes = slice(one * HEAD, (one + 1) * HEAD)
            key_rows, value_rows = k_out[keys, lanes], v_out[keys, lanes]
            for head in range(one * group, (one + 1) * group):
                at = slice(head * HEAD, (head + 1) * HEAD)
                weights = soft_weights(q_out[rows, at], key_rows, allowed).astype(jnp.bfloat16)
                mixed_ref[rows, at] = jnp.dot(
                    weights, value_rows, preferred_element_type=jnp.float32
                ).astype(jnp.bfloat16)


def attend_back_kernel(
    q_ref, k_ref, v_ref, grad_ref, cos_ref, sin_ref, seg_col_ref, seg_row_ref,
    dq_ref, dk_ref, dv_ref, dq_sum, dk_sum, dv_sum
):
    cosine, sine = cos_ref[...], sin_ref[...]
    pair = 2 * HEAD
    group = HEADS // KV_HEADS
    block = TOK_MB // 2
    over_rows = (((0,), (0,)), ((), ()))
    over_lanes = (((1,), (1,)), ((), ()))
    for first in range(TOK_MB - block, -1, -block):
        rows, keys = slice(first, first + block), slice(0, first + block)
        allowed = allowed_keys(seg_col_ref, seg_row_ref, first, block)
        for one in range(2):
            lanes = slice(one * HEAD, (one + 1) * HEAD)
            key_rows, value_rows = k_ref[keys, lanes], v_ref[keys, lanes]
            grad_keys = grad_values = 0.0
            for head in range(one * group, (one + 1) * group):
                at = slice(head * HEAD, (head + 1) * HEAD)
                queries, grads = q_ref[rows, at], grad_ref[rows, at]
                weights = soft_weights(queries, key_rows, allowed)
                grad_weights = lax.dot_general(
                    grads, value_rows, over_lanes, preferred_element_type=jnp.float32
                )
                grad_values += lax.dot_general(
                    weights.astype(jnp.bfloat16), grads, over_rows,
                    preferred_element_type=jnp.float32,
                )
                inner = jnp.sum(grad_weights * weights, axis=-1, keepdims=True)
                grad_scores = (weights * (grad_weights - inner)).astype(jnp.bfloat16)
                dq_sum[rows, at] = jnp.dot(
                    grad_scores, key_rows, preferred_element_type=jnp.float32
                ) * HEAD ** (-0.5)
                grad_keys += lax.dot_general(
                    grad_scores, queries, over_rows, preferred_element_type=jnp.float32
                )
            if first == TOK_MB - block:
                dk_sum[keys, lanes] = grad_keys
                dv_sum[keys, lanes] = grad_values
            else:
                dk_sum[keys, lanes] = dk_sum[keys, lanes] + grad_keys
                dv_sum[keys, lanes] = dv_sum[keys, lanes] + grad_values
    for start in range(0, q_ref.shape[1], pair):
        values = dq_sum[:, start : start + pair]
        dq_ref[:, start : start + pair] = (
            values * cosine - partner(values) * sine
        ).astype(jnp.bfloat16)
    values = dk_sum[...]
    dk_ref[...] = (values * cosine - partner(values) * sine).astype(jnp.bfloat16)
    dv_ref[...] = dv_sum[...].astype(jnp.bfloat16)


def attend_blocks(row_count):
    pair = 2 * HEAD
    wide = pair * (HEADS // KV_HEADS)
    narrow = pl.BlockSpec((TOK_MB, pair), lambda b, g: (b, g))
    broad = pl.BlockSpec((TOK_MB, wide), lambda b, g: (b, g))
    sides = [
        pl.BlockSpec((TOK_MB, pair), lambda b, g: (b, 0)),
        pl.BlockSpec((TOK_MB, pair), lambda b, g: (b, 0)),
        pl.BlockSpec((1, TOK_MB, 1), lambda b, g: (b, 0, 0)),
        pl.BlockSpec((1, 1, TOK_MB), lambda b, g: (b, 0, 0)),
    ]
    return (row_count // TOK_MB, KV_HEADS // 2), narrow, broad, sides


def attend(projected, sides):
    row_count = projected.shape[0]
    grid, narrow, broad, side_specs = attend_blocks(row_count)
    q_dim, kv_dim, pair = HEADS * HEAD, KV_HEADS * HEAD, 2 * HEAD
    key_start, value_start = q_dim // pair, (q_dim + kv_dim) // pair
    q_shape = jax.ShapeDtypeStruct((row_count, q_dim), jnp.bfloat16)
    kv_shape = jax.ShapeDtypeStruct((row_count, kv_dim), jnp.bfloat16)
    return pl.pallas_call(
        attend_kernel,
        grid=grid,
        out_shape=(q_shape, kv_shape, kv_shape, q_shape),
        in_specs=[
            broad,
            pl.BlockSpec((TOK_MB, pair), lambda b, g: (b, key_start + g)),
            pl.BlockSpec((TOK_MB, pair), lambda b, g: (b, value_start + g)),
        ]
        + side_specs,
        out_specs=(broad, narrow, narrow, broad),
        name="attend",
    )(projected, projected, projected, *sides)


def attend_back(queries, key_rows, value_rows, grad_mixed, sides):
    row_count = queries.shape[0]
    grid, narrow, broad, side_specs = attend_blocks(row_count)
    shapes = [jax.ShapeDtypeStruct(x.shape, jnp.bfloat16) for x in (queries, key_rows, value_rows)]
    return pl.pallas_call(
        attend_back_kernel,
        grid=grid,
        out_shape=tuple(shapes),
        in_specs=[broad, narrow, narrow, broad] + side_specs,
        out_specs=(broad, narrow, narrow),
        scratch_shapes=[
            pltpu.VMEM((TOK_MB, 2 * HEAD * (HEADS // KV_HEADS)), jnp.float32),
            pltpu.VMEM((TOK_MB, 2 * HEAD), jnp.float32),
            pltpu.VMEM((TOK_MB, 2 * HEAD), jnp.float32),
        ],
        name="attend_back",
    )(queries, key_rows, value_rows, grad_mixed, *sides)


def pick(rows, index):
    return jnp.take(rows, index, axis=0, mode="clip")


def hold(value, *after):
    anywhere = pl.BlockSpec(memory_space=pl.ANY)
    return pl.pallas_call(
        lambda *refs: None,
        out_shape=jax.ShapeDtypeStruct(value.shape, value.dtype),
        in_specs=[anywhere] * (1 + len(after)),
        out_specs=anywhere,
        input_output_aliases={0: 0},
        name="hold",
    )(value, *after)


def norm_back(values, scale, gain, grad_normed):
    scaled_grad = grad_normed * gain
    grad_gain = jnp.sum(grad_normed * values * scale, axis=0)
    grad_values = scale * scaled_grad - values * scale * scale * scale * jnp.mean(
        scaled_grad * values, axis=1, keepdims=True
    )
    return (grad_gain, grad_values)


MESH = pl.DeviceIdType.MESH


def flip(value, bits):
    bit = 1
    while bit <= bits:
        if bits & bit:
            value = value + bit * (1 - 2 * ((value // bit) % 2))
        bit *= 2
    return value


def place():
    return lax.axis_index("hi"), lax.axis_index("lo"), lax.axis_index("core")


def greet_all(sizes):
    hi_count, lo_count, _ = sizes
    count = hi_count * lo_count * 2
    hi, lo, core = place()
    me = (hi * lo_count + lo) * 2 + core
    barrier = pltpu.get_barrier_semaphore()

    def greet(step, carry):
        peer = (me + step) % count
        pl.semaphore_signal(
            barrier,
            inc=1,
            device_id=(peer // (2 * lo_count), (peer // 2) % lo_count, peer % 2),
            device_id_type=MESH,
        )
        return carry

    lax.fori_loop(1, count, greet, 0)
    pl.semaphore_wait(barrier, count - 1)


def send_rows(sizes, source, target, send_sem, recv_sem):
    hi_count, lo_count, _ = sizes
    count = hi_count * lo_count * 2
    hi, lo, core = place()
    me = (hi * lo_count + lo) * 2 + core

    def one(step, carry):
        peer = (me + step) % count
        pltpu.make_async_remote_copy(
            src_ref=source.at[peer],
            dst_ref=target.at[me],
            send_sem=send_sem,
            recv_sem=recv_sem,
            device_id=(peer // (2 * lo_count), (peer // 2) % lo_count, peer % 2),
            device_id_type=MESH,
        ).start()
        return carry

    lax.fori_loop(1, count, one, 0)


def wait_rows(source, target, send_sem, recv_sem):
    rest = pl.ds(0, source.shape[0] - 1)
    pltpu.make_async_copy(source.at[rest], source.at[rest], send_sem).wait()
    pltpu.make_async_copy(target.at[rest], target.at[rest], recv_sem).wait()


def lo_steps(lo_count, turn):
    bits = []
    bit = 1
    while bit < lo_count:
        bits.append(bit)
        bit *= 2
    if turn:
        bits = bits[::-1]
    held, steps = [0], []
    for bit in bits:
        steps.append((bit, list(held)))
        held = held + [offset ^ bit for offset in held]
    return steps


def opening_kernel(
    sizes, rows_ref, grads_ref, shard_ref, got_ref, got_grads_ref, full_ref,
    own_sem, row_sems, hi_sems, lo_sems, core_sems
):
    hi_count, lo_count, _ = sizes
    hi, lo, core = place()
    me = (hi * lo_count + lo) * 2 + core
    own = [
        pltpu.make_async_copy(shard_ref, full_ref.at[hi, lo, core], own_sem.at[0]),
        pltpu.make_async_copy(rows_ref.at[me], got_ref.at[me], own_sem.at[1]),
        pltpu.make_async_copy(grads_ref.at[me], got_grads_ref.at[me], own_sem.at[2]),
    ]
    for copy in own:
        copy.start()
    greet_all(sizes)

    def hop(source, at, device, sems, *index):
        return pltpu.make_async_remote_copy(
            src_ref=source,
            dst_ref=full_ref.at[at[0], at[1], at[2]],
            send_sem=sems.at[0, *index],
            recv_sem=sems.at[1, *index],
            device_id=device,
            device_id_type=MESH,
        )

    along_hi = {}
    for step in range(1, hi_count):
        along_hi[step] = hop(
            shard_ref, (hi, lo, core), (flip(hi, step), lo, core), hi_sems, step - 1
        )
        along_hi[step].start()
    send_rows(sizes, rows_ref, got_ref, row_sems.at[0, 0], row_sems.at[1, 0])
    send_rows(sizes, grads_ref, got_grads_ref, row_sems.at[0, 1], row_sems.at[1, 1])

    def across(plane, offset, first):
        at = (flip(hi, plane), flip(lo, offset), core)
        source = shard_ref if first else full_ref.at[at[0], at[1], at[2]]
        copy = hop(source, at, (hi, lo, 1 - core), core_sems, plane, offset)
        copy.start()
        return copy

    started, waits = [], []
    for plane in range(hi_count):
        if plane:
            along_hi[plane].wait_recv()
        started.append(across(plane, 0, plane == 0))
        number = 0
        for bit, offsets in lo_steps(lo_count, plane % 2):
            for offset in offsets:
                at = (flip(hi, plane), flip(lo, offset), core)
                source = shard_ref if plane == 0 and offset == 0 else full_ref.at[at[0], at[1], at[2]]
                copy = hop(source, at, (hi, flip(lo, bit), core), lo_sems, plane, number)
                number += 1
                if offset == 0:
                    copy.start()
                    started.append(copy)
                waits.append((copy, plane, offset, bit))
    arrived = {}
    for copy, plane, offset, bit in waits:
        if offset:
            copy.start()
            started.append(copy)
        copy.wait_recv()
        started.append(across(plane, offset ^ bit, False))
    for copy in started:
        copy.wait_send()
    for step in range(1, hi_count):
        along_hi[step].wait_send()
    for plane in range(hi_count):
        for offset in range(lo_count):
            at = (flip(hi, plane), flip(lo, offset), core)
            hop(
                full_ref.at[at[0], at[1], at[2]], at, (hi, lo, 1 - core), core_sems, plane, offset
            ).wait_recv()
    wait_rows(rows_ref, got_ref, row_sems.at[0, 0], row_sems.at[1, 0])
    wait_rows(grads_ref, got_grads_ref, row_sems.at[0, 1], row_sems.at[1, 1])
    for copy in own:
        copy.wait()


def opening(sizes, rows, grads, shard):
    hi_count, lo_count, _ = sizes
    anywhere = pl.BlockSpec(memory_space=pl.ANY)
    return pl.pallas_call(
        functools.partial(opening_kernel, sizes),
        out_shape=(
            jax.ShapeDtypeStruct(rows.shape, rows.dtype),
            jax.ShapeDtypeStruct(grads.shape, grads.dtype),
            jax.ShapeDtypeStruct(sizes + shard.shape, shard.dtype),
        ),
        in_specs=[anywhere] * 3,
        out_specs=(anywhere, anywhere, anywhere),
        scratch_shapes=[
            pltpu.SemaphoreType.DMA((3,)),
            pltpu.SemaphoreType.DMA((2, 2)),
            pltpu.SemaphoreType.DMA((2, hi_count)),
            pltpu.SemaphoreType.DMA((2, hi_count, lo_count)),
            pltpu.SemaphoreType.DMA((2, hi_count, lo_count)),
        ],
        compiler_params=pltpu.CompilerParams(collective_id=0, has_side_effects=True),
        name="opening",
    )(rows, grads, shard)


def add_blocks(target, first, second):
    rows = target.shape[0]
    tile = 16 if rows % 16 == 0 else rows

    def one(index, carry):
        at = pl.ds(index * tile, tile)
        target[at, :] = (
            first[at, :].astype(jnp.float32) + second[at, :].astype(jnp.float32)
        ).astype(target.dtype)
        return carry

    lax.fori_loop(0, rows // tile, one, 0)


def closing_kernel(
    sizes, out_ref, grad_ref, parts_ref, got_out, got_grad, sum_ref,
    from_core, from_lo, from_hi, held, own_sem, row_sems, hi_sems, lo_sems, core_sems
):
    hi_count, lo_count, _ = sizes
    hi, lo, core = place()
    me = (hi * lo_count + lo) * 2 + core
    own = [
        pltpu.make_async_copy(out_ref.at[me], got_out.at[me], own_sem.at[0]),
        pltpu.make_async_copy(grad_ref.at[me], got_grad.at[me], own_sem.at[1]),
    ]
    for copy in own:
        copy.start()
    greet_all(sizes)

    def hop(source, target, device, sems, *index):
        return pltpu.make_async_remote_copy(
            src_ref=source,
            dst_ref=target,
            send_sem=sems.at[0, *index],
            recv_sem=sems.at[1, *index],
            device_id=device,
            device_id_type=MESH,
        )

    planes = [plane for plane in range(1, hi_count)] + [0]
    across = {}
    for plane in planes:
        for offset in reversed(range(lo_count)):
            across[plane, offset] = hop(
                parts_ref.at[flip(hi, plane), flip(lo, offset), 1 - core],
                from_core.at[plane, offset],
                (hi, lo, 1 - core),
                core_sems,
                plane,
                offset,
            )
            across[plane, offset].start()
    send_rows(sizes, grad_ref, got_grad, row_sems.at[0, 0], row_sems.at[1, 0])
    send_rows(sizes, out_ref, got_out, row_sems.at[0, 1], row_sems.at[1, 1])
    started = []
    plans = {plane: lo_steps(lo_count, plane % 2)[::-1] for plane in planes}
    moves = {}
    for depth in range(len(plans[0])):
        for plane in planes:
            bit, kept = plans[plane][depth]
            base = lo_count - 2 * len(kept)
            if depth == 0:
                for offset in [keep ^ bit for keep in kept] + kept:
                    across[plane, offset].wait_recv()
                    add_blocks(
                        held.at[plane, offset],
                        parts_ref.at[flip(hi, plane), flip(lo, offset), core],
                        from_core.at[plane, offset],
                    )
            else:
                before = plans[plane][depth - 1]
                for number, offset in enumerate(before[1]):
                    copy, spot = moves[plane, depth - 1, offset]
                    copy.wait_recv()
                    add_blocks(held.at[plane, offset], held.at[plane, offset], from_lo.at[plane, spot])
            for number, offset in enumerate(kept):
                spot = base + number
                copy = hop(
                    held.at[plane, offset ^ bit],
                    from_lo.at[plane, spot],
                    (hi, flip(lo, bit), core),
                    lo_sems,
                    plane,
                    spot,
                )
                copy.start()
                started.append(copy)
                moves[plane, depth, offset] = (copy, spot)
    last = len(plans[0]) - 1
    along = {}
    for plane in planes:
        copy, spot = moves[plane, last, 0]
        copy.wait_recv()
        add_blocks(held.at[plane, 0], held.at[plane, 0], from_lo.at[plane, spot])
        if plane:
            along[plane] = hop(
                held.at[plane, 0],
                from_hi.at[plane],
                (flip(hi, plane), lo, core),
                hi_sems,
                plane,
            )
            along[plane].start()
            started.append(along[plane])
    for plane in range(1, hi_count):
        along[plane].wait_recv()
    rows = sum_ref.shape[0]
    tile = 16 if rows % 16 == 0 else rows

    def total(index, carry):
        at = pl.ds(index * tile, tile)
        value = held[0, 0, at, :].astype(jnp.float32)
        for plane in range(1, hi_count):
            value = value + from_hi[plane, at, :].astype(jnp.float32)
        sum_ref[at, :] = value
        return carry

    lax.fori_loop(0, rows // tile, total, 0)
    for copy in started:
        copy.wait_send()
    for copy in across.values():
        copy.wait_send()
    wait_rows(grad_ref, got_grad, row_sems.at[0, 0], row_sems.at[1, 0])
    wait_rows(out_ref, got_out, row_sems.at[0, 1], row_sems.at[1, 1])
    for copy in own:
        copy.wait()


def closing(sizes, out_rows, grad_rows, parts):
    hi_count, lo_count, _ = sizes
    block = parts.shape[3:]
    anywhere = pl.BlockSpec(memory_space=pl.ANY)
    near = pl.BlockSpec(memory_space=pltpu.VMEM)
    return pl.pallas_call(
        functools.partial(closing_kernel, sizes),
        out_shape=(
            jax.ShapeDtypeStruct(out_rows.shape, out_rows.dtype),
            jax.ShapeDtypeStruct(grad_rows.shape, grad_rows.dtype),
            jax.ShapeDtypeStruct(block, jnp.float32),
        ),
        in_specs=[anywhere, anywhere, near],
        out_specs=(anywhere, anywhere, near),
        scratch_shapes=[
            pltpu.VMEM((hi_count, lo_count) + block, jnp.bfloat16),
            pltpu.VMEM((hi_count, lo_count) + block, jnp.bfloat16),
            pltpu.VMEM((hi_count,) + block, jnp.bfloat16),
            pltpu.VMEM((hi_count, lo_count) + block, jnp.bfloat16),
            pltpu.SemaphoreType.DMA((2,)),
            pltpu.SemaphoreType.DMA((2, 2)),
            pltpu.SemaphoreType.DMA((2, hi_count)),
            pltpu.SemaphoreType.DMA((2, hi_count, lo_count)),
            pltpu.SemaphoreType.DMA((2, hi_count, lo_count)),
        ],
        compiler_params=pltpu.CompilerParams(
            collective_id=1, has_side_effects=True, vmem_limit_bytes=60 << 20
        ),
        name="closing",
    )(out_rows, grad_rows, parts)


def dispatch_kernel(weighted, choose_ref, rows_ref, *refs):
    count, capacity, rows = choose_ref.shape[1:]
    chosen = choose_ref[0].reshape(count * capacity, rows)
    width = rows_ref.shape[1]
    tile = 256 if width % 256 == 0 else width
    for start in range(0, width, tile):
        at = pl.ds(start, tile)
        slots = jnp.dot(chosen, rows_ref[:, at], preferred_element_type=jnp.float32)
        slots = slots.reshape(count, capacity, tile)
        if weighted:
            slots = slots * refs[0][:, 0]
        refs[-1][:, 0, :, at] = slots.astype(jnp.bfloat16)


def dispatch(choose, rows, first, stride, slots, weight):
    _, count, capacity, _ = choose.shape
    width = rows.shape[1]
    operands = [choose, rows]
    in_specs = [
        pl.BlockSpec((1, count, capacity, TOK_MB), lambda b: (first + b * stride, 0, 0, 0)),
        pl.BlockSpec((TOK_MB, width), lambda b: (b, 0)),
    ]
    if weight is not None:
        operands.append(weight)
        in_specs.append(pl.BlockSpec((count, 1, capacity, 1), lambda b: (0, first + b * stride, 0, 0)))
    aliases = {}
    if slots is not None:
        aliases = {len(operands): 0}
        operands.append(slots)
        in_specs.append(pl.BlockSpec(memory_space=pl.ANY))
    return pl.pallas_call(
        functools.partial(dispatch_kernel, weight is not None),
        grid=(rows.shape[0] // TOK_MB,),
        out_shape=jax.ShapeDtypeStruct((count, choose.shape[0], capacity, width), jnp.bfloat16),
        in_specs=in_specs,
        out_specs=pl.BlockSpec((count, 1, capacity, width), lambda b: (0, first + b * stride, 0, 0)),
        input_output_aliases=aliases,
        name="dispatch",
    )(*operands)


def middle_kernel(rows_ref, weight_ref, grad_ref, hidden_ref, grad_out_ref):
    half = grad_ref.shape[3]
    for part in range(weight_ref.shape[1]):
        gate_up = jnp.dot(rows_ref[0], weight_ref[0, part], preferred_element_type=jnp.float32)
        gate, up = gate_up[:, :half], gate_up[:, half:]
        sigmoid_gate = jax.nn.sigmoid(gate)
        active = gate * sigmoid_gate
        grad_hidden = grad_ref[0, part].astype(jnp.float32)
        hidden_ref[0, part] = (active * up).astype(jnp.bfloat16)
        slope = sigmoid_gate * (1.0 + gate * (1.0 - sigmoid_gate))
        grad_out_ref[0, part, :, :half] = (grad_hidden * up * slope).astype(jnp.bfloat16)
        grad_out_ref[0, part, :, half:] = (grad_hidden * active).astype(jnp.bfloat16)


def middle(expert_rows, weights_in, grad_hidden):
    count, row_count, width = expert_rows.shape
    parts, both = weights_in.shape[1], weights_in.shape[3]
    tile = 512 if row_count % 512 == 0 else row_count
    return pl.pallas_call(
        middle_kernel,
        grid=(count, row_count // tile),
        out_shape=(
            jax.ShapeDtypeStruct((count, parts, row_count, both // 2), jnp.bfloat16),
            jax.ShapeDtypeStruct((count, parts, row_count, both), jnp.bfloat16),
        ),
        in_specs=[
            pl.BlockSpec((1, tile, width), lambda e, t: (e, t, 0)),
            pl.BlockSpec((1, parts, width, both), lambda e, t: (e, 0, 0, 0)),
            pl.BlockSpec((1, parts, tile, both // 2), lambda e, t: (e, 0, t, 0)),
        ],
        out_specs=(
            pl.BlockSpec((1, parts, tile, both // 2), lambda e, t: (e, 0, t, 0)),
            pl.BlockSpec((1, parts, tile, both), lambda e, t: (e, 0, t, 0)),
        ),
        name="middle",
    )(expert_rows, weights_in, grad_hidden)


def shards(
    tokens,
    cotangent,
    permutation,
    lengths,
    expert_ids,
    gate_weights,
    attn_gain,
    qkv_weight,
    out_weight,
    ffn_gain,
    expert_in,
    expert_out,
):
    device_count = lax.axis_size(ALL)
    hi_count = lax.axis_size("hi")
    lo_count = lax.axis_size("lo")
    tok_dev = permutation.shape[0]
    model_width = tokens.shape[1]
    peer_rows = tok_dev // device_count
    positions = jnp.arange(tok_dev, dtype=jnp.int32)
    expert_count = expert_in.shape[2] * device_count // FF_E
    capacity = TOK_MB * TOPK // expert_count
    source = permutation // tok_dev
    local_row = permutation % tok_dev
    from_source = (source[:, None] == jnp.arange(device_count, dtype=jnp.int32)[None, :]).astype(
        jnp.int32
    )
    earlier = jnp.cumsum(from_source, axis=0, dtype=jnp.int32) - from_source
    arrival = source * peer_rows + jnp.sum(earlier * from_source, axis=1, dtype=jnp.int32)
    arrival_match = arrival[:, None] == positions[None, :]
    wanted = jnp.sum(jnp.where(arrival_match, local_row[:, None], 0), axis=0, dtype=jnp.int32)
    by_arrival = jnp.sum(jnp.where(arrival_match, positions[:, None], 0), axis=0, dtype=jnp.int32)
    def swap(block, step):
        return lax.ppermute(block, "lo", [(i, i ^ step) for i in range(lo_count)])

    def spread(block):
        if lo_count != 4:
            return [[block]] + [[swap(block, step)] for step in range(1, lo_count)]
        half = block.shape[0] // 2
        one, two = swap(block, 1), swap(block, 2)
        return [[block], [one], [two], [swap(one[:half], 2), swap(two[half:], 1)]]

    if lo_count == 4:
        order = [(0, 0), (0, 1), (1, 0), (3, 0), (2, 1), (3, 1), (1, 1), (2, 0)]
    else:
        order = [(step, batch) for step in range(lo_count) for batch in range(MB)]
    routing = jnp.concatenate([expert_ids.astype(jnp.float32), gate_weights], axis=1)
    routing_all = [routing] + [swap(routing, step) for step in range(1, lo_count)]
    routing_all = jnp.stack(
        [routing_all[step][batch * TOK_MB : (batch + 1) * TOK_MB] for step, batch in order]
    )
    asked_rows = lax.all_to_all(
        wanted.reshape(device_count, peer_rows),
        ALL,
        split_axis=0,
        concat_axis=0,
        tiled=True,
    ).reshape(tok_dev)
    asked_rows, routing_all = lax.optimization_barrier((asked_rows, routing_all))
    asked_match = asked_rows[:, None] == positions[None, :]
    by_asked = jnp.sum(jnp.where(asked_match, positions[:, None], 0), axis=0, dtype=jnp.int32)
    sizes = (hi_count, lo_count, 2)
    shard_rows = qkv_weight.shape[0]
    qkv_cols = qkv_weight.shape[1]
    weight_shard = jnp.concatenate(
        [
            qkv_weight,
            out_weight,
            attn_gain[:, None],
            ffn_gain[:, None],
            jnp.zeros((shard_rows, 126), jnp.bfloat16),
        ],
        axis=1,
    )
    asked_tokens = pick(tokens, asked_rows).reshape(device_count, peer_rows, model_width)
    asked_grads = pick(cotangent, asked_rows).reshape(
        device_count, peer_rows, model_width
    )
    got_rows, got_grad, packed = opening(sizes, asked_tokens, asked_grads, weight_shard)
    got_rows, packed, expert_in = lax.optimization_barrier((got_rows, packed, expert_in))
    packed = packed.reshape(model_width, -1)
    grad_bf = pick(got_grad.reshape(tok_dev, model_width), arrival)
    got_rows = hold(got_rows, grad_bf)
    grad_blocks = spread(grad_bf)
    rows_in = pick(got_rows.reshape(tok_dev, model_width), arrival).astype(jnp.float32)
    qkv_full = packed[:, :qkv_cols]
    out_full = packed[:, qkv_cols : qkv_cols + model_width]
    gain_pair = packed[:, qkv_cols + model_width :].astype(jnp.float32)
    gain_one = gain_pair[:, 0]
    gain_two = gain_pair[:, 1]
    shard_cols = expert_in.shape[2]
    weights_in = lax.all_gather(
        expert_in.reshape(model_width, 2 * shard_cols), ("hi", "core"), axis=0
    ).reshape(hi_count, 2, model_width, 2 * shard_cols)
    weights_out = lax.all_gather(expert_out, ("hi", "core"), axis=0).reshape(
        hi_count, 2, shard_cols, model_width
    )
    segment, position = layout_rows(lengths)
    scale_one = lax.rsqrt(jnp.mean(rows_in * rows_in, axis=1, keepdims=True) + epsilon)
    normed = (rows_in * scale_one * gain_one).astype(jnp.bfloat16)
    projected = jnp.dot(normed, qkv_full, preferred_element_type=jnp.float32)
    cosine_table, sine_table = rope_tables(position)
    if lo_count == 4:
        segment = hold(segment, grad_blocks[1][0], grad_blocks[2][0])
    sides = (
        jnp.tile(cosine_table, (1, 4)),
        jnp.concatenate([-sine_table, sine_table] * 2, axis=1),
        segment.reshape(-1, TOK_MB, 1),
        segment.reshape(-1, 1, TOK_MB),
    )
    queries, key_rows, value_rows, mixed_rows = attend(projected, sides)
    attended = jnp.dot(mixed_rows, out_full, preferred_element_type=jnp.float32)
    residual = rows_in + attended
    scale_two = lax.rsqrt(jnp.mean(residual * residual, axis=1, keepdims=True) + epsilon)
    normed_two = (residual * scale_two * gain_two).astype(jnp.bfloat16)
    grad_output = grad_bf.astype(jnp.float32)
    home = lax.axis_index("lo")
    if lo_count == 4:
        normed_two = hold(normed_two, *grad_blocks[3])
    row_blocks = spread(normed_two)
    normed_two, grad_blocks = lax.optimization_barrier((normed_two, grad_blocks))
    choose, slot_gate = slot_tables(
        routing_all[..., :TOPK].astype(jnp.int32),
        routing_all[..., TOPK:],
        home + lo_count * jnp.arange(hi_count, dtype=jnp.int32),
        capacity,
    )
    slot_weight = jnp.transpose(slot_gate, (1, 0, 2))[..., None]
    place_of = {name: number for number, name in enumerate(order)}

    def fill(blocks, slots, weight):
        for step, pieces in blocks:
            batch = 0
            for piece in pieces:
                first = place_of[step, batch]
                stride = place_of[step, MB - 1] - place_of[step, 0]
                slots = dispatch(choose, piece, first, stride, slots, weight)
                batch += piece.shape[0] // TOK_MB
        return slots

    grad_expert = fill(list(enumerate(grad_blocks)), None, slot_weight)
    grad_expert = grad_expert.reshape(hi_count, -1, model_width)
    grad_hidden = jnp.einsum(
        "erd,ekfd->ekrf", grad_expert, weights_out, preferred_element_type=jnp.float32
    ).astype(jnp.bfloat16)
    expert_rows = fill([(0, [normed_two])], None, None)
    grad_hidden, expert_rows, others = lax.optimization_barrier(
        (grad_hidden, expert_rows, row_blocks[1:])
    )
    expert_rows = fill(list(enumerate(others, 1)), expert_rows, None)
    expert_rows = expert_rows.reshape(hi_count, -1, model_width)
    hidden, grad_gate_up = middle(expert_rows, weights_in, grad_hidden)
    grad_weights_out = jnp.einsum(
        "ekrf,erd->ekfd", hidden, grad_expert, preferred_element_type=jnp.float32
    ).astype(jnp.bfloat16)
    grad_weights_out, grad_gate_up = lax.optimization_barrier((grad_weights_out, grad_gate_up))
    shard_out = lax.psum_scatter(
        grad_weights_out.reshape(hi_count * 2 * shard_cols, model_width),
        ("hi", "core"),
        scatter_dimension=0,
        tiled=True,
    ).astype(jnp.float32)
    grad_expert_rows = jnp.einsum(
        "ekrf,ekdf->erd", grad_gate_up, weights_in, preferred_element_type=jnp.float32
    ).astype(jnp.bfloat16)

    def split_back(slot_values):
        return jnp.einsum(
            "becr,ebcd->brd",
            choose,
            slot_values.reshape(hi_count, lo_count * MB, capacity, model_width),
            preferred_element_type=jnp.float32,
        ).astype(jnp.bfloat16)

    def wide(value):
        return value.astype(jnp.float32)

    def bring_back(parts):
        if lo_count != 4:
            parts = parts.reshape(lo_count, tok_dev, model_width)
            return [parts[0]] + [swap(parts[step], step) for step in range(1, lo_count)]
        one = swap(parts[2:4], 1)
        two = swap(parts[4:6], 2)
        for_one = (wide(parts[6]) + wide(two[1])).astype(jnp.bfloat16)
        for_two = (wide(parts[7]) + wide(one[1])).astype(jnp.bfloat16)
        return [parts[:2], one, two, swap(for_two, 2), swap(for_one, 1)]

    def total_of(terms):
        if lo_count != 4:
            total = wide(terms[0])
            for term in terms[1:]:
                total = total + wide(term)
            return total
        own, one, two, last_two, last_one = terms
        return jnp.concatenate(
            [
                wide(own[0]) + wide(one[0]) + wide(last_two),
                wide(own[1]) + wide(two[0]) + wide(last_one),
            ],
            axis=0,
        )

    back = split_back(grad_expert_rows)
    back_parts = bring_back(back)
    produced = (
        jnp.einsum("ekrf,ekfd->erd", hidden, weights_out, preferred_element_type=jnp.float32)
        * slot_weight.reshape(hi_count, -1, 1)
    ).astype(jnp.bfloat16)
    ahead = split_back(produced)
    grad_gate_up = hold(grad_gate_up, ahead, *back_parts[1:3])
    grad_weights_in = jnp.einsum(
        "ekrf,erd->ekfd", grad_gate_up, expert_rows, preferred_element_type=jnp.float32
    ).astype(jnp.bfloat16)
    shard_in = lax.psum_scatter(
        grad_weights_in.reshape(hi_count * 2 * 2 * shard_cols, model_width),
        ("hi", "core"),
        scatter_dimension=0,
        tiled=True,
    )
    shard_in = shard_in.T.astype(jnp.float32).reshape(model_width, 2, shard_cols)
    ahead, back_parts = lax.optimization_barrier((ahead, back_parts))
    ahead_parts = bring_back(ahead)
    grad_normed_two = total_of(back_parts)
    grad_gain_two, grad_from_norm = norm_back(residual, scale_two, gain_two, grad_normed_two)
    grad_residual = grad_output + grad_from_norm
    grad_attended = grad_residual.astype(jnp.bfloat16)
    grad_out_weight = jnp.einsum(
        "nq,nd->qd", mixed_rows, grad_attended, preferred_element_type=jnp.float32
    )
    grad_mixed = jnp.einsum(
        "nd,qd->nq", grad_attended, out_full, preferred_element_type=jnp.float32
    ).astype(jnp.bfloat16)
    grad_projected = jnp.concatenate(
        attend_back(queries, key_rows, value_rows, grad_mixed, sides), axis=1
    )
    if lo_count == 4:
        normed = hold(normed, *ahead_parts[1:3])
    grad_qkv_weight = jnp.einsum(
        "nd,nc->dc", normed, grad_projected, preferred_element_type=jnp.float32
    )
    grad_normed = jnp.einsum(
        "nc,dc->nd", grad_projected, qkv_full, preferred_element_type=jnp.float32
    )
    grad_gain_one, grad_from_first = norm_back(rows_in, scale_one, gain_one, grad_normed)
    grad_input = (grad_residual + grad_from_first).astype(jnp.bfloat16)
    gains = jnp.pad(jnp.stack([grad_gain_one, grad_gain_two], axis=1), ((0, 0), (0, 126)))
    parts = jnp.concatenate(
        [
            grad_qkv_weight.astype(jnp.bfloat16),
            grad_out_weight.astype(jnp.bfloat16),
            gains.astype(jnp.bfloat16),
        ],
        axis=1,
    ).reshape(sizes + (shard_rows, -1))
    parts, shard_out, ahead_parts = lax.optimization_barrier((parts, shard_out, ahead_parts))
    output_rows = (residual + total_of(ahead_parts)).astype(jnp.bfloat16)
    home_out, home_grad, sums = closing(
        sizes,
        pick(output_rows, by_arrival).reshape(device_count, peer_rows, model_width),
        pick(grad_input, by_arrival).reshape(device_count, peer_rows, model_width),
        parts,
    )
    shard_qkv = sums[:, :qkv_cols]
    shard_attn_out = sums[:, qkv_cols : qkv_cols + model_width]
    shard_gain_one = sums[:, qkv_cols + model_width]
    shard_gain_two = sums[:, qkv_cols + model_width + 1]
    output = pick(home_out.reshape(tok_dev, model_width), by_asked)
    input_grad = pick(home_grad.reshape(tok_dev, model_width), by_asked)
    return (
        output,
        input_grad,
        shard_gain_one,
        shard_qkv,
        shard_attn_out,
        shard_gain_two,
        shard_in,
        shard_out,
    )


def solution(mesh):
    dp_count = mesh.shape["dp"]
    hi_count = 4 if dp_count % 4 == 0 else 1
    split = jax.sharding.Mesh(
        mesh.devices.reshape(hi_count, dp_count // hi_count, mesh.shape["expert"]), ALL
    )
    rows, columns = P(ALL, None), P(None, None, ALL)
    return jax.shard_map(
        shards,
        mesh=split,
        in_specs=(rows, rows, P(ALL), rows, rows, rows, P(ALL), rows, rows, P(ALL), columns, rows),
        out_specs=(rows, rows, P(ALL), rows, rows, P(ALL), columns, rows),
        check_vma=False,
    )
```

```python
import functools

import jax
import jax.numpy as jnp
from jax import lax
from jax.experimental import pallas as pl
from jax.experimental.pallas import tpu as pltpu
from jax.sharding import PartitionSpec as P

HEADS = 24
KV_HEADS = 8
HEAD = 64
FF_E = 512
TOPK = 8
MB = 2
SEQS = 4
TOK_MB = 256
ALL = ("hi", "lo", "core")


epsilon = 1e-05
theta_base = 10000.0


def layout_rows(length_rows):
    seq_ends = jnp.cumsum(length_rows, axis=1, dtype=jnp.int32)
    starts = seq_ends - length_rows
    within = jnp.arange(TOK_MB, dtype=jnp.int32)
    segment = jnp.sum(
        (within[None, :, None] >= seq_ends[:, None, :]).astype(jnp.int32), axis=2, dtype=jnp.int32
    )
    chosen = segment[:, :, None] == jnp.arange(SEQS, dtype=jnp.int32)[None, None, :]
    seq_begin = jnp.sum(jnp.where(chosen, starts[:, None, :], 0), axis=2, dtype=jnp.int32)
    position = within[None, :] - seq_begin
    segment = segment + jnp.arange(MB, dtype=jnp.int32)[:, None] * SEQS
    return (segment.reshape(-1), position.reshape(-1))


def rope_tables(position):
    half_width = HEAD // 2
    frequency = theta_base ** (-(2.0 / HEAD) * jnp.arange(half_width, dtype=jnp.float32))
    angles = position.astype(jnp.float32)[:, None] * frequency[None, :]
    return (jnp.cos(angles), jnp.sin(angles))


def slot_tables(ids, gates, experts, capacity):
    count = experts.shape[0]
    named = ids[..., None] == experts
    picked = jnp.any(named, axis=2)
    weight = jnp.sum(jnp.where(named, gates[..., None], 0.0), axis=2)
    rows = jnp.arange(TOK_MB, dtype=jnp.int32)
    below = (rows[:, None] > rows[None, :]).astype(jnp.bfloat16)
    shaped = picked.reshape(-1, TOK_MB, count)
    slot = jnp.einsum(
        "rq,bqe->ber", below, shaped.astype(jnp.bfloat16), preferred_element_type=jnp.float32
    ).astype(jnp.int32)
    kept = jnp.transpose(shaped, (0, 2, 1))
    hit = kept[:, :, None, :] & (
        slot[:, :, None, :] == jnp.arange(capacity, dtype=jnp.int32)[None, None, :, None]
    )
    weight = jnp.transpose(weight.reshape(-1, TOK_MB, count), (0, 2, 1))
    slot_gate = jnp.sum(jnp.where(hit, weight[:, :, None, :], 0.0), axis=3)
    return hit.astype(jnp.bfloat16), slot_gate


def partner(values):
    half = HEAD // 2
    lane = lax.broadcasted_iota(jnp.int32, values.shape, 1) % HEAD
    return jnp.where(
        lane < half, pltpu.roll(values, 2 * HEAD - half, 1), pltpu.roll(values, half, 1)
    )


def allowed_keys(seg_col_ref, seg_row_ref, first, count):
    keys = first + count
    rows = lax.broadcasted_iota(jnp.int32, (count, keys), 0) + first
    columns = lax.broadcasted_iota(jnp.int32, (count, keys), 1)
    same = seg_col_ref[0, first : first + count, :] == seg_row_ref[0, :, :keys]
    return same & (rows >= columns)


def stacked(ref, rows, one, group):
    starts = range(one * group * HEAD, (one + 1) * group * HEAD, HEAD)
    return jnp.concatenate([ref[rows, start : start + HEAD] for start in starts], axis=0)


def unstack(ref, rows, one, values):
    count = rows.stop - rows.start
    group = values.shape[0] // count
    for head in range(group):
        start = (one * group + head) * HEAD
        ref[rows, start : start + HEAD] = values[head * count : (head + 1) * count]


def soft_weights(queries, keys, allowed):
    scores = lax.dot_general(
        queries, keys, (((1,), (1,)), ((), ())), preferred_element_type=jnp.float32
    )
    scores = jnp.where(allowed, scores, -1e30)
    weights = jnp.exp(scores - jnp.max(scores, axis=-1, keepdims=True))
    return weights * (1.0 / jnp.sum(weights, axis=-1, keepdims=True))


def attend_kernel(
    q_ref, k_ref, v_ref, cos_ref, sin_ref, seg_col_ref, seg_row_ref,
    q_out, k_out, v_out, mixed_ref
):
    cosine, sine = cos_ref[...], sin_ref[...]
    pair = 2 * HEAD
    group = HEADS // KV_HEADS
    for start in range(0, q_ref.shape[1], pair):
        values = q_ref[:, start : start + pair]
        turned = (values * cosine + partner(values) * sine).astype(jnp.bfloat16)
        q_out[:, start : start + pair] = turned * jnp.bfloat16(HEAD**-0.5)
    values = k_ref[...]
    k_out[...] = (values * cosine + partner(values) * sine).astype(jnp.bfloat16)
    v_out[...] = v_ref[...].astype(jnp.bfloat16)
    block = TOK_MB // 2
    for first in range(0, TOK_MB, block):
        rows, keys = slice(first, first + block), slice(0, first + block)
        allowed = allowed_keys(seg_col_ref, seg_row_ref, first, block)
        allowed = jnp.concatenate([allowed] * group, axis=0)
        for one in range(2):
            lanes = slice(one * HEAD, (one + 1) * HEAD)
            weights = soft_weights(
                stacked(q_out, rows, one, group), k_out[keys, lanes], allowed
            ).astype(jnp.bfloat16)
            mixed = jnp.dot(weights, v_out[keys, lanes], preferred_element_type=jnp.float32)
            unstack(mixed_ref, rows, one, mixed.astype(jnp.bfloat16))


def attend_back_kernel(
    q_ref, k_ref, v_ref, grad_ref, cos_ref, sin_ref, seg_col_ref, seg_row_ref,
    dq_ref, dk_ref, dv_ref, dq_sum, dk_sum, dv_sum
):
    cosine, sine = cos_ref[...], sin_ref[...]
    pair = 2 * HEAD
    group = HEADS // KV_HEADS
    block = TOK_MB // 2
    over_rows = (((0,), (0,)), ((), ()))
    over_lanes = (((1,), (1,)), ((), ()))
    for first in range(TOK_MB - block, -1, -block):
        rows, keys = slice(first, first + block), slice(0, first + block)
        allowed = allowed_keys(seg_col_ref, seg_row_ref, first, block)
        allowed = jnp.concatenate([allowed] * group, axis=0)
        for one in range(2):
            lanes = slice(one * HEAD, (one + 1) * HEAD)
            key_rows, value_rows = k_ref[keys, lanes], v_ref[keys, lanes]
            queries = stacked(q_ref, rows, one, group)
            grads = stacked(grad_ref, rows, one, group)
            weights = soft_weights(queries, key_rows, allowed)
            grad_weights = lax.dot_general(
                grads, value_rows, over_lanes, preferred_element_type=jnp.float32
            )
            grad_values = lax.dot_general(
                weights.astype(jnp.bfloat16), grads, over_rows, preferred_element_type=jnp.float32
            )
            inner = jnp.sum(grad_weights * weights, axis=-1, keepdims=True)
            grad_scores = (weights * (grad_weights - inner)).astype(jnp.bfloat16)
            grad_queries = jnp.dot(grad_scores, key_rows, preferred_element_type=jnp.float32)
            unstack(dq_sum, rows, one, grad_queries * HEAD ** (-0.5))
            grad_keys = lax.dot_general(
                grad_scores, queries, over_rows, preferred_element_type=jnp.float32
            )
            if first == TOK_MB - block:
                dk_sum[keys, lanes] = grad_keys
                dv_sum[keys, lanes] = grad_values
            else:
                dk_sum[keys, lanes] = dk_sum[keys, lanes] + grad_keys
                dv_sum[keys, lanes] = dv_sum[keys, lanes] + grad_values
    for start in range(0, q_ref.shape[1], pair):
        values = dq_sum[:, start : start + pair]
        dq_ref[:, start : start + pair] = (
            values * cosine - partner(values) * sine
        ).astype(jnp.bfloat16)
    values = dk_sum[...]
    dk_ref[...] = (values * cosine - partner(values) * sine).astype(jnp.bfloat16)
    dv_ref[...] = dv_sum[...].astype(jnp.bfloat16)


def attend_blocks(row_count):
    pair = 2 * HEAD
    wide = pair * (HEADS // KV_HEADS)
    narrow = pl.BlockSpec((TOK_MB, pair), lambda b, g: (b, g))
    broad = pl.BlockSpec((TOK_MB, wide), lambda b, g: (b, g))
    sides = [
        pl.BlockSpec((TOK_MB, pair), lambda b, g: (b, 0)),
        pl.BlockSpec((TOK_MB, pair), lambda b, g: (b, 0)),
        pl.BlockSpec((1, TOK_MB, 1), lambda b, g: (b, 0, 0)),
        pl.BlockSpec((1, 1, TOK_MB), lambda b, g: (b, 0, 0)),
    ]
    return (row_count // TOK_MB, KV_HEADS // 2), narrow, broad, sides


def attend(projected, sides):
    row_count = projected.shape[0]
    grid, narrow, broad, side_specs = attend_blocks(row_count)
    q_dim, kv_dim, pair = HEADS * HEAD, KV_HEADS * HEAD, 2 * HEAD
    key_start, value_start = q_dim // pair, (q_dim + kv_dim) // pair
    q_shape = jax.ShapeDtypeStruct((row_count, q_dim), jnp.bfloat16)
    kv_shape = jax.ShapeDtypeStruct((row_count, kv_dim), jnp.bfloat16)
    return pl.pallas_call(
        attend_kernel,
        grid=grid,
        out_shape=(q_shape, kv_shape, kv_shape, q_shape),
        in_specs=[
            broad,
            pl.BlockSpec((TOK_MB, pair), lambda b, g: (b, key_start + g)),
            pl.BlockSpec((TOK_MB, pair), lambda b, g: (b, value_start + g)),
        ]
        + side_specs,
        out_specs=(broad, narrow, narrow, broad),
        name="attend",
    )(projected, projected, projected, *sides)


def attend_back(queries, key_rows, value_rows, grad_mixed, sides):
    row_count = queries.shape[0]
    grid, narrow, broad, side_specs = attend_blocks(row_count)
    shapes = [jax.ShapeDtypeStruct(x.shape, jnp.bfloat16) for x in (queries, key_rows, value_rows)]
    return pl.pallas_call(
        attend_back_kernel,
        grid=grid,
        out_shape=tuple(shapes),
        in_specs=[broad, narrow, narrow, broad] + side_specs,
        out_specs=(broad, narrow, narrow),
        scratch_shapes=[
            pltpu.VMEM((TOK_MB, 2 * HEAD * (HEADS // KV_HEADS)), jnp.float32),
            pltpu.VMEM((TOK_MB, 2 * HEAD), jnp.float32),
            pltpu.VMEM((TOK_MB, 2 * HEAD), jnp.float32),
        ],
        name="attend_back",
    )(queries, key_rows, value_rows, grad_mixed, *sides)


def pick(rows, index):
    return jnp.take(rows, index, axis=0, mode="clip")


def hold(value, *after):
    anywhere = pl.BlockSpec(memory_space=pl.ANY)
    return pl.pallas_call(
        lambda *refs: None,
        out_shape=jax.ShapeDtypeStruct(value.shape, value.dtype),
        in_specs=[anywhere] * (1 + len(after)),
        out_specs=anywhere,
        input_output_aliases={0: 0},
        name="hold",
    )(value, *after)


def norm_back(values, scale, gain, grad_normed):
    scaled_grad = grad_normed * gain
    grad_gain = jnp.sum(grad_normed * values * scale, axis=0)
    grad_values = scale * scaled_grad - values * scale * scale * scale * jnp.mean(
        scaled_grad * values, axis=1, keepdims=True
    )
    return (grad_gain, grad_values)


MESH = pl.DeviceIdType.MESH


def flip(value, bits):
    bit = 1
    while bit <= bits:
        if bits & bit:
            value = value + bit * (1 - 2 * ((value // bit) % 2))
        bit *= 2
    return value


def place():
    return lax.axis_index("hi"), lax.axis_index("lo"), lax.axis_index("core")


def greet_all(sizes):
    hi_count, lo_count, _ = sizes
    count = hi_count * lo_count * 2
    hi, lo, core = place()
    me = (hi * lo_count + lo) * 2 + core
    barrier = pltpu.get_barrier_semaphore()

    def greet(step, carry):
        peer = (me + step) % count
        pl.semaphore_signal(
            barrier,
            inc=1,
            device_id=(peer // (2 * lo_count), (peer // 2) % lo_count, peer % 2),
            device_id_type=MESH,
        )
        return carry

    lax.fori_loop(1, count, greet, 0)
    pl.semaphore_wait(barrier, count - 1)


def send_rows(sizes, source, target, send_sem, recv_sem):
    hi_count, lo_count, _ = sizes
    count = hi_count * lo_count * 2
    hi, lo, core = place()
    me = (hi * lo_count + lo) * 2 + core

    def one(step, carry):
        peer = (me + step) % count
        pltpu.make_async_remote_copy(
            src_ref=source.at[peer],
            dst_ref=target.at[me],
            send_sem=send_sem,
            recv_sem=recv_sem,
            device_id=(peer // (2 * lo_count), (peer // 2) % lo_count, peer % 2),
            device_id_type=MESH,
        ).start()
        return carry

    lax.fori_loop(1, count, one, 0)


def wait_rows(source, target, send_sem, recv_sem):
    rest = pl.ds(0, source.shape[0] - 1)
    pltpu.make_async_copy(source.at[rest], source.at[rest], send_sem).wait()
    pltpu.make_async_copy(target.at[rest], target.at[rest], recv_sem).wait()


def lo_steps(lo_count, turn):
    bits = []
    bit = 1
    while bit < lo_count:
        bits.append(bit)
        bit *= 2
    if turn:
        bits = bits[::-1]
    held, steps = [0], []
    for bit in bits:
        steps.append((bit, list(held)))
        held = held + [offset ^ bit for offset in held]
    return steps


def opening_kernel(
    sizes, rows_ref, grads_ref, shard_ref, got_ref, got_grads_ref, full_ref,
    own_sem, row_sems, hi_sems, lo_sems, core_sems
):
    hi_count, lo_count, _ = sizes
    hi, lo, core = place()
    me = (hi * lo_count + lo) * 2 + core
    own = [
        pltpu.make_async_copy(shard_ref, full_ref.at[hi, lo, core], own_sem.at[0]),
        pltpu.make_async_copy(rows_ref.at[me], got_ref.at[me], own_sem.at[1]),
        pltpu.make_async_copy(grads_ref.at[me], got_grads_ref.at[me], own_sem.at[2]),
    ]
    for copy in own:
        copy.start()
    greet_all(sizes)

    def hop(source, at, device, sems, *index):
        return pltpu.make_async_remote_copy(
            src_ref=source,
            dst_ref=full_ref.at[at[0], at[1], at[2]],
            send_sem=sems.at[0, *index],
            recv_sem=sems.at[1, *index],
            device_id=device,
            device_id_type=MESH,
        )

    along_hi = {}
    for step in range(1, hi_count):
        along_hi[step] = hop(
            shard_ref, (hi, lo, core), (flip(hi, step), lo, core), hi_sems, step - 1
        )
        along_hi[step].start()
    send_rows(sizes, rows_ref, got_ref, row_sems.at[0, 0], row_sems.at[1, 0])
    send_rows(sizes, grads_ref, got_grads_ref, row_sems.at[0, 1], row_sems.at[1, 1])

    def across(plane, offset, first):
        at = (flip(hi, plane), flip(lo, offset), core)
        source = shard_ref if first else full_ref.at[at[0], at[1], at[2]]
        copy = hop(source, at, (hi, lo, 1 - core), core_sems, plane, offset)
        copy.start()
        return copy

    started, waits = [], []
    for plane in range(hi_count):
        if plane:
            along_hi[plane].wait_recv()
        started.append(across(plane, 0, plane == 0))
        number = 0
        for bit, offsets in lo_steps(lo_count, plane % 2):
            for offset in offsets:
                at = (flip(hi, plane), flip(lo, offset), core)
                source = shard_ref if plane == 0 and offset == 0 else full_ref.at[at[0], at[1], at[2]]
                copy = hop(source, at, (hi, flip(lo, bit), core), lo_sems, plane, number)
                number += 1
                if offset == 0:
                    copy.start()
                    started.append(copy)
                waits.append((copy, plane, offset, bit))
    arrived = {}
    for copy, plane, offset, bit in waits:
        if offset:
            copy.start()
            started.append(copy)
        copy.wait_recv()
        started.append(across(plane, offset ^ bit, False))
    for copy in started:
        copy.wait_send()
    for step in range(1, hi_count):
        along_hi[step].wait_send()
    for plane in range(hi_count):
        for offset in range(lo_count):
            at = (flip(hi, plane), flip(lo, offset), core)
            hop(
                full_ref.at[at[0], at[1], at[2]], at, (hi, lo, 1 - core), core_sems, plane, offset
            ).wait_recv()
    wait_rows(rows_ref, got_ref, row_sems.at[0, 0], row_sems.at[1, 0])
    wait_rows(grads_ref, got_grads_ref, row_sems.at[0, 1], row_sems.at[1, 1])
    for copy in own:
        copy.wait()


def opening(sizes, rows, grads, shard):
    hi_count, lo_count, _ = sizes
    anywhere = pl.BlockSpec(memory_space=pl.ANY)
    return pl.pallas_call(
        functools.partial(opening_kernel, sizes),
        out_shape=(
            jax.ShapeDtypeStruct(rows.shape, rows.dtype),
            jax.ShapeDtypeStruct(grads.shape, grads.dtype),
            jax.ShapeDtypeStruct(sizes + shard.shape, shard.dtype),
        ),
        in_specs=[anywhere] * 3,
        out_specs=(anywhere, anywhere, anywhere),
        scratch_shapes=[
            pltpu.SemaphoreType.DMA((3,)),
            pltpu.SemaphoreType.DMA((2, 2)),
            pltpu.SemaphoreType.DMA((2, hi_count)),
            pltpu.SemaphoreType.DMA((2, hi_count, lo_count)),
            pltpu.SemaphoreType.DMA((2, hi_count, lo_count)),
        ],
        compiler_params=pltpu.CompilerParams(collective_id=0, has_side_effects=True),
        name="opening",
    )(rows, grads, shard)


def add_blocks(target, first, second):
    rows = target.shape[0]
    tile = 16 if rows % 16 == 0 else rows

    def one(index, carry):
        at = pl.ds(index * tile, tile)
        target[at, :] = (
            first[at, :].astype(jnp.float32) + second[at, :].astype(jnp.float32)
        ).astype(target.dtype)
        return carry

    lax.fori_loop(0, rows // tile, one, 0)


def closing_kernel(
    sizes, out_ref, grad_ref, parts_ref, got_out, got_grad, sum_ref,
    from_core, from_lo, from_hi, held, own_sem, row_sems, hi_sems, lo_sems, core_sems
):
    hi_count, lo_count, _ = sizes
    hi, lo, core = place()
    me = (hi * lo_count + lo) * 2 + core
    own = [
        pltpu.make_async_copy(out_ref.at[me], got_out.at[me], own_sem.at[0]),
        pltpu.make_async_copy(grad_ref.at[me], got_grad.at[me], own_sem.at[1]),
    ]
    for copy in own:
        copy.start()
    greet_all(sizes)

    def hop(source, target, device, sems, *index):
        return pltpu.make_async_remote_copy(
            src_ref=source,
            dst_ref=target,
            send_sem=sems.at[0, *index],
            recv_sem=sems.at[1, *index],
            device_id=device,
            device_id_type=MESH,
        )

    planes = [plane for plane in range(1, hi_count)] + [0]
    across = {}
    for plane in planes:
        for offset in reversed(range(lo_count)):
            across[plane, offset] = hop(
                parts_ref.at[flip(hi, plane), flip(lo, offset), 1 - core],
                from_core.at[plane, offset],
                (hi, lo, 1 - core),
                core_sems,
                plane,
                offset,
            )
            across[plane, offset].start()
    send_rows(sizes, grad_ref, got_grad, row_sems.at[0, 0], row_sems.at[1, 0])
    send_rows(sizes, out_ref, got_out, row_sems.at[0, 1], row_sems.at[1, 1])
    started = []
    plans = {plane: lo_steps(lo_count, plane % 2)[::-1] for plane in planes}
    moves = {}
    for depth in range(len(plans[0])):
        for plane in planes:
            bit, kept = plans[plane][depth]
            base = lo_count - 2 * len(kept)
            if depth == 0:
                for offset in [keep ^ bit for keep in kept] + kept:
                    across[plane, offset].wait_recv()
                    add_blocks(
                        held.at[plane, offset],
                        parts_ref.at[flip(hi, plane), flip(lo, offset), core],
                        from_core.at[plane, offset],
                    )
            else:
                before = plans[plane][depth - 1]
                for number, offset in enumerate(before[1]):
                    copy, spot = moves[plane, depth - 1, offset]
                    copy.wait_recv()
                    add_blocks(held.at[plane, offset], held.at[plane, offset], from_lo.at[plane, spot])
            for number, offset in enumerate(kept):
                spot = base + number
                copy = hop(
                    held.at[plane, offset ^ bit],
                    from_lo.at[plane, spot],
                    (hi, flip(lo, bit), core),
                    lo_sems,
                    plane,
                    spot,
                )
                copy.start()
                started.append(copy)
                moves[plane, depth, offset] = (copy, spot)
    last = len(plans[0]) - 1
    along = {}
    for plane in planes:
        copy, spot = moves[plane, last, 0]
        copy.wait_recv()
        add_blocks(held.at[plane, 0], held.at[plane, 0], from_lo.at[plane, spot])
        if plane:
            along[plane] = hop(
                held.at[plane, 0],
                from_hi.at[plane],
                (flip(hi, plane), lo, core),
                hi_sems,
                plane,
            )
            along[plane].start()
            started.append(along[plane])
    for plane in range(1, hi_count):
        along[plane].wait_recv()
    rows = sum_ref.shape[0]
    tile = 16 if rows % 16 == 0 else rows

    def total(index, carry):
        at = pl.ds(index * tile, tile)
        value = held[0, 0, at, :].astype(jnp.float32)
        for plane in range(1, hi_count):
            value = value + from_hi[plane, at, :].astype(jnp.float32)
        sum_ref[at, :] = value
        return carry

    lax.fori_loop(0, rows // tile, total, 0)
    for copy in started:
        copy.wait_send()
    for copy in across.values():
        copy.wait_send()
    wait_rows(grad_ref, got_grad, row_sems.at[0, 0], row_sems.at[1, 0])
    wait_rows(out_ref, got_out, row_sems.at[0, 1], row_sems.at[1, 1])
    for copy in own:
        copy.wait()


def closing(sizes, out_rows, grad_rows, parts):
    hi_count, lo_count, _ = sizes
    block = parts.shape[3:]
    anywhere = pl.BlockSpec(memory_space=pl.ANY)
    near = pl.BlockSpec(memory_space=pltpu.VMEM)
    return pl.pallas_call(
        functools.partial(closing_kernel, sizes),
        out_shape=(
            jax.ShapeDtypeStruct(out_rows.shape, out_rows.dtype),
            jax.ShapeDtypeStruct(grad_rows.shape, grad_rows.dtype),
            jax.ShapeDtypeStruct(block, jnp.float32),
        ),
        in_specs=[anywhere, anywhere, near],
        out_specs=(anywhere, anywhere, near),
        scratch_shapes=[
            pltpu.VMEM((hi_count, lo_count) + block, jnp.bfloat16),
            pltpu.VMEM((hi_count, lo_count) + block, jnp.bfloat16),
            pltpu.VMEM((hi_count,) + block, jnp.bfloat16),
            pltpu.VMEM((hi_count, lo_count) + block, jnp.bfloat16),
            pltpu.SemaphoreType.DMA((2,)),
            pltpu.SemaphoreType.DMA((2, 2)),
            pltpu.SemaphoreType.DMA((2, hi_count)),
            pltpu.SemaphoreType.DMA((2, hi_count, lo_count)),
            pltpu.SemaphoreType.DMA((2, hi_count, lo_count)),
        ],
        compiler_params=pltpu.CompilerParams(
            collective_id=1, has_side_effects=True, vmem_limit_bytes=60 << 20
        ),
        name="closing",
    )(out_rows, grad_rows, parts)


def dispatch_kernel(weighted, choose_ref, rows_ref, *refs):
    count, capacity, rows = choose_ref.shape[1:]
    chosen = choose_ref[0].reshape(count * capacity, rows)
    width = rows_ref.shape[1]
    tile = 256 if width % 256 == 0 else width
    for start in range(0, width, tile):
        at = pl.ds(start, tile)
        slots = jnp.dot(chosen, rows_ref[:, at], preferred_element_type=jnp.float32)
        slots = slots.reshape(count, capacity, tile)
        if weighted:
            slots = slots * refs[0][:, 0]
        refs[-1][:, 0, :, at] = slots.astype(jnp.bfloat16)


def dispatch(choose, rows, first, stride, slots, weight):
    _, count, capacity, _ = choose.shape
    width = rows.shape[1]
    operands = [choose, rows]
    in_specs = [
        pl.BlockSpec((1, count, capacity, TOK_MB), lambda b: (first + b * stride, 0, 0, 0)),
        pl.BlockSpec((TOK_MB, width), lambda b: (b, 0)),
    ]
    if weight is not None:
        operands.append(weight)
        in_specs.append(pl.BlockSpec((count, 1, capacity, 1), lambda b: (0, first + b * stride, 0, 0)))
    aliases = {}
    if slots is not None:
        aliases = {len(operands): 0}
        operands.append(slots)
        in_specs.append(pl.BlockSpec(memory_space=pl.ANY))
    return pl.pallas_call(
        functools.partial(dispatch_kernel, weight is not None),
        grid=(rows.shape[0] // TOK_MB,),
        out_shape=jax.ShapeDtypeStruct((count, choose.shape[0], capacity, width), jnp.bfloat16),
        in_specs=in_specs,
        out_specs=pl.BlockSpec((count, 1, capacity, width), lambda b: (0, first + b * stride, 0, 0)),
        input_output_aliases=aliases,
        name="dispatch",
    )(*operands)


def middle_kernel(rows_ref, weight_ref, grad_ref, hidden_ref, grad_out_ref):
    half = grad_ref.shape[3]
    for part in range(weight_ref.shape[1]):
        gate_up = jnp.dot(rows_ref[0], weight_ref[0, part], preferred_element_type=jnp.float32)
        gate, up = gate_up[:, :half], gate_up[:, half:]
        sigmoid_gate = jax.nn.sigmoid(gate)
        active = gate * sigmoid_gate
        grad_hidden = grad_ref[0, part].astype(jnp.float32)
        hidden_ref[0, part] = (active * up).astype(jnp.bfloat16)
        slope = sigmoid_gate * (1.0 + gate * (1.0 - sigmoid_gate))
        grad_out_ref[0, part, :, :half] = (grad_hidden * up * slope).astype(jnp.bfloat16)
        grad_out_ref[0, part, :, half:] = (grad_hidden * active).astype(jnp.bfloat16)


def middle(expert_rows, weights_in, grad_hidden):
    count, row_count, width = expert_rows.shape
    parts, both = weights_in.shape[1], weights_in.shape[3]
    tile = 512 if row_count % 512 == 0 else row_count
    return pl.pallas_call(
        middle_kernel,
        grid=(count, row_count // tile),
        out_shape=(
            jax.ShapeDtypeStruct((count, parts, row_count, both // 2), jnp.bfloat16),
            jax.ShapeDtypeStruct((count, parts, row_count, both), jnp.bfloat16),
        ),
        in_specs=[
            pl.BlockSpec((1, tile, width), lambda e, t: (e, t, 0)),
            pl.BlockSpec((1, parts, width, both), lambda e, t: (e, 0, 0, 0)),
            pl.BlockSpec((1, parts, tile, both // 2), lambda e, t: (e, 0, t, 0)),
        ],
        out_specs=(
            pl.BlockSpec((1, parts, tile, both // 2), lambda e, t: (e, 0, t, 0)),
            pl.BlockSpec((1, parts, tile, both), lambda e, t: (e, 0, t, 0)),
        ),
        name="middle",
    )(expert_rows, weights_in, grad_hidden)


def shards(
    tokens,
    cotangent,
    permutation,
    lengths,
    expert_ids,
    gate_weights,
    attn_gain,
    qkv_weight,
    out_weight,
    ffn_gain,
    expert_in,
    expert_out,
):
    device_count = lax.axis_size(ALL)
    hi_count = lax.axis_size("hi")
    lo_count = lax.axis_size("lo")
    tok_dev = permutation.shape[0]
    model_width = tokens.shape[1]
    peer_rows = tok_dev // device_count
    positions = jnp.arange(tok_dev, dtype=jnp.int32)
    expert_count = expert_in.shape[2] * device_count // FF_E
    capacity = TOK_MB * TOPK // expert_count
    source = permutation // tok_dev
    local_row = permutation % tok_dev
    from_source = (source[:, None] == jnp.arange(device_count, dtype=jnp.int32)[None, :]).astype(
        jnp.int32
    )
    earlier = jnp.cumsum(from_source, axis=0, dtype=jnp.int32) - from_source
    arrival = source * peer_rows + jnp.sum(earlier * from_source, axis=1, dtype=jnp.int32)
    arrival_match = arrival[:, None] == positions[None, :]
    wanted = jnp.sum(jnp.where(arrival_match, local_row[:, None], 0), axis=0, dtype=jnp.int32)
    by_arrival = jnp.sum(jnp.where(arrival_match, positions[:, None], 0), axis=0, dtype=jnp.int32)
    def swap(block, step):
        return lax.ppermute(block, "lo", [(i, i ^ step) for i in range(lo_count)])

    def spread(block):
        if lo_count != 4:
            return [[block]] + [[swap(block, step)] for step in range(1, lo_count)]
        half = block.shape[0] // 2
        one, two = swap(block, 1), swap(block, 2)
        return [[block], [one], [two], [swap(one[:half], 2), swap(two[half:], 1)]]

    if lo_count == 4:
        order = [(0, 0), (0, 1), (1, 0), (3, 0), (2, 1), (3, 1), (1, 1), (2, 0)]
    else:
        order = [(step, batch) for step in range(lo_count) for batch in range(MB)]
    routing = jnp.concatenate([expert_ids.astype(jnp.float32), gate_weights], axis=1)
    routing_all = [routing] + [swap(routing, step) for step in range(1, lo_count)]
    routing_all = jnp.stack(
        [routing_all[step][batch * TOK_MB : (batch + 1) * TOK_MB] for step, batch in order]
    )
    asked_rows = lax.all_to_all(
        wanted.reshape(device_count, peer_rows),
        ALL,
        split_axis=0,
        concat_axis=0,
        tiled=True,
    ).reshape(tok_dev)
    asked_rows, routing_all = lax.optimization_barrier((asked_rows, routing_all))
    asked_match = asked_rows[:, None] == positions[None, :]
    by_asked = jnp.sum(jnp.where(asked_match, positions[:, None], 0), axis=0, dtype=jnp.int32)
    sizes = (hi_count, lo_count, 2)
    shard_rows = qkv_weight.shape[0]
    qkv_cols = qkv_weight.shape[1]
    weight_shard = jnp.concatenate(
        [
            qkv_weight,
            out_weight,
            attn_gain[:, None],
            ffn_gain[:, None],
            jnp.zeros((shard_rows, 126), jnp.bfloat16),
        ],
        axis=1,
    )
    asked_tokens = pick(tokens, asked_rows).reshape(device_count, peer_rows, model_width)
    asked_grads = pick(cotangent, asked_rows).reshape(
        device_count, peer_rows, model_width
    )
    got_rows, got_grad, packed = opening(sizes, asked_tokens, asked_grads, weight_shard)
    got_rows, packed, expert_in = lax.optimization_barrier((got_rows, packed, expert_in))
    packed = packed.reshape(model_width, -1)
    grad_bf = pick(got_grad.reshape(tok_dev, model_width), arrival)
    got_rows = hold(got_rows, grad_bf)
    grad_blocks = spread(grad_bf)
    rows_in = pick(got_rows.reshape(tok_dev, model_width), arrival).astype(jnp.float32)
    qkv_full = packed[:, :qkv_cols]
    out_full = packed[:, qkv_cols : qkv_cols + model_width]
    gain_pair = packed[:, qkv_cols + model_width :].astype(jnp.float32)
    gain_one = gain_pair[:, 0]
    gain_two = gain_pair[:, 1]
    shard_cols = expert_in.shape[2]
    weights_in = lax.all_gather(
        expert_in.reshape(model_width, 2 * shard_cols), ("hi", "core"), axis=0
    ).reshape(hi_count, 2, model_width, 2 * shard_cols)
    weights_out = lax.all_gather(expert_out, ("hi", "core"), axis=0).reshape(
        hi_count, 2, shard_cols, model_width
    )
    segment, position = layout_rows(lengths)
    scale_one = lax.rsqrt(jnp.mean(rows_in * rows_in, axis=1, keepdims=True) + epsilon)
    normed = (rows_in * scale_one * gain_one).astype(jnp.bfloat16)
    projected = jnp.dot(normed, qkv_full, preferred_element_type=jnp.float32)
    cosine_table, sine_table = rope_tables(position)
    sides = (
        jnp.tile(cosine_table, (1, 4)),
        jnp.concatenate([-sine_table, sine_table] * 2, axis=1),
        segment.reshape(-1, TOK_MB, 1),
        segment.reshape(-1, 1, TOK_MB),
    )
    queries, key_rows, value_rows, mixed_rows = attend(projected, sides)
    if lo_count == 4:
        mixed_rows = hold(mixed_rows, grad_blocks[1][0], grad_blocks[2][0])
    attended = jnp.dot(mixed_rows, out_full, preferred_element_type=jnp.float32)
    residual = rows_in + attended
    scale_two = lax.rsqrt(jnp.mean(residual * residual, axis=1, keepdims=True) + epsilon)
    normed_two = (residual * scale_two * gain_two).astype(jnp.bfloat16)
    grad_output = grad_bf.astype(jnp.float32)
    home = lax.axis_index("lo")
    if lo_count == 4:
        normed_two = hold(normed_two, *grad_blocks[3])
    row_blocks = spread(normed_two)
    normed_two, grad_blocks = lax.optimization_barrier((normed_two, grad_blocks))
    choose, slot_gate = slot_tables(
        routing_all[..., :TOPK].astype(jnp.int32),
        routing_all[..., TOPK:],
        home + lo_count * jnp.arange(hi_count, dtype=jnp.int32),
        capacity,
    )
    slot_weight = jnp.transpose(slot_gate, (1, 0, 2))[..., None]
    place_of = {name: number for number, name in enumerate(order)}

    def fill(blocks, slots, weight):
        for step, pieces in blocks:
            batch = 0
            for piece in pieces:
                first = place_of[step, batch]
                stride = place_of[step, MB - 1] - place_of[step, 0]
                slots = dispatch(choose, piece, first, stride, slots, weight)
                batch += piece.shape[0] // TOK_MB
        return slots

    grad_expert = fill(list(enumerate(grad_blocks)), None, slot_weight)
    grad_expert = grad_expert.reshape(hi_count, -1, model_width)
    grad_hidden = jnp.einsum(
        "erd,ekfd->ekrf", grad_expert, weights_out, preferred_element_type=jnp.float32
    ).astype(jnp.bfloat16)
    expert_rows = fill([(0, [normed_two])], None, None)
    grad_hidden, expert_rows, others = lax.optimization_barrier(
        (grad_hidden, expert_rows, row_blocks[1:])
    )
    expert_rows = fill(list(enumerate(others, 1)), expert_rows, None)
    expert_rows = expert_rows.reshape(hi_count, -1, model_width)
    hidden, grad_gate_up = middle(expert_rows, weights_in, grad_hidden)
    grad_weights_out = jnp.einsum(
        "ekrf,erd->ekfd", hidden, grad_expert, preferred_element_type=jnp.float32
    ).astype(jnp.bfloat16)
    grad_weights_out, grad_gate_up = lax.optimization_barrier((grad_weights_out, grad_gate_up))
    shard_out = lax.psum_scatter(
        grad_weights_out.reshape(hi_count * 2 * shard_cols, model_width),
        ("hi", "core"),
        scatter_dimension=0,
        tiled=True,
    ).astype(jnp.float32)
    grad_expert_rows = jnp.einsum(
        "ekrf,ekdf->erd", grad_gate_up, weights_in, preferred_element_type=jnp.float32
    ).astype(jnp.bfloat16)

    def split_back(slot_values):
        return jnp.einsum(
            "becr,ebcd->brd",
            choose,
            slot_values.reshape(hi_count, lo_count * MB, capacity, model_width),
            preferred_element_type=jnp.float32,
        ).astype(jnp.bfloat16)

    def wide(value):
        return value.astype(jnp.float32)

    def bring_back(parts):
        if lo_count != 4:
            parts = parts.reshape(lo_count, tok_dev, model_width)
            return [parts[0]] + [swap(parts[step], step) for step in range(1, lo_count)]
        one = swap(parts[2:4], 1)
        two = swap(parts[4:6], 2)
        for_one = (wide(parts[6]) + wide(two[1])).astype(jnp.bfloat16)
        for_two = (wide(parts[7]) + wide(one[1])).astype(jnp.bfloat16)
        return [parts[:2], one, two, swap(for_two, 2), swap(for_one, 1)]

    def total_of(terms):
        if lo_count != 4:
            total = wide(terms[0])
            for term in terms[1:]:
                total = total + wide(term)
            return total
        own, one, two, last_two, last_one = terms
        return jnp.concatenate(
            [
                wide(own[0]) + wide(one[0]) + wide(last_two),
                wide(own[1]) + wide(two[0]) + wide(last_one),
            ],
            axis=0,
        )

    back = split_back(grad_expert_rows)
    back_parts = bring_back(back)
    produced = (
        jnp.einsum("ekrf,ekfd->erd", hidden, weights_out, preferred_element_type=jnp.float32)
        * slot_weight.reshape(hi_count, -1, 1)
    ).astype(jnp.bfloat16)
    ahead = split_back(produced)
    grad_gate_up = hold(grad_gate_up, ahead, *back_parts[1:3])
    grad_weights_in = jnp.einsum(
        "ekrf,erd->ekfd", grad_gate_up, expert_rows, preferred_element_type=jnp.float32
    ).astype(jnp.bfloat16)
    shard_in = lax.psum_scatter(
        grad_weights_in.reshape(hi_count * 2 * 2 * shard_cols, model_width),
        ("hi", "core"),
        scatter_dimension=0,
        tiled=True,
    )
    shard_in = shard_in.T.astype(jnp.float32).reshape(model_width, 2, shard_cols)
    ahead, back_parts = lax.optimization_barrier((ahead, back_parts))
    ahead_parts = bring_back(ahead)
    grad_normed_two = total_of(back_parts)
    grad_gain_two, grad_from_norm = norm_back(residual, scale_two, gain_two, grad_normed_two)
    grad_residual = grad_output + grad_from_norm
    grad_attended = grad_residual.astype(jnp.bfloat16)
    grad_out_weight = jnp.einsum(
        "nq,nd->qd", mixed_rows, grad_attended, preferred_element_type=jnp.float32
    )
    grad_mixed = jnp.einsum(
        "nd,qd->nq", grad_attended, out_full, preferred_element_type=jnp.float32
    ).astype(jnp.bfloat16)
    grad_projected = jnp.concatenate(
        attend_back(queries, key_rows, value_rows, grad_mixed, sides), axis=1
    )
    if lo_count == 4:
        normed = hold(normed, *ahead_parts[1:3])
    grad_qkv_weight = jnp.einsum(
        "nd,nc->dc", normed, grad_projected, preferred_element_type=jnp.float32
    )
    grad_normed = jnp.einsum(
        "nc,dc->nd", grad_projected, qkv_full, preferred_element_type=jnp.float32
    )
    grad_gain_one, grad_from_first = norm_back(rows_in, scale_one, gain_one, grad_normed)
    grad_input = (grad_residual + grad_from_first).astype(jnp.bfloat16)
    gains = jnp.pad(jnp.stack([grad_gain_one, grad_gain_two], axis=1), ((0, 0), (0, 126)))
    parts = jnp.concatenate(
        [
            grad_qkv_weight.astype(jnp.bfloat16),
            grad_out_weight.astype(jnp.bfloat16),
            gains.astype(jnp.bfloat16),
        ],
        axis=1,
    ).reshape(sizes + (shard_rows, -1))
    parts, shard_out, ahead_parts = lax.optimization_barrier((parts, shard_out, ahead_parts))
    output_rows = (residual + total_of(ahead_parts)).astype(jnp.bfloat16)
    home_out, home_grad, sums = closing(
        sizes,
        pick(output_rows, by_arrival).reshape(device_count, peer_rows, model_width),
        pick(grad_input, by_arrival).reshape(device_count, peer_rows, model_width),
        parts,
    )
    shard_qkv = sums[:, :qkv_cols]
    shard_attn_out = sums[:, qkv_cols : qkv_cols + model_width]
    shard_gain_one = sums[:, qkv_cols + model_width]
    shard_gain_two = sums[:, qkv_cols + model_width + 1]
    output = pick(home_out.reshape(tok_dev, model_width), by_asked)
    input_grad = pick(home_grad.reshape(tok_dev, model_width), by_asked)
    return (
        output,
        input_grad,
        shard_gain_one,
        shard_qkv,
        shard_attn_out,
        shard_gain_two,
        shard_in,
        shard_out,
    )


def solution(mesh):
    dp_count = mesh.shape["dp"]
    hi_count = 4 if dp_count % 4 == 0 else 1
    split = jax.sharding.Mesh(
        mesh.devices.reshape(hi_count, dp_count // hi_count, mesh.shape["expert"]), ALL
    )
    rows, columns = P(ALL, None), P(None, None, ALL)
    return jax.shard_map(
        shards,
        mesh=split,
        in_specs=(rows, rows, P(ALL), rows, rows, rows, P(ALL), rows, rows, P(ALL), columns, rows),
        out_specs=(rows, rows, P(ALL), rows, rows, P(ALL), columns, rows),
        check_vma=False,
    )
```

```python
import functools

import jax
import jax.numpy as jnp
from jax import lax
from jax.experimental import pallas as pl
from jax.experimental.pallas import tpu as pltpu
from jax.sharding import PartitionSpec as P

HEADS = 24
KV_HEADS = 8
HEAD = 64
FF_E = 512
TOPK = 8
MB = 2
SEQS = 4
TOK_MB = 256
ALL = ("hi", "lo", "core")


epsilon = 1e-05
theta_base = 10000.0


def layout_rows(length_rows):
    seq_ends = jnp.cumsum(length_rows, axis=1, dtype=jnp.int32)
    starts = seq_ends - length_rows
    within = jnp.arange(TOK_MB, dtype=jnp.int32)
    segment = jnp.sum(
        (within[None, :, None] >= seq_ends[:, None, :]).astype(jnp.int32), axis=2, dtype=jnp.int32
    )
    chosen = segment[:, :, None] == jnp.arange(SEQS, dtype=jnp.int32)[None, None, :]
    seq_begin = jnp.sum(jnp.where(chosen, starts[:, None, :], 0), axis=2, dtype=jnp.int32)
    position = within[None, :] - seq_begin
    segment = segment + jnp.arange(MB, dtype=jnp.int32)[:, None] * SEQS
    return (segment.reshape(-1), position.reshape(-1))


def rope_tables(position):
    half_width = HEAD // 2
    frequency = theta_base ** (-(2.0 / HEAD) * jnp.arange(half_width, dtype=jnp.float32))
    angles = position.astype(jnp.float32)[:, None] * frequency[None, :]
    return (jnp.cos(angles), jnp.sin(angles))


def slot_tables(ids, gates, experts, capacity):
    count = experts.shape[0]
    named = ids[..., None] == experts
    picked = jnp.any(named, axis=2)
    weight = jnp.sum(jnp.where(named, gates[..., None], 0.0), axis=2)
    rows = jnp.arange(TOK_MB, dtype=jnp.int32)
    below = (rows[:, None] > rows[None, :]).astype(jnp.bfloat16)
    shaped = picked.reshape(-1, TOK_MB, count)
    slot = jnp.einsum(
        "rq,bqe->ber", below, shaped.astype(jnp.bfloat16), preferred_element_type=jnp.float32
    ).astype(jnp.int32)
    kept = jnp.transpose(shaped, (0, 2, 1))
    hit = kept[:, :, None, :] & (
        slot[:, :, None, :] == jnp.arange(capacity, dtype=jnp.int32)[None, None, :, None]
    )
    weight = jnp.transpose(weight.reshape(-1, TOK_MB, count), (0, 2, 1))
    slot_gate = jnp.sum(jnp.where(hit, weight[:, :, None, :], 0.0), axis=3)
    return hit.astype(jnp.bfloat16), slot_gate


def partner(values):
    half = HEAD // 2
    lane = lax.broadcasted_iota(jnp.int32, values.shape, 1) % HEAD
    return jnp.where(
        lane < half, pltpu.roll(values, 2 * HEAD - half, 1), pltpu.roll(values, half, 1)
    )


OVER_ROWS = (((0,), (0,)), ((), ()))
OVER_LANES = (((1,), (1,)), ((), ()))


def allowed_keys(seg_col_ref, seg_row_ref, first, count):
    keys = first + count
    key_at = lax.broadcasted_iota(jnp.int32, (keys, count), 0)
    row_at = lax.broadcasted_iota(jnp.int32, (keys, count), 1) + first
    same = seg_col_ref[0, :keys, :] == seg_row_ref[0, :, first : first + count]
    return same & (row_at >= key_at)


def stacked(ref, rows, one, group):
    starts = range(one * group * HEAD, (one + 1) * group * HEAD, HEAD)
    return jnp.concatenate([ref[rows, start : start + HEAD] for start in starts], axis=0)


def unstack(ref, rows, one, values):
    count = rows.stop - rows.start
    group = values.shape[0] // count
    for head in range(group):
        start = (one * group + head) * HEAD
        ref[rows, start : start + HEAD] = values[head * count : (head + 1) * count]


def soft_weights(queries, keys, allowed):
    scores = lax.dot_general(keys, queries, OVER_LANES, preferred_element_type=jnp.float32)
    scores = jnp.where(allowed, scores, -1e30)
    weights = jnp.exp(scores - jnp.max(scores, axis=0, keepdims=True))
    return weights * (1.0 / jnp.sum(weights, axis=0, keepdims=True))


def attend_kernel(
    q_ref, k_ref, v_ref, cos_ref, sin_ref, seg_col_ref, seg_row_ref,
    q_out, k_out, v_out, mixed_ref
):
    cosine, sine = cos_ref[...], sin_ref[...]
    pair = 2 * HEAD
    group = HEADS // KV_HEADS
    for start in range(0, q_ref.shape[1], pair):
        values = q_ref[:, start : start + pair]
        turned = (values * cosine + partner(values) * sine).astype(jnp.bfloat16)
        q_out[:, start : start + pair] = turned * jnp.bfloat16(HEAD**-0.5)
    values = k_ref[...]
    k_out[...] = (values * cosine + partner(values) * sine).astype(jnp.bfloat16)
    v_out[...] = v_ref[...].astype(jnp.bfloat16)
    block = TOK_MB // 2
    for first in range(0, TOK_MB, block):
        rows, keys = slice(first, first + block), slice(0, first + block)
        allowed = allowed_keys(seg_col_ref, seg_row_ref, first, block)
        allowed = jnp.concatenate([allowed] * group, axis=1)
        for one in range(2):
            lanes = slice(one * HEAD, (one + 1) * HEAD)
            weights = soft_weights(
                stacked(q_out, rows, one, group), k_out[keys, lanes], allowed
            ).astype(jnp.bfloat16)
            mixed = lax.dot_general(
                weights, v_out[keys, lanes], OVER_ROWS, preferred_element_type=jnp.float32
            )
            unstack(mixed_ref, rows, one, mixed.astype(jnp.bfloat16))


def attend_back_kernel(
    q_ref, k_ref, v_ref, grad_ref, cos_ref, sin_ref, seg_col_ref, seg_row_ref,
    dq_ref, dk_ref, dv_ref, dq_sum, dk_sum, dv_sum
):
    cosine, sine = cos_ref[...], sin_ref[...]
    pair = 2 * HEAD
    group = HEADS // KV_HEADS
    block = TOK_MB // 2
    for first in range(TOK_MB - block, -1, -block):
        rows, keys = slice(first, first + block), slice(0, first + block)
        allowed = allowed_keys(seg_col_ref, seg_row_ref, first, block)
        allowed = jnp.concatenate([allowed] * group, axis=1)
        for one in range(2):
            lanes = slice(one * HEAD, (one + 1) * HEAD)
            key_rows, value_rows = k_ref[keys, lanes], v_ref[keys, lanes]
            queries = stacked(q_ref, rows, one, group)
            grads = stacked(grad_ref, rows, one, group)
            weights = soft_weights(queries, key_rows, allowed)
            grad_weights = lax.dot_general(
                value_rows, grads, OVER_LANES, preferred_element_type=jnp.float32
            )
            grad_values = jnp.dot(
                weights.astype(jnp.bfloat16), grads, preferred_element_type=jnp.float32
            )
            inner = jnp.sum(grad_weights * weights, axis=0, keepdims=True)
            grad_scores = (weights * (grad_weights - inner)).astype(jnp.bfloat16)
            grad_queries = lax.dot_general(
                grad_scores, key_rows, OVER_ROWS, preferred_element_type=jnp.float32
            )
            unstack(dq_sum, rows, one, grad_queries * HEAD ** (-0.5))
            grad_keys = jnp.dot(grad_scores, queries, preferred_element_type=jnp.float32)
            if first == TOK_MB - block:
                dk_sum[keys, lanes] = grad_keys
                dv_sum[keys, lanes] = grad_values
            else:
                dk_sum[keys, lanes] = dk_sum[keys, lanes] + grad_keys
                dv_sum[keys, lanes] = dv_sum[keys, lanes] + grad_values
    for start in range(0, q_ref.shape[1], pair):
        values = dq_sum[:, start : start + pair]
        dq_ref[:, start : start + pair] = (
            values * cosine - partner(values) * sine
        ).astype(jnp.bfloat16)
    values = dk_sum[...]
    dk_ref[...] = (values * cosine - partner(values) * sine).astype(jnp.bfloat16)
    dv_ref[...] = dv_sum[...].astype(jnp.bfloat16)


def attend_blocks(row_count):
    pair = 2 * HEAD
    wide = pair * (HEADS // KV_HEADS)
    narrow = pl.BlockSpec((TOK_MB, pair), lambda b, g: (b, g))
    broad = pl.BlockSpec((TOK_MB, wide), lambda b, g: (b, g))
    sides = [
        pl.BlockSpec((TOK_MB, pair), lambda b, g: (b, 0)),
        pl.BlockSpec((TOK_MB, pair), lambda b, g: (b, 0)),
        pl.BlockSpec((1, TOK_MB, 1), lambda b, g: (b, 0, 0)),
        pl.BlockSpec((1, 1, TOK_MB), lambda b, g: (b, 0, 0)),
    ]
    return (row_count // TOK_MB, KV_HEADS // 2), narrow, broad, sides


def attend(projected, sides):
    row_count = projected.shape[0]
    grid, narrow, broad, side_specs = attend_blocks(row_count)
    q_dim, kv_dim, pair = HEADS * HEAD, KV_HEADS * HEAD, 2 * HEAD
    key_start, value_start = q_dim // pair, (q_dim + kv_dim) // pair
    q_shape = jax.ShapeDtypeStruct((row_count, q_dim), jnp.bfloat16)
    kv_shape = jax.ShapeDtypeStruct((row_count, kv_dim), jnp.bfloat16)
    return pl.pallas_call(
        attend_kernel,
        grid=grid,
        out_shape=(q_shape, kv_shape, kv_shape, q_shape),
        in_specs=[
            broad,
            pl.BlockSpec((TOK_MB, pair), lambda b, g: (b, key_start + g)),
            pl.BlockSpec((TOK_MB, pair), lambda b, g: (b, value_start + g)),
        ]
        + side_specs,
        out_specs=(broad, narrow, narrow, broad),
        name="attend",
    )(projected, projected, projected, *sides)


def attend_back(queries, key_rows, value_rows, grad_mixed, sides):
    row_count = queries.shape[0]
    grid, narrow, broad, side_specs = attend_blocks(row_count)
    shapes = [jax.ShapeDtypeStruct(x.shape, jnp.bfloat16) for x in (queries, key_rows, value_rows)]
    return pl.pallas_call(
        attend_back_kernel,
        grid=grid,
        out_shape=tuple(shapes),
        in_specs=[broad, narrow, narrow, broad] + side_specs,
        out_specs=(broad, narrow, narrow),
        scratch_shapes=[
            pltpu.VMEM((TOK_MB, 2 * HEAD * (HEADS // KV_HEADS)), jnp.float32),
            pltpu.VMEM((TOK_MB, 2 * HEAD), jnp.float32),
            pltpu.VMEM((TOK_MB, 2 * HEAD), jnp.float32),
        ],
        name="attend_back",
    )(queries, key_rows, value_rows, grad_mixed, *sides)


def pick(rows, index):
    return jnp.take(rows, index, axis=0, mode="clip")


def hold(value, *after):
    anywhere = pl.BlockSpec(memory_space=pl.ANY)
    return pl.pallas_call(
        lambda *refs: None,
        out_shape=jax.ShapeDtypeStruct(value.shape, value.dtype),
        in_specs=[anywhere] * (1 + len(after)),
        out_specs=anywhere,
        input_output_aliases={0: 0},
        name="hold",
    )(value, *after)


def norm_back(values, scale, gain, grad_normed):
    scaled_grad = grad_normed * gain
    grad_gain = jnp.sum(grad_normed * values * scale, axis=0)
    grad_values = scale * scaled_grad - values * scale * scale * scale * jnp.mean(
        scaled_grad * values, axis=1, keepdims=True
    )
    return (grad_gain, grad_values)


MESH = pl.DeviceIdType.MESH


def flip(value, bits):
    bit = 1
    while bit <= bits:
        if bits & bit:
            value = value + bit * (1 - 2 * ((value // bit) % 2))
        bit *= 2
    return value


def place():
    return lax.axis_index("hi"), lax.axis_index("lo"), lax.axis_index("core")


def greet_all(sizes):
    hi_count, lo_count, _ = sizes
    count = hi_count * lo_count * 2
    hi, lo, core = place()
    me = (hi * lo_count + lo) * 2 + core
    barrier = pltpu.get_barrier_semaphore()

    def greet(step, carry):
        peer = (me + step) % count
        pl.semaphore_signal(
            barrier,
            inc=1,
            device_id=(peer // (2 * lo_count), (peer // 2) % lo_count, peer % 2),
            device_id_type=MESH,
        )
        return carry

    lax.fori_loop(1, count, greet, 0)
    pl.semaphore_wait(barrier, count - 1)


def send_rows(sizes, source, target, send_sem, recv_sem):
    hi_count, lo_count, _ = sizes
    count = hi_count * lo_count * 2
    hi, lo, core = place()
    me = (hi * lo_count + lo) * 2 + core

    def one(step, carry):
        peer = (me + step) % count
        pltpu.make_async_remote_copy(
            src_ref=source.at[peer],
            dst_ref=target.at[me],
            send_sem=send_sem,
            recv_sem=recv_sem,
            device_id=(peer // (2 * lo_count), (peer // 2) % lo_count, peer % 2),
            device_id_type=MESH,
        ).start()
        return carry

    lax.fori_loop(1, count, one, 0)


def wait_rows(source, target, send_sem, recv_sem):
    rest = pl.ds(0, source.shape[0] - 1)
    pltpu.make_async_copy(source.at[rest], source.at[rest], send_sem).wait()
    pltpu.make_async_copy(target.at[rest], target.at[rest], recv_sem).wait()


def lo_steps(lo_count, turn):
    bits = []
    bit = 1
    while bit < lo_count:
        bits.append(bit)
        bit *= 2
    if turn:
        bits = bits[::-1]
    held, steps = [0], []
    for bit in bits:
        steps.append((bit, list(held)))
        held = held + [offset ^ bit for offset in held]
    return steps


def opening_kernel(
    sizes, rows_ref, grads_ref, shard_ref, got_ref, got_grads_ref, full_ref,
    own_sem, row_sems, hi_sems, lo_sems, core_sems
):
    hi_count, lo_count, _ = sizes
    hi, lo, core = place()
    me = (hi * lo_count + lo) * 2 + core
    own = [
        pltpu.make_async_copy(shard_ref, full_ref.at[hi, lo, core], own_sem.at[0]),
        pltpu.make_async_copy(rows_ref.at[me], got_ref.at[me], own_sem.at[1]),
        pltpu.make_async_copy(grads_ref.at[me], got_grads_ref.at[me], own_sem.at[2]),
    ]
    for copy in own:
        copy.start()
    greet_all(sizes)

    def hop(source, at, device, sems, *index):
        return pltpu.make_async_remote_copy(
            src_ref=source,
            dst_ref=full_ref.at[at[0], at[1], at[2]],
            send_sem=sems.at[0, *index],
            recv_sem=sems.at[1, *index],
            device_id=device,
            device_id_type=MESH,
        )

    along_hi = {}
    for step in range(1, hi_count):
        along_hi[step] = hop(
            shard_ref, (hi, lo, core), (flip(hi, step), lo, core), hi_sems, step - 1
        )
        along_hi[step].start()
    send_rows(sizes, rows_ref, got_ref, row_sems.at[0, 0], row_sems.at[1, 0])
    send_rows(sizes, grads_ref, got_grads_ref, row_sems.at[0, 1], row_sems.at[1, 1])

    def across(plane, offset, first):
        at = (flip(hi, plane), flip(lo, offset), core)
        source = shard_ref if first else full_ref.at[at[0], at[1], at[2]]
        copy = hop(source, at, (hi, lo, 1 - core), core_sems, plane, offset)
        copy.start()
        return copy

    started, waits = [], []
    for plane in range(hi_count):
        if plane:
            along_hi[plane].wait_recv()
        started.append(across(plane, 0, plane == 0))
        number = 0
        for bit, offsets in lo_steps(lo_count, plane % 2):
            for offset in offsets:
                at = (flip(hi, plane), flip(lo, offset), core)
                source = shard_ref if plane == 0 and offset == 0 else full_ref.at[at[0], at[1], at[2]]
                copy = hop(source, at, (hi, flip(lo, bit), core), lo_sems, plane, number)
                number += 1
                if offset == 0:
                    copy.start()
                    started.append(copy)
                waits.append((copy, plane, offset, bit))
    arrived = {}
    for copy, plane, offset, bit in waits:
        if offset:
            copy.start()
            started.append(copy)
        copy.wait_recv()
        started.append(across(plane, offset ^ bit, False))
    for copy in started:
        copy.wait_send()
    for step in range(1, hi_count):
        along_hi[step].wait_send()
    for plane in range(hi_count):
        for offset in range(lo_count):
            at = (flip(hi, plane), flip(lo, offset), core)
            hop(
                full_ref.at[at[0], at[1], at[2]], at, (hi, lo, 1 - core), core_sems, plane, offset
            ).wait_recv()
    wait_rows(rows_ref, got_ref, row_sems.at[0, 0], row_sems.at[1, 0])
    wait_rows(grads_ref, got_grads_ref, row_sems.at[0, 1], row_sems.at[1, 1])
    for copy in own:
        copy.wait()


def opening(sizes, rows, grads, shard):
    hi_count, lo_count, _ = sizes
    anywhere = pl.BlockSpec(memory_space=pl.ANY)
    return pl.pallas_call(
        functools.partial(opening_kernel, sizes),
        out_shape=(
            jax.ShapeDtypeStruct(rows.shape, rows.dtype),
            jax.ShapeDtypeStruct(grads.shape, grads.dtype),
            jax.ShapeDtypeStruct(sizes + shard.shape, shard.dtype),
        ),
        in_specs=[anywhere] * 3,
        out_specs=(anywhere, anywhere, anywhere),
        scratch_shapes=[
            pltpu.SemaphoreType.DMA((3,)),
            pltpu.SemaphoreType.DMA((2, 2)),
            pltpu.SemaphoreType.DMA((2, hi_count)),
            pltpu.SemaphoreType.DMA((2, hi_count, lo_count)),
            pltpu.SemaphoreType.DMA((2, hi_count, lo_count)),
        ],
        compiler_params=pltpu.CompilerParams(collective_id=0, has_side_effects=True),
        name="opening",
    )(rows, grads, shard)


def add_blocks(target, first, second):
    rows = target.shape[0]
    tile = 16 if rows % 16 == 0 else rows

    def one(index, carry):
        at = pl.ds(index * tile, tile)
        target[at, :] = (
            first[at, :].astype(jnp.float32) + second[at, :].astype(jnp.float32)
        ).astype(target.dtype)
        return carry

    lax.fori_loop(0, rows // tile, one, 0)


def closing_kernel(
    sizes, out_ref, grad_ref, parts_ref, got_out, got_grad, sum_ref,
    from_core, from_lo, from_hi, held, own_sem, row_sems, hi_sems, lo_sems, core_sems
):
    hi_count, lo_count, _ = sizes
    hi, lo, core = place()
    me = (hi * lo_count + lo) * 2 + core
    own = [
        pltpu.make_async_copy(out_ref.at[me], got_out.at[me], own_sem.at[0]),
        pltpu.make_async_copy(grad_ref.at[me], got_grad.at[me], own_sem.at[1]),
    ]
    for copy in own:
        copy.start()
    greet_all(sizes)

    def hop(source, target, device, sems, *index):
        return pltpu.make_async_remote_copy(
            src_ref=source,
            dst_ref=target,
            send_sem=sems.at[0, *index],
            recv_sem=sems.at[1, *index],
            device_id=device,
            device_id_type=MESH,
        )

    planes = [plane for plane in range(1, hi_count)] + [0]
    across = {}
    for plane in planes:
        for offset in reversed(range(lo_count)):
            across[plane, offset] = hop(
                parts_ref.at[flip(hi, plane), flip(lo, offset), 1 - core],
                from_core.at[plane, offset],
                (hi, lo, 1 - core),
                core_sems,
                plane,
                offset,
            )
            across[plane, offset].start()
    send_rows(sizes, grad_ref, got_grad, row_sems.at[0, 0], row_sems.at[1, 0])
    send_rows(sizes, out_ref, got_out, row_sems.at[0, 1], row_sems.at[1, 1])
    started = []
    plans = {plane: lo_steps(lo_count, plane % 2)[::-1] for plane in planes}
    moves = {}
    for depth in range(len(plans[0])):
        for plane in planes:
            bit, kept = plans[plane][depth]
            base = lo_count - 2 * len(kept)
            if depth == 0:
                for offset in [keep ^ bit for keep in kept] + kept:
                    across[plane, offset].wait_recv()
                    add_blocks(
                        held.at[plane, offset],
                        parts_ref.at[flip(hi, plane), flip(lo, offset), core],
                        from_core.at[plane, offset],
                    )
            else:
                before = plans[plane][depth - 1]
                for number, offset in enumerate(before[1]):
                    copy, spot = moves[plane, depth - 1, offset]
                    copy.wait_recv()
                    add_blocks(held.at[plane, offset], held.at[plane, offset], from_lo.at[plane, spot])
            for number, offset in enumerate(kept):
                spot = base + number
                copy = hop(
                    held.at[plane, offset ^ bit],
                    from_lo.at[plane, spot],
                    (hi, flip(lo, bit), core),
                    lo_sems,
                    plane,
                    spot,
                )
                copy.start()
                started.append(copy)
                moves[plane, depth, offset] = (copy, spot)
    last = len(plans[0]) - 1
    along = {}
    for plane in planes:
        copy, spot = moves[plane, last, 0]
        copy.wait_recv()
        add_blocks(held.at[plane, 0], held.at[plane, 0], from_lo.at[plane, spot])
        if plane:
            along[plane] = hop(
                held.at[plane, 0],
                from_hi.at[plane],
                (flip(hi, plane), lo, core),
                hi_sems,
                plane,
            )
            along[plane].start()
            started.append(along[plane])
    for plane in range(1, hi_count):
        along[plane].wait_recv()
    rows = sum_ref.shape[0]
    tile = 16 if rows % 16 == 0 else rows

    def total(index, carry):
        at = pl.ds(index * tile, tile)
        value = held[0, 0, at, :].astype(jnp.float32)
        for plane in range(1, hi_count):
            value = value + from_hi[plane, at, :].astype(jnp.float32)
        sum_ref[at, :] = value
        return carry

    lax.fori_loop(0, rows // tile, total, 0)
    for copy in started:
        copy.wait_send()
    for copy in across.values():
        copy.wait_send()
    wait_rows(grad_ref, got_grad, row_sems.at[0, 0], row_sems.at[1, 0])
    wait_rows(out_ref, got_out, row_sems.at[0, 1], row_sems.at[1, 1])
    for copy in own:
        copy.wait()


def closing(sizes, out_rows, grad_rows, parts):
    hi_count, lo_count, _ = sizes
    block = parts.shape[3:]
    anywhere = pl.BlockSpec(memory_space=pl.ANY)
    near = pl.BlockSpec(memory_space=pltpu.VMEM)
    return pl.pallas_call(
        functools.partial(closing_kernel, sizes),
        out_shape=(
            jax.ShapeDtypeStruct(out_rows.shape, out_rows.dtype),
            jax.ShapeDtypeStruct(grad_rows.shape, grad_rows.dtype),
            jax.ShapeDtypeStruct(block, jnp.float32),
        ),
        in_specs=[anywhere, anywhere, near],
        out_specs=(anywhere, anywhere, near),
        scratch_shapes=[
            pltpu.VMEM((hi_count, lo_count) + block, jnp.bfloat16),
            pltpu.VMEM((hi_count, lo_count) + block, jnp.bfloat16),
            pltpu.VMEM((hi_count,) + block, jnp.bfloat16),
            pltpu.VMEM((hi_count, lo_count) + block, jnp.bfloat16),
            pltpu.SemaphoreType.DMA((2,)),
            pltpu.SemaphoreType.DMA((2, 2)),
            pltpu.SemaphoreType.DMA((2, hi_count)),
            pltpu.SemaphoreType.DMA((2, hi_count, lo_count)),
            pltpu.SemaphoreType.DMA((2, hi_count, lo_count)),
        ],
        compiler_params=pltpu.CompilerParams(
            collective_id=1, has_side_effects=True, vmem_limit_bytes=60 << 20
        ),
        name="closing",
    )(out_rows, grad_rows, parts)


def dispatch_kernel(weighted, choose_ref, rows_ref, *refs):
    count, capacity, rows = choose_ref.shape[1:]
    chosen = choose_ref[0].reshape(count * capacity, rows)
    width = rows_ref.shape[1]
    tile = 256 if width % 256 == 0 else width
    for start in range(0, width, tile):
        at = pl.ds(start, tile)
        slots = jnp.dot(chosen, rows_ref[:, at], preferred_element_type=jnp.float32)
        slots = slots.reshape(count, capacity, tile)
        if weighted:
            slots = slots * refs[0][:, 0]
        refs[-1][:, 0, :, at] = slots.astype(jnp.bfloat16)


def dispatch(choose, rows, first, stride, slots, weight):
    _, count, capacity, _ = choose.shape
    width = rows.shape[1]
    operands = [choose, rows]
    in_specs = [
        pl.BlockSpec((1, count, capacity, TOK_MB), lambda b: (first + b * stride, 0, 0, 0)),
        pl.BlockSpec((TOK_MB, width), lambda b: (b, 0)),
    ]
    if weight is not None:
        operands.append(weight)
        in_specs.append(pl.BlockSpec((count, 1, capacity, 1), lambda b: (0, first + b * stride, 0, 0)))
    aliases = {}
    if slots is not None:
        aliases = {len(operands): 0}
        operands.append(slots)
        in_specs.append(pl.BlockSpec(memory_space=pl.ANY))
    return pl.pallas_call(
        functools.partial(dispatch_kernel, weight is not None),
        grid=(rows.shape[0] // TOK_MB,),
        out_shape=jax.ShapeDtypeStruct((count, choose.shape[0], capacity, width), jnp.bfloat16),
        in_specs=in_specs,
        out_specs=pl.BlockSpec((count, 1, capacity, width), lambda b: (0, first + b * stride, 0, 0)),
        input_output_aliases=aliases,
        name="dispatch",
    )(*operands)


def middle_kernel(rows_ref, weight_ref, grad_ref, hidden_ref, grad_out_ref):
    half = grad_ref.shape[3]
    for part in range(weight_ref.shape[1]):
        gate_up = jnp.dot(rows_ref[0], weight_ref[0, part], preferred_element_type=jnp.float32)
        gate, up = gate_up[:, :half], gate_up[:, half:]
        sigmoid_gate = jax.nn.sigmoid(gate)
        active = gate * sigmoid_gate
        grad_hidden = grad_ref[0, part].astype(jnp.float32)
        hidden_ref[0, part] = (active * up).astype(jnp.bfloat16)
        slope = sigmoid_gate * (1.0 + gate * (1.0 - sigmoid_gate))
        grad_out_ref[0, part, :, :half] = (grad_hidden * up * slope).astype(jnp.bfloat16)
        grad_out_ref[0, part, :, half:] = (grad_hidden * active).astype(jnp.bfloat16)


def middle(expert_rows, weights_in, grad_hidden):
    count, row_count, width = expert_rows.shape
    parts, both = weights_in.shape[1], weights_in.shape[3]
    tile = 512 if row_count % 512 == 0 else row_count
    return pl.pallas_call(
        middle_kernel,
        grid=(count, row_count // tile),
        out_shape=(
            jax.ShapeDtypeStruct((count, parts, row_count, both // 2), jnp.bfloat16),
            jax.ShapeDtypeStruct((count, parts, row_count, both), jnp.bfloat16),
        ),
        in_specs=[
            pl.BlockSpec((1, tile, width), lambda e, t: (e, t, 0)),
            pl.BlockSpec((1, parts, width, both), lambda e, t: (e, 0, 0, 0)),
            pl.BlockSpec((1, parts, tile, both // 2), lambda e, t: (e, 0, t, 0)),
        ],
        out_specs=(
            pl.BlockSpec((1, parts, tile, both // 2), lambda e, t: (e, 0, t, 0)),
            pl.BlockSpec((1, parts, tile, both), lambda e, t: (e, 0, t, 0)),
        ),
        name="middle",
    )(expert_rows, weights_in, grad_hidden)


def shards(
    tokens,
    cotangent,
    permutation,
    lengths,
    expert_ids,
    gate_weights,
    attn_gain,
    qkv_weight,
    out_weight,
    ffn_gain,
    expert_in,
    expert_out,
):
    device_count = lax.axis_size(ALL)
    hi_count = lax.axis_size("hi")
    lo_count = lax.axis_size("lo")
    tok_dev = permutation.shape[0]
    model_width = tokens.shape[1]
    peer_rows = tok_dev // device_count
    positions = jnp.arange(tok_dev, dtype=jnp.int32)
    expert_count = expert_in.shape[2] * device_count // FF_E
    capacity = TOK_MB * TOPK // expert_count
    source = permutation // tok_dev
    local_row = permutation % tok_dev
    from_source = (source[:, None] == jnp.arange(device_count, dtype=jnp.int32)[None, :]).astype(
        jnp.int32
    )
    earlier = jnp.cumsum(from_source, axis=0, dtype=jnp.int32) - from_source
    arrival = source * peer_rows + jnp.sum(earlier * from_source, axis=1, dtype=jnp.int32)
    arrival_match = arrival[:, None] == positions[None, :]
    wanted = jnp.sum(jnp.where(arrival_match, local_row[:, None], 0), axis=0, dtype=jnp.int32)
    by_arrival = jnp.sum(jnp.where(arrival_match, positions[:, None], 0), axis=0, dtype=jnp.int32)
    def swap(block, step):
        return lax.ppermute(block, "lo", [(i, i ^ step) for i in range(lo_count)])

    def spread(block):
        if lo_count != 4:
            return [[block]] + [[swap(block, step)] for step in range(1, lo_count)]
        half = block.shape[0] // 2
        one, two = swap(block, 1), swap(block, 2)
        return [[block], [one], [two], [swap(one[:half], 2), swap(two[half:], 1)]]

    if lo_count == 4:
        order = [(0, 0), (0, 1), (1, 0), (3, 0), (2, 1), (3, 1), (1, 1), (2, 0)]
    else:
        order = [(step, batch) for step in range(lo_count) for batch in range(MB)]
    routing = jnp.concatenate([expert_ids.astype(jnp.float32), gate_weights], axis=1)
    routing_all = [routing] + [swap(routing, step) for step in range(1, lo_count)]
    routing_all = jnp.stack(
        [routing_all[step][batch * TOK_MB : (batch + 1) * TOK_MB] for step, batch in order]
    )
    asked_rows = lax.all_to_all(
        wanted.reshape(device_count, peer_rows),
        ALL,
        split_axis=0,
        concat_axis=0,
        tiled=True,
    ).reshape(tok_dev)
    asked_rows, routing_all = lax.optimization_barrier((asked_rows, routing_all))
    asked_match = asked_rows[:, None] == positions[None, :]
    by_asked = jnp.sum(jnp.where(asked_match, positions[:, None], 0), axis=0, dtype=jnp.int32)
    sizes = (hi_count, lo_count, 2)
    shard_rows = qkv_weight.shape[0]
    qkv_cols = qkv_weight.shape[1]
    weight_shard = jnp.concatenate(
        [
            qkv_weight,
            out_weight,
            attn_gain[:, None],
            ffn_gain[:, None],
            jnp.zeros((shard_rows, 126), jnp.bfloat16),
        ],
        axis=1,
    )
    asked_tokens = pick(tokens, asked_rows).reshape(device_count, peer_rows, model_width)
    asked_grads = pick(cotangent, asked_rows).reshape(
        device_count, peer_rows, model_width
    )
    got_rows, got_grad, packed = opening(sizes, asked_tokens, asked_grads, weight_shard)
    got_rows, packed, expert_in = lax.optimization_barrier((got_rows, packed, expert_in))
    packed = packed.reshape(model_width, -1)
    grad_bf = pick(got_grad.reshape(tok_dev, model_width), arrival)
    got_rows = hold(got_rows, grad_bf)
    grad_blocks = spread(grad_bf)
    rows_in = pick(got_rows.reshape(tok_dev, model_width), arrival).astype(jnp.float32)
    qkv_full = packed[:, :qkv_cols]
    out_full = packed[:, qkv_cols : qkv_cols + model_width]
    gain_pair = packed[:, qkv_cols + model_width :].astype(jnp.float32)
    gain_one = gain_pair[:, 0]
    gain_two = gain_pair[:, 1]
    shard_cols = expert_in.shape[2]
    weights_in = lax.all_gather(
        expert_in.reshape(model_width, 2 * shard_cols), ("hi", "core"), axis=0
    ).reshape(hi_count, 2, model_width, 2 * shard_cols)
    weights_out = lax.all_gather(expert_out, ("hi", "core"), axis=0).reshape(
        hi_count, 2, shard_cols, model_width
    )
    segment, position = layout_rows(lengths)
    scale_one = lax.rsqrt(jnp.mean(rows_in * rows_in, axis=1, keepdims=True) + epsilon)
    normed = (rows_in * scale_one * gain_one).astype(jnp.bfloat16)
    projected = jnp.dot(normed, qkv_full, preferred_element_type=jnp.float32)
    cosine_table, sine_table = rope_tables(position)
    sides = (
        jnp.tile(cosine_table, (1, 4)),
        jnp.concatenate([-sine_table, sine_table] * 2, axis=1),
        segment.reshape(-1, TOK_MB, 1),
        segment.reshape(-1, 1, TOK_MB),
    )
    queries, key_rows, value_rows, mixed_rows = attend(projected, sides)
    if lo_count == 4:
        mixed_rows = hold(mixed_rows, grad_blocks[1][0], grad_blocks[2][0])
    attended = jnp.dot(mixed_rows, out_full, preferred_element_type=jnp.float32)
    residual = rows_in + attended
    scale_two = lax.rsqrt(jnp.mean(residual * residual, axis=1, keepdims=True) + epsilon)
    normed_two = (residual * scale_two * gain_two).astype(jnp.bfloat16)
    grad_output = grad_bf.astype(jnp.float32)
    home = lax.axis_index("lo")
    if lo_count == 4:
        normed_two = hold(normed_two, *grad_blocks[3])
    row_blocks = spread(normed_two)
    normed_two, grad_blocks = lax.optimization_barrier((normed_two, grad_blocks))
    choose, slot_gate = slot_tables(
        routing_all[..., :TOPK].astype(jnp.int32),
        routing_all[..., TOPK:],
        home + lo_count * jnp.arange(hi_count, dtype=jnp.int32),
        capacity,
    )
    slot_weight = jnp.transpose(slot_gate, (1, 0, 2))[..., None]
    place_of = {name: number for number, name in enumerate(order)}

    def fill(blocks, slots, weight):
        for step, pieces in blocks:
            batch = 0
            for piece in pieces:
                first = place_of[step, batch]
                stride = place_of[step, MB - 1] - place_of[step, 0]
                slots = dispatch(choose, piece, first, stride, slots, weight)
                batch += piece.shape[0] // TOK_MB
        return slots

    grad_expert = fill(list(enumerate(grad_blocks)), None, slot_weight)
    grad_expert = grad_expert.reshape(hi_count, -1, model_width)
    grad_hidden = jnp.einsum(
        "erd,ekfd->ekrf", grad_expert, weights_out, preferred_element_type=jnp.float32
    ).astype(jnp.bfloat16)
    expert_rows = fill([(0, [normed_two])], None, None)
    grad_hidden, expert_rows, others = lax.optimization_barrier(
        (grad_hidden, expert_rows, row_blocks[1:])
    )
    expert_rows = fill(list(enumerate(others, 1)), expert_rows, None)
    expert_rows = expert_rows.reshape(hi_count, -1, model_width)
    hidden, grad_gate_up = middle(expert_rows, weights_in, grad_hidden)
    grad_weights_out = jnp.einsum(
        "ekrf,erd->ekfd", hidden, grad_expert, preferred_element_type=jnp.float32
    ).astype(jnp.bfloat16)
    grad_weights_out, grad_gate_up = lax.optimization_barrier((grad_weights_out, grad_gate_up))
    shard_out = lax.psum_scatter(
        grad_weights_out.reshape(hi_count * 2 * shard_cols, model_width),
        ("hi", "core"),
        scatter_dimension=0,
        tiled=True,
    ).astype(jnp.float32)
    grad_expert_rows = jnp.einsum(
        "ekrf,ekdf->erd", grad_gate_up, weights_in, preferred_element_type=jnp.float32
    ).astype(jnp.bfloat16)

    def split_back(slot_values):
        return jnp.einsum(
            "becr,ebcd->brd",
            choose,
            slot_values.reshape(hi_count, lo_count * MB, capacity, model_width),
            preferred_element_type=jnp.float32,
        ).astype(jnp.bfloat16)

    def wide(value):
        return value.astype(jnp.float32)

    def bring_back(parts):
        if lo_count != 4:
            parts = parts.reshape(lo_count, tok_dev, model_width)
            swapped = [swap(parts[step], step) for step in range(1, lo_count)]
            return [parts[0]] + swapped, ()
        one = swap(parts[2:4], 1)
        two = swap(parts[4:6], 2)
        for_one = (wide(parts[6]) + wide(two[1])).astype(jnp.bfloat16)
        for_two = (wide(parts[7]) + wide(one[1])).astype(jnp.bfloat16)
        return [parts[:2], one, two, swap(for_two, 2), swap(for_one, 1)], (for_one, for_two)

    def total_of(terms):
        if lo_count != 4:
            total = wide(terms[0])
            for term in terms[1:]:
                total = total + wide(term)
            return total
        own, one, two, last_two, last_one = terms
        return jnp.concatenate(
            [
                wide(own[0]) + wide(one[0]) + wide(last_two),
                wide(own[1]) + wide(two[0]) + wide(last_one),
            ],
            axis=0,
        )

    back = split_back(grad_expert_rows)
    back_parts, passed_on = bring_back(back)
    produced = (
        jnp.einsum("ekrf,ekfd->erd", hidden, weights_out, preferred_element_type=jnp.float32)
        * slot_weight.reshape(hi_count, -1, 1)
    ).astype(jnp.bfloat16)
    ahead = split_back(produced)
    grad_gate_up = hold(grad_gate_up, ahead, *passed_on)
    grad_weights_in = jnp.einsum(
        "ekrf,erd->ekfd", grad_gate_up, expert_rows, preferred_element_type=jnp.float32
    ).astype(jnp.bfloat16)
    shard_in = lax.psum_scatter(
        grad_weights_in.reshape(hi_count * 2 * 2 * shard_cols, model_width),
        ("hi", "core"),
        scatter_dimension=0,
        tiled=True,
    )
    shard_in = shard_in.astype(jnp.float32).reshape(2, shard_cols, model_width)
    shard_in = jnp.transpose(shard_in, (2, 0, 1))
    ahead, back_parts = lax.optimization_barrier((ahead, back_parts))
    ahead_parts, _ = bring_back(ahead)
    grad_normed_two = total_of(back_parts)
    grad_gain_two, grad_from_norm = norm_back(residual, scale_two, gain_two, grad_normed_two)
    grad_residual = grad_output + grad_from_norm
    grad_attended = grad_residual.astype(jnp.bfloat16)
    grad_out_weight = jnp.einsum(
        "nq,nd->qd", mixed_rows, grad_attended, preferred_element_type=jnp.float32
    )
    grad_mixed = jnp.einsum(
        "nd,qd->nq", grad_attended, out_full, preferred_element_type=jnp.float32
    ).astype(jnp.bfloat16)
    grad_projected = jnp.concatenate(
        attend_back(queries, key_rows, value_rows, grad_mixed, sides), axis=1
    )
    if lo_count == 4:
        normed = hold(normed, *ahead_parts[1:3])
    grad_qkv_weight = jnp.einsum(
        "nd,nc->dc", normed, grad_projected, preferred_element_type=jnp.float32
    )
    grad_normed = jnp.einsum(
        "nc,dc->nd", grad_projected, qkv_full, preferred_element_type=jnp.float32
    )
    grad_gain_one, grad_from_first = norm_back(rows_in, scale_one, gain_one, grad_normed)
    grad_input = (grad_residual + grad_from_first).astype(jnp.bfloat16)
    gains = jnp.pad(jnp.stack([grad_gain_one, grad_gain_two], axis=1), ((0, 0), (0, 126)))
    parts = jnp.concatenate(
        [
            grad_qkv_weight.astype(jnp.bfloat16),
            grad_out_weight.astype(jnp.bfloat16),
            gains.astype(jnp.bfloat16),
        ],
        axis=1,
    ).reshape(sizes + (shard_rows, -1))
    parts, shard_out, ahead_parts = lax.optimization_barrier((parts, shard_out, ahead_parts))
    output_rows = (residual + total_of(ahead_parts)).astype(jnp.bfloat16)
    home_out, home_grad, sums = closing(
        sizes,
        pick(output_rows, by_arrival).reshape(device_count, peer_rows, model_width),
        pick(grad_input, by_arrival).reshape(device_count, peer_rows, model_width),
        parts,
    )
    shard_qkv = sums[:, :qkv_cols]
    shard_attn_out = sums[:, qkv_cols : qkv_cols + model_width]
    shard_gain_one = sums[:, qkv_cols + model_width]
    shard_gain_two = sums[:, qkv_cols + model_width + 1]
    output = pick(home_out.reshape(tok_dev, model_width), by_asked)
    input_grad = pick(home_grad.reshape(tok_dev, model_width), by_asked)
    return (
        output,
        input_grad,
        shard_gain_one,
        shard_qkv,
        shard_attn_out,
        shard_gain_two,
        shard_in,
        shard_out,
    )


def solution(mesh):
    dp_count = mesh.shape["dp"]
    hi_count = 4 if dp_count % 4 == 0 else 1
    split = jax.sharding.Mesh(
        mesh.devices.reshape(hi_count, dp_count // hi_count, mesh.shape["expert"]), ALL
    )
    rows, columns = P(ALL, None), P(None, None, ALL)
    return jax.shard_map(
        shards,
        mesh=split,
        in_specs=(rows, rows, P(ALL), rows, rows, rows, P(ALL), rows, rows, P(ALL), columns, rows),
        out_specs=(rows, rows, P(ALL), rows, rows, P(ALL), columns, rows),
        check_vma=False,
    )
```

```python
import functools

import jax
import jax.numpy as jnp
from jax import lax
from jax.experimental import pallas as pl
from jax.experimental.pallas import tpu as pltpu
from jax.sharding import PartitionSpec as P

HEADS = 24
KV_HEADS = 8
HEAD = 64
FF_E = 512
TOPK = 8
MB = 2
SEQS = 4
TOK_MB = 256
ALL = ("hi", "lo", "core")


epsilon = 1e-05
theta_base = 10000.0


def layout_rows(length_rows):
    seq_ends = jnp.cumsum(length_rows, axis=1, dtype=jnp.int32)
    starts = seq_ends - length_rows
    within = jnp.arange(TOK_MB, dtype=jnp.int32)
    segment = jnp.sum(
        (within[None, :, None] >= seq_ends[:, None, :]).astype(jnp.int32), axis=2, dtype=jnp.int32
    )
    chosen = segment[:, :, None] == jnp.arange(SEQS, dtype=jnp.int32)[None, None, :]
    seq_begin = jnp.sum(jnp.where(chosen, starts[:, None, :], 0), axis=2, dtype=jnp.int32)
    position = within[None, :] - seq_begin
    segment = segment + jnp.arange(MB, dtype=jnp.int32)[:, None] * SEQS
    return (segment.reshape(-1), position.reshape(-1))


def rope_tables(position):
    half_width = HEAD // 2
    frequency = theta_base ** (-(2.0 / HEAD) * jnp.arange(half_width, dtype=jnp.float32))
    angles = position.astype(jnp.float32)[:, None] * frequency[None, :]
    return (jnp.cos(angles), jnp.sin(angles))


def slot_tables(ids, gates, experts, capacity):
    count = experts.shape[0]
    named = ids[..., None] == experts
    picked = jnp.any(named, axis=2)
    weight = jnp.sum(jnp.where(named, gates[..., None], 0.0), axis=2)
    rows = jnp.arange(TOK_MB, dtype=jnp.int32)
    below = (rows[:, None] > rows[None, :]).astype(jnp.bfloat16)
    shaped = picked.reshape(-1, TOK_MB, count)
    slot = jnp.einsum(
        "rq,bqe->ber", below, shaped.astype(jnp.bfloat16), preferred_element_type=jnp.float32
    ).astype(jnp.int32)
    kept = jnp.transpose(shaped, (0, 2, 1))
    hit = kept[:, :, None, :] & (
        slot[:, :, None, :] == jnp.arange(capacity, dtype=jnp.int32)[None, None, :, None]
    )
    weight = jnp.transpose(weight.reshape(-1, TOK_MB, count), (0, 2, 1))
    slot_gate = jnp.sum(jnp.where(hit, weight[:, :, None, :], 0.0), axis=3)
    return hit.astype(jnp.bfloat16), slot_gate


def partner(values):
    half = HEAD // 2
    lane = lax.broadcasted_iota(jnp.int32, values.shape, 1) % HEAD
    return jnp.where(
        lane < half, pltpu.roll(values, 2 * HEAD - half, 1), pltpu.roll(values, half, 1)
    )


OVER_ROWS = (((0,), (0,)), ((), ()))
OVER_LANES = (((1,), (1,)), ((), ()))


def allowed_keys(seg_col_ref, seg_row_ref, first, count):
    keys = first + count
    key_at = lax.broadcasted_iota(jnp.int32, (keys, count), 0)
    row_at = lax.broadcasted_iota(jnp.int32, (keys, count), 1) + first
    same = seg_col_ref[0, :keys, :] == seg_row_ref[0, :, first : first + count]
    return same & (row_at >= key_at)


def stacked(ref, rows, one, group):
    starts = range(one * group * HEAD, (one + 1) * group * HEAD, HEAD)
    return jnp.concatenate([ref[rows, start : start + HEAD] for start in starts], axis=0)


def unstack(ref, rows, one, values):
    count = rows.stop - rows.start
    group = values.shape[0] // count
    for head in range(group):
        start = (one * group + head) * HEAD
        ref[rows, start : start + HEAD] = values[head * count : (head + 1) * count]


def soft_weights(queries, keys, allowed):
    scores = lax.dot_general(keys, queries, OVER_LANES, preferred_element_type=jnp.float32)
    scores = jnp.where(allowed, scores, -1e30)
    weights = jnp.exp(scores - jnp.max(scores, axis=0, keepdims=True))
    return weights * (1.0 / jnp.sum(weights, axis=0, keepdims=True))


def attend_kernel(
    q_ref, k_ref, v_ref, cos_ref, sin_ref, seg_col_ref, seg_row_ref,
    q_out, k_out, v_out, mixed_ref
):
    cosine, sine = cos_ref[...], sin_ref[...]
    pair = 2 * HEAD
    group = HEADS // KV_HEADS
    for start in range(0, q_ref.shape[1], pair):
        values = q_ref[:, start : start + pair]
        turned = (values * cosine + partner(values) * sine).astype(jnp.bfloat16)
        q_out[:, start : start + pair] = turned * jnp.bfloat16(HEAD**-0.5)
    values = k_ref[...]
    k_out[...] = (values * cosine + partner(values) * sine).astype(jnp.bfloat16)
    v_out[...] = v_ref[...].astype(jnp.bfloat16)
    block = TOK_MB // 2
    for first in range(0, TOK_MB, block):
        rows, keys = slice(first, first + block), slice(0, first + block)
        allowed = allowed_keys(seg_col_ref, seg_row_ref, first, block)
        allowed = jnp.concatenate([allowed] * group, axis=1)
        for one in range(2):
            lanes = slice(one * HEAD, (one + 1) * HEAD)
            weights = soft_weights(
                stacked(q_out, rows, one, group), k_out[keys, lanes], allowed
            ).astype(jnp.bfloat16)
            mixed = lax.dot_general(
                weights, v_out[keys, lanes], OVER_ROWS, preferred_element_type=jnp.float32
            )
            unstack(mixed_ref, rows, one, mixed.astype(jnp.bfloat16))


def attend_back_kernel(
    q_ref, k_ref, v_ref, grad_ref, cos_ref, sin_ref, seg_col_ref, seg_row_ref,
    dq_ref, dk_ref, dv_ref, dq_sum, dk_sum, dv_sum
):
    cosine, sine = cos_ref[...], sin_ref[...]
    pair = 2 * HEAD
    group = HEADS // KV_HEADS
    block = TOK_MB // 2
    for first in range(TOK_MB - block, -1, -block):
        rows, keys = slice(first, first + block), slice(0, first + block)
        allowed = allowed_keys(seg_col_ref, seg_row_ref, first, block)
        allowed = jnp.concatenate([allowed] * group, axis=1)
        for one in range(2):
            lanes = slice(one * HEAD, (one + 1) * HEAD)
            key_rows, value_rows = k_ref[keys, lanes], v_ref[keys, lanes]
            queries = stacked(q_ref, rows, one, group)
            grads = stacked(grad_ref, rows, one, group)
            weights = soft_weights(queries, key_rows, allowed)
            grad_weights = lax.dot_general(
                value_rows, grads, OVER_LANES, preferred_element_type=jnp.float32
            )
            grad_values = jnp.dot(
                weights.astype(jnp.bfloat16), grads, preferred_element_type=jnp.float32
            )
            inner = jnp.sum(grad_weights * weights, axis=0, keepdims=True)
            grad_scores = (weights * (grad_weights - inner)).astype(jnp.bfloat16)
            grad_queries = lax.dot_general(
                grad_scores, key_rows, OVER_ROWS, preferred_element_type=jnp.float32
            )
            unstack(dq_sum, rows, one, grad_queries * HEAD ** (-0.5))
            grad_keys = jnp.dot(grad_scores, queries, preferred_element_type=jnp.float32)
            if first == TOK_MB - block:
                dk_sum[keys, lanes] = grad_keys
                dv_sum[keys, lanes] = grad_values
            else:
                dk_sum[keys, lanes] = dk_sum[keys, lanes] + grad_keys
                dv_sum[keys, lanes] = dv_sum[keys, lanes] + grad_values
    for start in range(0, q_ref.shape[1], pair):
        values = dq_sum[:, start : start + pair]
        dq_ref[:, start : start + pair] = (
            values * cosine - partner(values) * sine
        ).astype(jnp.bfloat16)
    values = dk_sum[...]
    dk_ref[...] = (values * cosine - partner(values) * sine).astype(jnp.bfloat16)
    dv_ref[...] = dv_sum[...].astype(jnp.bfloat16)


def attend_blocks(row_count):
    pair = 2 * HEAD
    wide = pair * (HEADS // KV_HEADS)
    narrow = pl.BlockSpec((TOK_MB, pair), lambda b, g: (b, g))
    broad = pl.BlockSpec((TOK_MB, wide), lambda b, g: (b, g))
    sides = [
        pl.BlockSpec((TOK_MB, pair), lambda b, g: (b, 0)),
        pl.BlockSpec((TOK_MB, pair), lambda b, g: (b, 0)),
        pl.BlockSpec((1, TOK_MB, 1), lambda b, g: (b, 0, 0)),
        pl.BlockSpec((1, 1, TOK_MB), lambda b, g: (b, 0, 0)),
    ]
    return (row_count // TOK_MB, KV_HEADS // 2), narrow, broad, sides


def attend(projected, sides):
    row_count = projected.shape[0]
    grid, narrow, broad, side_specs = attend_blocks(row_count)
    q_dim, kv_dim, pair = HEADS * HEAD, KV_HEADS * HEAD, 2 * HEAD
    key_start, value_start = q_dim // pair, (q_dim + kv_dim) // pair
    q_shape = jax.ShapeDtypeStruct((row_count, q_dim), jnp.bfloat16)
    kv_shape = jax.ShapeDtypeStruct((row_count, kv_dim), jnp.bfloat16)
    return pl.pallas_call(
        attend_kernel,
        grid=grid,
        out_shape=(q_shape, kv_shape, kv_shape, q_shape),
        in_specs=[
            broad,
            pl.BlockSpec((TOK_MB, pair), lambda b, g: (b, key_start + g)),
            pl.BlockSpec((TOK_MB, pair), lambda b, g: (b, value_start + g)),
        ]
        + side_specs,
        out_specs=(broad, narrow, narrow, broad),
        name="attend",
    )(projected, projected, projected, *sides)


def attend_back(queries, key_rows, value_rows, grad_mixed, sides):
    row_count = queries.shape[0]
    grid, narrow, broad, side_specs = attend_blocks(row_count)
    shapes = [jax.ShapeDtypeStruct(x.shape, jnp.bfloat16) for x in (queries, key_rows, value_rows)]
    return pl.pallas_call(
        attend_back_kernel,
        grid=grid,
        out_shape=tuple(shapes),
        in_specs=[broad, narrow, narrow, broad] + side_specs,
        out_specs=(broad, narrow, narrow),
        scratch_shapes=[
            pltpu.VMEM((TOK_MB, 2 * HEAD * (HEADS // KV_HEADS)), jnp.float32),
            pltpu.VMEM((TOK_MB, 2 * HEAD), jnp.float32),
            pltpu.VMEM((TOK_MB, 2 * HEAD), jnp.float32),
        ],
        name="attend_back",
    )(queries, key_rows, value_rows, grad_mixed, *sides)


def pick(rows, index):
    return jnp.take(rows, index, axis=0, mode="clip")


def hold(value, *after):
    anywhere = pl.BlockSpec(memory_space=pl.ANY)
    return pl.pallas_call(
        lambda *refs: None,
        out_shape=jax.ShapeDtypeStruct(value.shape, value.dtype),
        in_specs=[anywhere] * (1 + len(after)),
        out_specs=anywhere,
        input_output_aliases={0: 0},
        name="hold",
    )(value, *after)


def norm_back(values, scale, gain, grad_normed):
    scaled_grad = grad_normed * gain
    grad_gain = jnp.sum(grad_normed * values * scale, axis=0)
    grad_values = scale * scaled_grad - values * scale * scale * scale * jnp.mean(
        scaled_grad * values, axis=1, keepdims=True
    )
    return (grad_gain, grad_values)


MESH = pl.DeviceIdType.MESH


def flip(value, bits):
    bit = 1
    while bit <= bits:
        if bits & bit:
            value = value + bit * (1 - 2 * ((value // bit) % 2))
        bit *= 2
    return value


def place():
    return lax.axis_index("hi"), lax.axis_index("lo"), lax.axis_index("core")


def greet_all(sizes):
    hi_count, lo_count, _ = sizes
    count = hi_count * lo_count * 2
    hi, lo, core = place()
    me = (hi * lo_count + lo) * 2 + core
    barrier = pltpu.get_barrier_semaphore()

    def greet(step, carry):
        peer = (me + step) % count
        pl.semaphore_signal(
            barrier,
            inc=1,
            device_id=(peer // (2 * lo_count), (peer // 2) % lo_count, peer % 2),
            device_id_type=MESH,
        )
        return carry

    lax.fori_loop(1, count, greet, 0)
    pl.semaphore_wait(barrier, count - 1)


def send_rows(sizes, source, target, send_sem, recv_sem):
    hi_count, lo_count, _ = sizes
    count = hi_count * lo_count * 2
    hi, lo, core = place()
    me = (hi * lo_count + lo) * 2 + core

    def one(step, carry):
        peer = (me + step) % count
        pltpu.make_async_remote_copy(
            src_ref=source.at[peer],
            dst_ref=target.at[me],
            send_sem=send_sem,
            recv_sem=recv_sem,
            device_id=(peer // (2 * lo_count), (peer // 2) % lo_count, peer % 2),
            device_id_type=MESH,
        ).start()
        return carry

    lax.fori_loop(1, count, one, 0)


def wait_rows(source, target, send_sem, recv_sem):
    rest = pl.ds(0, source.shape[0] - 1)
    pltpu.make_async_copy(source.at[rest], source.at[rest], send_sem).wait()
    pltpu.make_async_copy(target.at[rest], target.at[rest], recv_sem).wait()


def lo_steps(lo_count, turn):
    bits = []
    bit = 1
    while bit < lo_count:
        bits.append(bit)
        bit *= 2
    if turn:
        bits = bits[::-1]
    held, steps = [0], []
    for bit in bits:
        steps.append((bit, list(held)))
        held = held + [offset ^ bit for offset in held]
    return steps


def opening_kernel(
    sizes, rows_ref, grads_ref, shard_ref, got_ref, got_grads_ref, full_ref,
    own_sem, row_sems, hi_sems, lo_sems, core_sems
):
    hi_count, lo_count, _ = sizes
    hi, lo, core = place()
    me = (hi * lo_count + lo) * 2 + core
    own = [
        pltpu.make_async_copy(shard_ref, full_ref.at[hi, lo, core], own_sem.at[0]),
        pltpu.make_async_copy(rows_ref.at[me], got_ref.at[me], own_sem.at[1]),
        pltpu.make_async_copy(grads_ref.at[me], got_grads_ref.at[me], own_sem.at[2]),
    ]
    for copy in own:
        copy.start()
    greet_all(sizes)

    def hop(source, at, device, sems, *index):
        return pltpu.make_async_remote_copy(
            src_ref=source,
            dst_ref=full_ref.at[at[0], at[1], at[2]],
            send_sem=sems.at[0, *index],
            recv_sem=sems.at[1, *index],
            device_id=device,
            device_id_type=MESH,
        )

    along_hi = {}
    for step in range(1, hi_count):
        along_hi[step] = hop(
            shard_ref, (hi, lo, core), (flip(hi, step), lo, core), hi_sems, step - 1
        )
        along_hi[step].start()
    send_rows(sizes, rows_ref, got_ref, row_sems.at[0, 0], row_sems.at[1, 0])
    send_rows(sizes, grads_ref, got_grads_ref, row_sems.at[0, 1], row_sems.at[1, 1])

    def across(plane, offset, first):
        at = (flip(hi, plane), flip(lo, offset), core)
        source = shard_ref if first else full_ref.at[at[0], at[1], at[2]]
        copy = hop(source, at, (hi, lo, 1 - core), core_sems, plane, offset)
        copy.start()
        return copy

    started, waits = [], []
    for plane in range(hi_count):
        if plane:
            along_hi[plane].wait_recv()
        started.append(across(plane, 0, plane == 0))
        number = 0
        for bit, offsets in lo_steps(lo_count, plane % 2):
            for offset in offsets:
                at = (flip(hi, plane), flip(lo, offset), core)
                source = shard_ref if plane == 0 and offset == 0 else full_ref.at[at[0], at[1], at[2]]
                copy = hop(source, at, (hi, flip(lo, bit), core), lo_sems, plane, number)
                number += 1
                if offset == 0:
                    copy.start()
                    started.append(copy)
                waits.append((copy, plane, offset, bit))
    arrived = {}
    for copy, plane, offset, bit in waits:
        if offset:
            copy.start()
            started.append(copy)
        copy.wait_recv()
        started.append(across(plane, offset ^ bit, False))
    for copy in started:
        copy.wait_send()
    for step in range(1, hi_count):
        along_hi[step].wait_send()
    for plane in range(hi_count):
        for offset in range(lo_count):
            at = (flip(hi, plane), flip(lo, offset), core)
            hop(
                full_ref.at[at[0], at[1], at[2]], at, (hi, lo, 1 - core), core_sems, plane, offset
            ).wait_recv()
    wait_rows(rows_ref, got_ref, row_sems.at[0, 0], row_sems.at[1, 0])
    wait_rows(grads_ref, got_grads_ref, row_sems.at[0, 1], row_sems.at[1, 1])
    for copy in own:
        copy.wait()


def opening(sizes, rows, grads, shard):
    hi_count, lo_count, _ = sizes
    anywhere = pl.BlockSpec(memory_space=pl.ANY)
    return pl.pallas_call(
        functools.partial(opening_kernel, sizes),
        out_shape=(
            jax.ShapeDtypeStruct(rows.shape, rows.dtype),
            jax.ShapeDtypeStruct(grads.shape, grads.dtype),
            jax.ShapeDtypeStruct(sizes + shard.shape, shard.dtype),
        ),
        in_specs=[anywhere] * 3,
        out_specs=(anywhere, anywhere, anywhere),
        scratch_shapes=[
            pltpu.SemaphoreType.DMA((3,)),
            pltpu.SemaphoreType.DMA((2, 2)),
            pltpu.SemaphoreType.DMA((2, hi_count)),
            pltpu.SemaphoreType.DMA((2, hi_count, lo_count)),
            pltpu.SemaphoreType.DMA((2, hi_count, lo_count)),
        ],
        compiler_params=pltpu.CompilerParams(collective_id=0, has_side_effects=True),
        name="opening",
    )(rows, grads, shard)


def add_blocks(target, first, second):
    rows = target.shape[0]
    tile = 16 if rows % 16 == 0 else rows

    def one(index, carry):
        at = pl.ds(index * tile, tile)
        target[at, :] = (
            first[at, :].astype(jnp.float32) + second[at, :].astype(jnp.float32)
        ).astype(target.dtype)
        return carry

    lax.fori_loop(0, rows // tile, one, 0)


def closing_kernel(
    sizes, out_ref, grad_ref, parts_ref, got_out, got_grad, sum_ref,
    from_core, from_lo, from_hi, held, own_sem, row_sems, hi_sems, lo_sems, core_sems
):
    hi_count, lo_count, _ = sizes
    hi, lo, core = place()
    me = (hi * lo_count + lo) * 2 + core
    own = [
        pltpu.make_async_copy(out_ref.at[me], got_out.at[me], own_sem.at[0]),
        pltpu.make_async_copy(grad_ref.at[me], got_grad.at[me], own_sem.at[1]),
    ]
    for copy in own:
        copy.start()
    greet_all(sizes)

    def hop(source, target, device, sems, *index):
        return pltpu.make_async_remote_copy(
            src_ref=source,
            dst_ref=target,
            send_sem=sems.at[0, *index],
            recv_sem=sems.at[1, *index],
            device_id=device,
            device_id_type=MESH,
        )

    planes = [plane for plane in range(1, hi_count)] + [0]
    across = {}
    for plane in planes:
        for offset in reversed(range(lo_count)):
            across[plane, offset] = hop(
                parts_ref.at[flip(hi, plane), flip(lo, offset), 1 - core],
                from_core.at[plane, offset],
                (hi, lo, 1 - core),
                core_sems,
                plane,
                offset,
            )
            across[plane, offset].start()
    send_rows(sizes, grad_ref, got_grad, row_sems.at[0, 0], row_sems.at[1, 0])
    send_rows(sizes, out_ref, got_out, row_sems.at[0, 1], row_sems.at[1, 1])
    started = []
    plans = {plane: lo_steps(lo_count, plane % 2)[::-1] for plane in planes}
    moves = {}
    for depth in range(len(plans[0])):
        for plane in planes:
            bit, kept = plans[plane][depth]
            base = lo_count - 2 * len(kept)
            if depth == 0:
                for offset in [keep ^ bit for keep in kept] + kept:
                    across[plane, offset].wait_recv()
                    add_blocks(
                        held.at[plane, offset],
                        parts_ref.at[flip(hi, plane), flip(lo, offset), core],
                        from_core.at[plane, offset],
                    )
            else:
                before = plans[plane][depth - 1]
                for number, offset in enumerate(before[1]):
                    copy, spot = moves[plane, depth - 1, offset]
                    copy.wait_recv()
                    add_blocks(held.at[plane, offset], held.at[plane, offset], from_lo.at[plane, spot])
            for number, offset in enumerate(kept):
                spot = base + number
                copy = hop(
                    held.at[plane, offset ^ bit],
                    from_lo.at[plane, spot],
                    (hi, flip(lo, bit), core),
                    lo_sems,
                    plane,
                    spot,
                )
                copy.start()
                started.append(copy)
                moves[plane, depth, offset] = (copy, spot)
    last = len(plans[0]) - 1
    along = {}
    for plane in planes:
        copy, spot = moves[plane, last, 0]
        copy.wait_recv()
        add_blocks(held.at[plane, 0], held.at[plane, 0], from_lo.at[plane, spot])
        if plane:
            along[plane] = hop(
                held.at[plane, 0],
                from_hi.at[plane],
                (flip(hi, plane), lo, core),
                hi_sems,
                plane,
            )
            along[plane].start()
            started.append(along[plane])
    for plane in range(1, hi_count):
        along[plane].wait_recv()
    rows = sum_ref.shape[0]
    tile = 16 if rows % 16 == 0 else rows

    def total(index, carry):
        at = pl.ds(index * tile, tile)
        value = held[0, 0, at, :].astype(jnp.float32)
        for plane in range(1, hi_count):
            value = value + from_hi[plane, at, :].astype(jnp.float32)
        sum_ref[at, :] = value
        return carry

    lax.fori_loop(0, rows // tile, total, 0)
    for copy in started:
        copy.wait_send()
    for copy in across.values():
        copy.wait_send()
    wait_rows(grad_ref, got_grad, row_sems.at[0, 0], row_sems.at[1, 0])
    wait_rows(out_ref, got_out, row_sems.at[0, 1], row_sems.at[1, 1])
    for copy in own:
        copy.wait()


def closing(sizes, out_rows, grad_rows, parts):
    hi_count, lo_count, _ = sizes
    block = parts.shape[3:]
    anywhere = pl.BlockSpec(memory_space=pl.ANY)
    near = pl.BlockSpec(memory_space=pltpu.VMEM)
    return pl.pallas_call(
        functools.partial(closing_kernel, sizes),
        out_shape=(
            jax.ShapeDtypeStruct(out_rows.shape, out_rows.dtype),
            jax.ShapeDtypeStruct(grad_rows.shape, grad_rows.dtype),
            jax.ShapeDtypeStruct(block, jnp.float32),
        ),
        in_specs=[anywhere, anywhere, near],
        out_specs=(anywhere, anywhere, near),
        scratch_shapes=[
            pltpu.VMEM((hi_count, lo_count) + block, jnp.bfloat16),
            pltpu.VMEM((hi_count, lo_count) + block, jnp.bfloat16),
            pltpu.VMEM((hi_count,) + block, jnp.bfloat16),
            pltpu.VMEM((hi_count, lo_count) + block, jnp.bfloat16),
            pltpu.SemaphoreType.DMA((2,)),
            pltpu.SemaphoreType.DMA((2, 2)),
            pltpu.SemaphoreType.DMA((2, hi_count)),
            pltpu.SemaphoreType.DMA((2, hi_count, lo_count)),
            pltpu.SemaphoreType.DMA((2, hi_count, lo_count)),
        ],
        compiler_params=pltpu.CompilerParams(
            collective_id=1, has_side_effects=True, vmem_limit_bytes=60 << 20
        ),
        name="closing",
    )(out_rows, grad_rows, parts)


def dispatch_kernel(weighted, choose_ref, rows_ref, *refs):
    count, capacity, rows = choose_ref.shape[1:]
    chosen = choose_ref[0].reshape(count * capacity, rows)
    width = rows_ref.shape[1]
    tile = 256 if width % 256 == 0 else width
    for start in range(0, width, tile):
        at = pl.ds(start, tile)
        slots = jnp.dot(chosen, rows_ref[:, at], preferred_element_type=jnp.float32)
        slots = slots.reshape(count, capacity, tile)
        if weighted:
            slots = slots * refs[0][:, 0]
        refs[-1][:, 0, :, at] = slots.astype(jnp.bfloat16)


def dispatch(choose, rows, first, stride, slots, weight):
    _, count, capacity, _ = choose.shape
    width = rows.shape[1]
    operands = [choose, rows]
    in_specs = [
        pl.BlockSpec((1, count, capacity, TOK_MB), lambda b: (first + b * stride, 0, 0, 0)),
        pl.BlockSpec((TOK_MB, width), lambda b: (b, 0)),
    ]
    if weight is not None:
        operands.append(weight)
        in_specs.append(pl.BlockSpec((count, 1, capacity, 1), lambda b: (0, first + b * stride, 0, 0)))
    aliases = {}
    if slots is not None:
        aliases = {len(operands): 0}
        operands.append(slots)
        in_specs.append(pl.BlockSpec(memory_space=pl.ANY))
    return pl.pallas_call(
        functools.partial(dispatch_kernel, weight is not None),
        grid=(rows.shape[0] // TOK_MB,),
        out_shape=jax.ShapeDtypeStruct((count, choose.shape[0], capacity, width), jnp.bfloat16),
        in_specs=in_specs,
        out_specs=pl.BlockSpec((count, 1, capacity, width), lambda b: (0, first + b * stride, 0, 0)),
        input_output_aliases=aliases,
        name="dispatch",
    )(*operands)


def middle_kernel(rows_ref, weight_ref, grad_ref, hidden_ref, grad_out_ref):
    half = grad_ref.shape[3]
    for part in range(weight_ref.shape[1]):
        gate_up = jnp.dot(rows_ref[0], weight_ref[0, part], preferred_element_type=jnp.float32)
        gate, up = gate_up[:, :half], gate_up[:, half:]
        sigmoid_gate = jax.nn.sigmoid(gate)
        active = gate * sigmoid_gate
        grad_hidden = grad_ref[0, part].astype(jnp.float32)
        hidden_ref[0, part] = (active * up).astype(jnp.bfloat16)
        slope = sigmoid_gate * (1.0 + gate * (1.0 - sigmoid_gate))
        grad_out_ref[0, part, :, :half] = (grad_hidden * up * slope).astype(jnp.bfloat16)
        grad_out_ref[0, part, :, half:] = (grad_hidden * active).astype(jnp.bfloat16)


def middle(expert_rows, weights_in, grad_hidden):
    count, row_count, width = expert_rows.shape
    parts, both = weights_in.shape[1], weights_in.shape[3]
    tile = 512 if row_count % 512 == 0 else row_count
    return pl.pallas_call(
        middle_kernel,
        grid=(count, row_count // tile),
        out_shape=(
            jax.ShapeDtypeStruct((count, parts, row_count, both // 2), jnp.bfloat16),
            jax.ShapeDtypeStruct((count, parts, row_count, both), jnp.bfloat16),
        ),
        in_specs=[
            pl.BlockSpec((1, tile, width), lambda e, t: (e, t, 0)),
            pl.BlockSpec((1, parts, width, both), lambda e, t: (e, 0, 0, 0)),
            pl.BlockSpec((1, parts, tile, both // 2), lambda e, t: (e, 0, t, 0)),
        ],
        out_specs=(
            pl.BlockSpec((1, parts, tile, both // 2), lambda e, t: (e, 0, t, 0)),
            pl.BlockSpec((1, parts, tile, both), lambda e, t: (e, 0, t, 0)),
        ),
        name="middle",
    )(expert_rows, weights_in, grad_hidden)


def shards(
    tokens,
    cotangent,
    permutation,
    lengths,
    expert_ids,
    gate_weights,
    attn_gain,
    qkv_weight,
    out_weight,
    ffn_gain,
    expert_in,
    expert_out,
):
    device_count = lax.axis_size(ALL)
    hi_count = lax.axis_size("hi")
    lo_count = lax.axis_size("lo")
    tok_dev = permutation.shape[0]
    model_width = tokens.shape[1]
    peer_rows = tok_dev // device_count
    positions = jnp.arange(tok_dev, dtype=jnp.int32)
    expert_count = expert_in.shape[2] * device_count // FF_E
    capacity = TOK_MB * TOPK // expert_count
    source = permutation // tok_dev
    local_row = permutation % tok_dev
    from_source = (source[:, None] == jnp.arange(device_count, dtype=jnp.int32)[None, :]).astype(
        jnp.int32
    )
    earlier = jnp.cumsum(from_source, axis=0, dtype=jnp.int32) - from_source
    arrival = source * peer_rows + jnp.sum(earlier * from_source, axis=1, dtype=jnp.int32)
    arrival_match = arrival[:, None] == positions[None, :]
    wanted = jnp.sum(jnp.where(arrival_match, local_row[:, None], 0), axis=0, dtype=jnp.int32)
    by_arrival = jnp.sum(jnp.where(arrival_match, positions[:, None], 0), axis=0, dtype=jnp.int32)
    def swap(block, step):
        return lax.ppermute(block, "lo", [(i, i ^ step) for i in range(lo_count)])

    def spread(block):
        if lo_count != 4:
            return [[block]] + [[swap(block, step)] for step in range(1, lo_count)]
        half = block.shape[0] // 2
        one, two = swap(block, 1), swap(block, 2)
        return [[block], [one], [two], [swap(one[:half], 2), swap(two[half:], 1)]]

    if lo_count == 4:
        order = [(0, 0), (0, 1), (1, 0), (3, 0), (2, 1), (3, 1), (1, 1), (2, 0)]
    else:
        order = [(step, batch) for step in range(lo_count) for batch in range(MB)]
    routing = jnp.concatenate([expert_ids.astype(jnp.float32), gate_weights], axis=1)
    routing_all = [routing] + [swap(routing, step) for step in range(1, lo_count)]
    routing_all = jnp.stack(
        [routing_all[step][batch * TOK_MB : (batch + 1) * TOK_MB] for step, batch in order]
    )
    asked_rows = lax.all_to_all(
        wanted.reshape(device_count, peer_rows),
        ALL,
        split_axis=0,
        concat_axis=0,
        tiled=True,
    ).reshape(tok_dev)
    asked_rows, routing_all = lax.optimization_barrier((asked_rows, routing_all))
    asked_match = asked_rows[:, None] == positions[None, :]
    by_asked = jnp.sum(jnp.where(asked_match, positions[:, None], 0), axis=0, dtype=jnp.int32)
    sizes = (hi_count, lo_count, 2)
    shard_rows = qkv_weight.shape[0]
    qkv_cols = qkv_weight.shape[1]
    weight_shard = jnp.concatenate(
        [
            qkv_weight,
            out_weight,
            attn_gain[:, None],
            ffn_gain[:, None],
            jnp.zeros((shard_rows, 126), jnp.bfloat16),
        ],
        axis=1,
    )
    asked_tokens = pick(tokens, asked_rows).reshape(device_count, peer_rows, model_width)
    asked_grads = pick(cotangent, asked_rows).reshape(
        device_count, peer_rows, model_width
    )
    segment, position = layout_rows(lengths)
    cosine_table, sine_table = rope_tables(position)
    sides = (
        jnp.tile(cosine_table, (1, 4)),
        jnp.concatenate([-sine_table, sine_table] * 2, axis=1),
        segment.reshape(-1, TOK_MB, 1),
        segment.reshape(-1, 1, TOK_MB),
    )
    asked_tokens = hold(asked_tokens, *sides)
    shard_cols = expert_in.shape[2]
    expert_in = expert_in.reshape(model_width, 2 * shard_cols)
    got_rows, got_grad, packed = opening(sizes, asked_tokens, asked_grads, weight_shard)
    got_rows, packed, expert_in = lax.optimization_barrier((got_rows, packed, expert_in))
    packed = packed.reshape(model_width, -1)
    grad_bf = pick(got_grad.reshape(tok_dev, model_width), arrival)
    got_rows = hold(got_rows, grad_bf)
    grad_blocks = spread(grad_bf)
    rows_in = pick(got_rows.reshape(tok_dev, model_width), arrival).astype(jnp.float32)
    qkv_full = packed[:, :qkv_cols]
    out_full = packed[:, qkv_cols : qkv_cols + model_width]
    gain_pair = packed[:, qkv_cols + model_width :].astype(jnp.float32)
    gain_one = gain_pair[:, 0]
    gain_two = gain_pair[:, 1]
    weights_in = lax.all_gather(
        expert_in, ("hi", "core"), axis=0
    ).reshape(hi_count, 2, model_width, 2 * shard_cols)
    weights_out = lax.all_gather(expert_out, ("hi", "core"), axis=0).reshape(
        hi_count, 2, shard_cols, model_width
    )
    scale_one = lax.rsqrt(jnp.mean(rows_in * rows_in, axis=1, keepdims=True) + epsilon)
    normed = (rows_in * scale_one * gain_one).astype(jnp.bfloat16)
    projected = jnp.dot(normed, qkv_full, preferred_element_type=jnp.float32)
    queries, key_rows, value_rows, mixed_rows = attend(projected, sides)
    if lo_count == 4:
        mixed_rows = hold(mixed_rows, grad_blocks[1][0], grad_blocks[2][0])
    attended = jnp.dot(mixed_rows, out_full, preferred_element_type=jnp.float32)
    residual = rows_in + attended
    scale_two = lax.rsqrt(jnp.mean(residual * residual, axis=1, keepdims=True) + epsilon)
    normed_two = (residual * scale_two * gain_two).astype(jnp.bfloat16)
    grad_output = grad_bf.astype(jnp.float32)
    home = lax.axis_index("lo")
    if lo_count == 4:
        normed_two = hold(normed_two, *grad_blocks[3])
    row_blocks = spread(normed_two)
    normed_two, grad_blocks = lax.optimization_barrier((normed_two, grad_blocks))
    choose, slot_gate = slot_tables(
        routing_all[..., :TOPK].astype(jnp.int32),
        routing_all[..., TOPK:],
        home + lo_count * jnp.arange(hi_count, dtype=jnp.int32),
        capacity,
    )
    slot_weight = jnp.transpose(slot_gate, (1, 0, 2))[..., None]
    place_of = {name: number for number, name in enumerate(order)}

    def fill(blocks, slots, weight):
        for step, pieces in blocks:
            batch = 0
            for piece in pieces:
                first = place_of[step, batch]
                stride = place_of[step, MB - 1] - place_of[step, 0]
                slots = dispatch(choose, piece, first, stride, slots, weight)
                batch += piece.shape[0] // TOK_MB
        return slots

    grad_expert = fill(list(enumerate(grad_blocks)), None, slot_weight)
    grad_expert = grad_expert.reshape(hi_count, -1, model_width)
    grad_hidden = jnp.einsum(
        "erd,ekfd->ekrf", grad_expert, weights_out, preferred_element_type=jnp.float32
    ).astype(jnp.bfloat16)
    expert_rows = fill([(0, [normed_two])], None, None)
    grad_hidden, expert_rows, others = lax.optimization_barrier(
        (grad_hidden, expert_rows, row_blocks[1:])
    )
    expert_rows = fill(list(enumerate(others, 1)), expert_rows, None)
    expert_rows = expert_rows.reshape(hi_count, -1, model_width)
    hidden, grad_gate_up = middle(expert_rows, weights_in, grad_hidden)
    grad_weights_out = jnp.einsum(
        "ekrf,erd->ekfd", hidden, grad_expert, preferred_element_type=jnp.float32
    ).astype(jnp.bfloat16)
    grad_weights_out, grad_gate_up = lax.optimization_barrier((grad_weights_out, grad_gate_up))
    shard_out = lax.psum_scatter(
        grad_weights_out.reshape(hi_count * 2 * shard_cols, model_width),
        ("hi", "core"),
        scatter_dimension=0,
        tiled=True,
    ).astype(jnp.float32)
    grad_expert_rows = jnp.einsum(
        "ekrf,ekdf->erd", grad_gate_up, weights_in, preferred_element_type=jnp.float32
    ).astype(jnp.bfloat16)

    def split_back(slot_values):
        return jnp.einsum(
            "becr,ebcd->brd",
            choose,
            slot_values.reshape(hi_count, lo_count * MB, capacity, model_width),
            preferred_element_type=jnp.float32,
        ).astype(jnp.bfloat16)

    def wide(value):
        return value.astype(jnp.float32)

    def bring_back(parts):
        if lo_count != 4:
            parts = parts.reshape(lo_count, tok_dev, model_width)
            swapped = [swap(parts[step], step) for step in range(1, lo_count)]
            return [parts[0]] + swapped
        one = swap(parts[2:4], 1)
        two = swap(parts[4:6], 2)
        for_one = (wide(parts[6]) + wide(two[1])).astype(jnp.bfloat16)
        for_two = (wide(parts[7]) + wide(one[1])).astype(jnp.bfloat16)
        return [parts[:2], one, two, swap(for_two, 2), swap(for_one, 1)]

    def total_of(terms):
        if lo_count != 4:
            total = wide(terms[0])
            for term in terms[1:]:
                total = total + wide(term)
            return total
        own, one, two, last_two, last_one = terms
        return jnp.concatenate(
            [
                wide(own[0]) + wide(one[0]) + wide(last_two),
                wide(own[1]) + wide(two[0]) + wide(last_one),
            ],
            axis=0,
        )

    back = split_back(grad_expert_rows)
    back_parts = bring_back(back)
    produced = (
        jnp.einsum("ekrf,ekfd->erd", hidden, weights_out, preferred_element_type=jnp.float32)
        * slot_weight.reshape(hi_count, -1, 1)
    ).astype(jnp.bfloat16)
    ahead = split_back(produced)
    grad_weights_in = jnp.einsum(
        "ekrf,erd->ekfd", grad_gate_up, expert_rows, preferred_element_type=jnp.float32
    ).astype(jnp.bfloat16)
    shard_in = lax.psum_scatter(
        grad_weights_in.reshape(hi_count * 2 * 2 * shard_cols, model_width),
        ("hi", "core"),
        scatter_dimension=0,
        tiled=True,
    )
    shard_in = shard_in.astype(jnp.float32).reshape(2, shard_cols, model_width)
    shard_in = jnp.transpose(shard_in, (2, 0, 1))
    ahead, back_parts = lax.optimization_barrier((ahead, back_parts))
    ahead_parts = bring_back(ahead)
    grad_normed_two = total_of(back_parts)
    grad_gain_two, grad_from_norm = norm_back(residual, scale_two, gain_two, grad_normed_two)
    grad_residual = grad_output + grad_from_norm
    grad_attended = grad_residual.astype(jnp.bfloat16)
    grad_out_weight = jnp.einsum(
        "nq,nd->qd", mixed_rows, grad_attended, preferred_element_type=jnp.float32
    )
    grad_mixed = jnp.einsum(
        "nd,qd->nq", grad_attended, out_full, preferred_element_type=jnp.float32
    ).astype(jnp.bfloat16)
    grad_projected = jnp.concatenate(
        attend_back(queries, key_rows, value_rows, grad_mixed, sides), axis=1
    )
    if lo_count == 4:
        normed = hold(normed, *ahead_parts[1:3])
    grad_qkv_weight = jnp.einsum(
        "nd,nc->dc", normed, grad_projected, preferred_element_type=jnp.float32
    )
    grad_normed = jnp.einsum(
        "nc,dc->nd", grad_projected, qkv_full, preferred_element_type=jnp.float32
    )
    grad_gain_one, grad_from_first = norm_back(rows_in, scale_one, gain_one, grad_normed)
    grad_input = (grad_residual + grad_from_first).astype(jnp.bfloat16)
    gains = jnp.pad(jnp.stack([grad_gain_one, grad_gain_two], axis=1), ((0, 0), (0, 126)))
    parts = jnp.concatenate(
        [
            grad_qkv_weight.astype(jnp.bfloat16),
            grad_out_weight.astype(jnp.bfloat16),
            gains.astype(jnp.bfloat16),
        ],
        axis=1,
    ).reshape(sizes + (shard_rows, -1))
    parts, shard_out, ahead_parts = lax.optimization_barrier((parts, shard_out, ahead_parts))
    output_rows = (residual + total_of(ahead_parts)).astype(jnp.bfloat16)
    home_out, home_grad, sums = closing(
        sizes,
        pick(output_rows, by_arrival).reshape(device_count, peer_rows, model_width),
        pick(grad_input, by_arrival).reshape(device_count, peer_rows, model_width),
        parts,
    )
    shard_qkv = sums[:, :qkv_cols]
    shard_attn_out = sums[:, qkv_cols : qkv_cols + model_width]
    shard_gain_one = sums[:, qkv_cols + model_width]
    shard_gain_two = sums[:, qkv_cols + model_width + 1]
    output = pick(home_out.reshape(tok_dev, model_width), by_asked)
    input_grad = pick(home_grad.reshape(tok_dev, model_width), by_asked)
    return (
        output,
        input_grad,
        shard_gain_one,
        shard_qkv,
        shard_attn_out,
        shard_gain_two,
        shard_in,
        shard_out,
    )


def solution(mesh):
    dp_count = mesh.shape["dp"]
    hi_count = 4 if dp_count % 4 == 0 else 1
    split = jax.sharding.Mesh(
        mesh.devices.reshape(hi_count, dp_count // hi_count, mesh.shape["expert"]), ALL
    )
    rows, columns = P(ALL, None), P(None, None, ALL)
    return jax.shard_map(
        shards,
        mesh=split,
        in_specs=(rows, rows, P(ALL), rows, rows, rows, P(ALL), rows, rows, P(ALL), columns, rows),
        out_specs=(rows, rows, P(ALL), rows, rows, P(ALL), columns, rows),
        check_vma=False,
    )
```
